32 devices in a mesh: ctx: 8 (over z, x), exp: 4 (over y, core).
Axes of the slice: x: 2, y: 2, z: 4, core: 2. Of those that a mesh axis runs over, the one named last changes fastest.
Arguments:
- residual: bfloat16 [4, 1024, 2048], P('exp', 'ctx'), may hold values from -54 to 54
- queries: bfloat16 [4, 1024, 2048], P('exp', 'ctx'), may hold values from -160 to 160
- key_states: bfloat16 [4, 1024, 256], P('exp', 'ctx'), may hold values from -6.1 to 6.1
- value_states: bfloat16 [4, 1024, 256], P('exp', 'ctx'), may hold values from -6 to 6
- expert_ids: int32 [4, 1024, 1], P('exp', 'ctx'), may hold values from 0 to 7; in each aligned block of 128 rows (0 to 127, 128 to 255, ..., all dimensions but the last counted through in order) at most 32 rows name the same one
- route_weight: float32 [4, 1024, 1], P('exp', 'ctx'), may hold values from 0.2 to 1
- gate_weight: bfloat16 [4, 8, 192, 2048], P('exp', 'ctx'), may hold values from -0.125 to 0.125
- up_weight: bfloat16 [4, 8, 192, 2048], P('exp', 'ctx'), may hold values from -0.125 to 0.125
- down_weight: bfloat16 [4, 8, 192, 2048], P('exp', 'ctx'), may hold values from -0.21875 to 0.21875
Outputs:
- output: bfloat16 [4, 1024, 2048], P('exp', 'ctx')
The draws below stay inside these ranges and needn't reach their ends.
Inputs may be any that keep to these rules, and one draw needn't show every extreme that they name: `expert_ids`: within each aligned block of 128 rows (sequence by sequence, positions in order), which is the rows of one device, no expert is named more than 32 times, a bound that some block reaches; every expert is named somewhere.
All inputs are finite; a program needn't handle non-finite values.
Results may differ from the reference program's by a relative error of at most 0.003.
Values may be sent and summed in bfloat16 or wider, within the bound.
No kernel may reach another device: no remote copies, remote signals or barrier semaphores. Data moves between devices by JAX's collectives and lax.ppermute only.
A program may use at most 64 MiB of HBM per device.

```python
import math
import jax
import jax.numpy as jnp
import numpy as np
from jax import lax

D = 2048
FF = 768
HD = 128
HEADS = 16
KV_HEADS = 2
PIECES = 4
TOPK = 1
TOK_DEV = 128
SEQ_LEN = 1024
SEQS = 4
EXPERTS = 8
CAP = 32
N_CTX = 8
N_EXP = 4


def attention_pair(key):
    key_base = jnp.clip(jax.random.normal(jax.random.fold_in(key, 11), (SEQS, SEQ_LEN, KV_HEADS, HD), jnp.float32), -6.0, 6.0)
    query_base = jnp.clip(jax.random.normal(jax.random.fold_in(key, 12), (SEQS, SEQ_LEN, HEADS, HD), jnp.float32), -6.0, 6.0)
    return (query_base.reshape(SEQS, SEQ_LEN, HEADS * HD), key_base.reshape(SEQS, SEQ_LEN, KV_HEADS * HD))


def draw_queries(key, part):
    return attention_pair(key)[0].astype(jnp.bfloat16)


def draw_key_states(key, part):
    return attention_pair(key)[1].astype(jnp.bfloat16)


def draw_residual(key, part):
    row_scale = jnp.exp(jax.random.uniform(jax.random.fold_in(key, 21), (SEQS, SEQ_LEN, 1), jnp.float32, math.log(0.3), math.log(3.0)))
    column_scale = jnp.exp(jax.random.uniform(jax.random.fold_in(key, 22), (1, 1, D), jnp.float32, math.log(0.3), math.log(3.0)))
    base = jnp.clip(jax.random.normal(jax.random.fold_in(key, 25), (SEQS, SEQ_LEN, D), jnp.float32), -6.0, 6.0)
    return (base * row_scale * column_scale).astype(jnp.bfloat16)


def levels(stream_key, shape, shards, smallest, largest):
    def one(dim, blocks):
        heights = jax.random.uniform(jax.random.fold_in(jax.random.fold_in(stream_key, 6), dim), (blocks,), jnp.float32, smallest / len(shards), largest / len(shards))
        return jnp.repeat(jnp.exp(heights), shape[dim] // blocks).reshape((-1,) + (1,) * (len(shape) - dim - 1))

    loudness = one(*shards[0])
    for cut in shards[1:]:
        loudness = loudness * one(*cut)
    return loudness


def routed_block(rng, own, number, rows, count, top, most, lean):
    ranking = jax.random.permutation(rng, count)
    crowded, ordinary = load_shares(count, rows * top, most, lean, True), load_shares(count, rows * top, most, lean, False)
    places = jnp.arange(count)

    def named(tallies, turn):
        used = int((tallies > 0).sum())
        fixed = max(1, used // 4)
        shifted = fixed + (places - fixed + turn * (used - fixed)) % max(1, count - fixed)
        return jnp.zeros((count,), jnp.int32).at[ranking[jnp.where(places < fixed, places, shifted)]].set(jnp.asarray(tallies, jnp.int32))

    tallies = jnp.where(number % 4 == 0, named(crowded, number // 4), named(ordinary, number - number // 4 - 1))
    mixed = jax.random.permutation(jax.random.fold_in(own, 3), count)
    donor, receiver = mixed[0:count // 2 * 2:2], mixed[1:count // 2 * 2:2]
    room = jnp.minimum(tallies[donor] - 1, most - tallies[receiver]) // 2
    room = jnp.where((donor == ranking[0]) | (receiver == ranking[0]) | (tallies[receiver] == 0), 0, jnp.maximum(room, 0))
    shifted = jax.random.randint(jax.random.fold_in(own, 4), (count // 2,), 0, 1 << 20) % (room + 1)
    tallies = tallies.at[donor].add(-shifted).at[receiver].add(shifted)
    members = jnp.searchsorted(jnp.cumsum(tallies), jnp.arange(rows * top), side="right").astype(jnp.int32)
    table = members.reshape(top, rows).T
    table = table[jax.random.permutation(jax.random.fold_in(own, 1), rows)]
    turn = jax.random.randint(jax.random.fold_in(own, 2), (rows, 1), 0, top)
    return jnp.take_along_axis(table, (jnp.arange(top)[None, :] + turn) % top, axis=1)


def load_shares(count, total, reach, lean, full):
    weights = [(1 << 20) // math.isqrt(standing ** lean) + 1 for standing in range(1, count + 1)]
    largest = reach if full else min(reach, max(-(-total // count), total * weights[0] // sum(weights)))
    least = 1 if total - largest >= count - 1 else 0
    given, surplus = [largest] + [least] * (count - 1), total - largest - least * (count - 1)
    while surplus > 0:
        movable = [i for i in range(1, count) if given[i] < largest] or [i for i in range(1, count) if given[i] < reach]
        mass, left = sum([weights[i] for i in movable]), surplus
        for i in movable:
            more = min(reach - given[i], max(1, left * weights[i] // mass), surplus)
            given[i] = given[i] + more
            surplus = surplus - more
    return np.array(given)


def scatter_about(rng, dims, deviation, bound, shards=(), held_as=jnp.bfloat16):
    values = deviation * jax.random.normal(rng, dims, jnp.float32)
    if shards:
        values = values * levels(rng, dims, shards, -0.22, 0.18)
    return jnp.clip(values, -bound, bound).astype(held_as)


def setup_inputs(seed: int = 0) -> dict:
    key_list = jax.random.split(jax.random.key(seed), 10)
    residual = draw_residual(jax.random.fold_in(key_list[9], 71), 0)
    queries = draw_queries(jax.random.fold_in(key_list[9], 71), 0)
    key_states = draw_key_states(jax.random.fold_in(key_list[9], 71), 0)
    value_states = scatter_about(key_list[3], (SEQS, SEQ_LEN, KV_HEADS * HD), 1.0, 6.0, ((0, 4), (1, 8)))
    expert_ids_keys = jax.random.split(jax.random.fold_in(key_list[4], 1), SEQS * SEQ_LEN // TOK_DEV)
    expert_ids_turns = jax.random.permutation(jax.random.fold_in(key_list[4], 3), SEQS * SEQ_LEN // TOK_DEV)
    expert_ids = jax.vmap(lambda own, number: routed_block(jax.random.fold_in(key_list[4], 2), own, number, TOK_DEV, EXPERTS, TOPK, CAP, 2))(expert_ids_keys, expert_ids_turns).reshape((SEQS, SEQ_LEN, TOPK))
    route_weight = jnp.clip(0.2 + 0.8 * jax.random.uniform(key_list[5], (SEQS, SEQ_LEN, TOPK), jnp.float32) ** levels(key_list[5], (SEQS, SEQ_LEN, TOPK), ((0, 4), (1, 8)), -0.2, 0.2), 0.2, 1.0)
    gate_weight = scatter_about(key_list[6], (N_EXP, N_CTX, FF // PIECES, D), D ** -0.5, 0.125, ((0, 4), (1, 8)))
    up_weight = scatter_about(key_list[7], (N_EXP, N_CTX, FF // PIECES, D), D ** -0.5, 0.125, ((0, 4), (1, 8)))
    down_weight = scatter_about(key_list[8], (N_EXP, N_CTX, FF // PIECES, D), FF ** -0.5, 0.21875, ((0, 4), (1, 8)))
    return {"residual": residual, "queries": queries, "key_states": key_states, "value_states": value_states, "expert_ids": expert_ids, "route_weight": route_weight, "gate_weight": gate_weight, "up_weight": up_weight, "down_weight": down_weight}


negative_fill = -1e+30
epsilon = 1e-06

def contract_rows(left_rows, weight_rows):
    return lax.dot_general(left_rows, weight_rows, (((1,), (1,)), ((), ())), preferred_element_type=jnp.float32)

def attend_all(queries, key_states, value_states):
    group_size = HEADS // KV_HEADS
    block_len = math.gcd(SEQ_LEN, 256)
    block_count = SEQ_LEN // block_len
    score_scale = 1.0 / math.sqrt(HD)
    query_grid = queries.reshape(SEQS * block_count, block_len, KV_HEADS, group_size, HD)
    key_grid = key_states.reshape(SEQS, SEQ_LEN, KV_HEADS, HD)
    value_grid = value_states.reshape(SEQS, SEQ_LEN, KV_HEADS, HD)
    key_pos = jnp.arange(SEQ_LEN, dtype=jnp.int32)

    def one_block(flat_index):
        seq_index = flat_index // block_count
        query_start = flat_index % block_count * block_len
        query_block = query_grid[flat_index].astype(jnp.float32)
        key_seq = key_grid[seq_index].astype(jnp.float32)
        value_seq = value_grid[seq_index].astype(jnp.float32)
        scores = jnp.einsum('tgjd,kgd->gjtk', query_block, key_seq) * score_scale
        query_pos = query_start + jnp.arange(block_len, dtype=jnp.int32)
        allowed = key_pos[None, None, None, :] <= query_pos[None, None, :, None]
        scores = jnp.where(allowed, scores, negative_fill)
        row_max = lax.optimization_barrier(jnp.max(scores, axis=-1, keepdims=True))
        exponent = jnp.where(allowed, jnp.exp(scores - row_max), 0.0)
        totals = lax.optimization_barrier(jnp.sum(exponent, axis=-1))
        rounded = lax.optimization_barrier(exponent.astype(jnp.bfloat16)).astype(jnp.float32)
        weighted = jnp.einsum('gjtk,kgd->tgjd', rounded, value_seq)
        result = weighted / jnp.transpose(totals, (2, 0, 1))[..., None]
        return result.astype(jnp.bfloat16).reshape(block_len, HEADS * HD)
    blocks_out = lax.map(one_block, jnp.arange(SEQS * block_count, dtype=jnp.int32))
    return blocks_out.reshape(SEQS, SEQ_LEN, HEADS * HD)

def reference(residual, queries, key_states, value_states, expert_ids, route_weight, gate_weight, up_weight, down_weight):
    attention = attend_all(queries, key_states, value_states)
    token_total = SEQS * SEQ_LEN
    block_total = token_total // TOK_DEV
    pair_each = TOK_DEV * TOPK
    summed = residual.astype(jnp.float32).reshape(token_total, D) + lax.optimization_barrier(attention).astype(jnp.float32).reshape(token_total, D)
    normed = (summed * lax.rsqrt(lax.optimization_barrier(jnp.mean(summed * summed, axis=-1, keepdims=True)) + epsilon)).astype(jnp.bfloat16)
    block_ids = expert_ids.reshape(block_total, pair_each).astype(jnp.int32)
    onehot = (block_ids[:, :, None] == jnp.arange(EXPERTS, dtype=jnp.int32)[None, None, :]).astype(jnp.int32)
    earlier = jnp.cumsum(onehot, axis=1).astype(jnp.int32) - onehot
    slot_index = lax.optimization_barrier(jnp.sum(earlier * onehot, axis=2)).astype(jnp.int32)
    slots_each = block_total * CAP
    block_index = jnp.arange(block_total, dtype=jnp.int32)[:, None]
    target = (block_ids * slots_each + block_index * CAP + slot_index).reshape(-1).astype(jnp.int32)
    pair_token = (block_index * TOK_DEV + jnp.arange(pair_each, dtype=jnp.int32)[None, :] // TOPK).reshape(-1).astype(jnp.int32)
    slot_table = jnp.full((EXPERTS * slots_each,), token_total, jnp.int32).at[target].set(pair_token)
    normed_pad = jnp.concatenate([normed, jnp.zeros((1, D), jnp.bfloat16)], axis=0)
    piece_width = FF // PIECES
    gate_all = gate_weight.reshape(EXPERTS, PIECES, piece_width, D)
    up_all = up_weight.reshape(EXPERTS, PIECES, piece_width, D)
    down_all = down_weight.reshape(EXPERTS, PIECES, piece_width, D)

    def expert_run(expert):
        row_ids = lax.dynamic_slice_in_dim(slot_table, expert * slots_each, slots_each)
        rows_in = normed_pad[row_ids]
        piece_total = jnp.zeros((slots_each, D), jnp.float32)
        for piece_id in range(PIECES):
            gate_part = contract_rows(rows_in, gate_all[expert, piece_id])
            up_part = contract_rows(rows_in, up_all[expert, piece_id])
            active = (jax.nn.silu(gate_part) * up_part).astype(jnp.bfloat16)
            partial_out = jnp.dot(active, down_all[expert, piece_id], preferred_element_type=jnp.float32).astype(jnp.bfloat16)
            piece_total = piece_total + lax.optimization_barrier(partial_out).astype(jnp.float32)
        return piece_total.astype(jnp.bfloat16)
    expert_outputs = lax.map(expert_run, jnp.arange(EXPERTS, dtype=jnp.int32))
    pair_out = lax.optimization_barrier(expert_outputs.reshape(EXPERTS * slots_each, D)[target]).astype(jnp.float32)
    weighted = pair_out * route_weight.reshape(token_total * TOPK, 1)
    mixture = lax.optimization_barrier(jnp.sum(weighted.reshape(token_total, TOPK, D), axis=1))
    return (summed + mixture).astype(jnp.bfloat16).reshape(SEQS, SEQ_LEN, D)
```

```python
from functools import partial
import math

import jax
import jax.numpy as jnp
from jax import lax
from jax.experimental import pallas as pl
from jax.experimental.pallas import tpu as pltpu
from jax.sharding import PartitionSpec as P

HD = 128
HEADS = 16
KV_HEADS = 2
PIECES = 4
TOPK = 1


negative_fill = -1e30
epsilon = 1e-06


def contract_rows(left_rows, weight_rows):
    return lax.dot_general(
        left_rows, weight_rows, (((1,), (1,)), ((), ())), preferred_element_type=jnp.float32
    )


def to_groups(half_block, heads_kv, group_size, head_dim):
    token_count = half_block.shape[0]
    shaped = half_block.reshape(token_count, heads_kv, group_size, head_dim)
    return jnp.transpose(shaped, (1, 0, 2, 3)).reshape(heads_kv, token_count * group_size, head_dim)


def keep_current(current):
    return current


def block_update(current, query_rows, query_pos, key_block, value_block, key_start, score_scale):
    running_max, running_total, accumulated = current
    scores = (
        jnp.einsum("gqd,kgd->gqk", query_rows, key_block, preferred_element_type=jnp.float32)
        * score_scale
    )
    key_pos = key_start + jnp.arange(key_block.shape[0], dtype=jnp.int32)
    allowed = key_pos[None, None, :] <= query_pos[None, :, None]
    scores = jnp.where(allowed, scores, negative_fill)
    new_max = jnp.maximum(running_max, jnp.max(scores, axis=-1))
    rescale = jnp.exp(running_max - new_max)
    exponent = jnp.where(allowed, jnp.exp(scores - new_max[..., None]), 0.0)
    new_total = running_total * rescale + jnp.sum(exponent, axis=-1)
    product = jnp.einsum(
        "gqk,kgd->gqd",
        exponent.astype(jnp.bfloat16),
        value_block,
        preferred_element_type=jnp.float32,
    )
    return (new_max, new_total, accumulated * rescale[..., None] + product)


def make_folder(query_sets, position_sets, last_positions, heads_kv, head_dim, score_scale):

    def fold_keys(running, key_piece, first_key):
        key_part, value_part = key_piece
        key_count = key_part.shape[1]
        key_width = math.gcd(key_count, 512)
        key_rows = key_part.reshape(key_count, heads_kv, head_dim)
        value_rows = value_part.reshape(key_count, heads_kv, head_dim)

        def one_block(block_index, current_sets):
            offset = block_index * key_width
            key_block = lax.dynamic_slice_in_dim(key_rows, offset, key_width, 0)
            value_block = lax.dynamic_slice_in_dim(value_rows, offset, key_width, 0)
            updated = []
            for current, query_rows, query_pos, last_pos in zip(
                current_sets, query_sets, position_sets, last_positions
            ):
                step_fn = partial(
                    block_update,
                    query_rows=query_rows,
                    query_pos=query_pos,
                    key_block=key_block,
                    value_block=value_block,
                    key_start=offset,
                    score_scale=score_scale,
                )
                updated.append(lax.cond(offset <= last_pos, step_fn, keep_current, current))
            return tuple(updated)

        return lax.fori_loop(0, key_count // key_width, one_block, running)

    return fold_keys


def finish(current, token_count, heads_kv, group_size, head_dim):
    running_max, running_total, accumulated = current
    result = accumulated / running_total[..., None]
    shaped = result.reshape(heads_kv, token_count, group_size, head_dim)
    return (
        jnp.transpose(shaped, (1, 0, 2, 3))
        .reshape(token_count, heads_kv * group_size * head_dim)
        .astype(jnp.bfloat16)
    )


def shards(
    residual,
    queries,
    key_states,
    value_states,
    expert_ids,
    route_weight,
    gate_weight,
    up_weight,
    down_weight,
):
    ctx_count = lax.axis_size("ctx")
    exp_count = lax.axis_size("exp")
    ctx_rank = lax.axis_index("ctx")
    tok_rows = residual.shape[1]
    half_rows = tok_rows // 2
    group_size = HEADS // KV_HEADS
    score_scale = 1.0 / math.sqrt(HD)
    local_queries = queries[0]
    first_half = local_queries[:half_rows]
    second_half = local_queries[half_rows:]
    first_start = ctx_rank * tok_rows
    second_start = first_start + half_rows
    offsets = jnp.repeat(jnp.arange(half_rows, dtype=jnp.int32), group_size)
    query_sets = (
        to_groups(first_half, KV_HEADS, group_size, HD),
        to_groups(second_half, KV_HEADS, group_size, HD),
    )
    position_sets = (first_start + offsets, second_start + offsets)
    last_positions = (first_start + half_rows - 1, second_start + half_rows - 1)
    row_total = half_rows * group_size
    empty_state = (
        jnp.full((KV_HEADS, row_total), negative_fill, jnp.float32),
        jnp.zeros((KV_HEADS, row_total), jnp.float32),
        jnp.zeros((KV_HEADS, row_total, HD), jnp.float32),
    )
    folder = make_folder(query_sets, position_sets, last_positions, KV_HEADS, HD, score_scale)
    final_sets = folder(
        (empty_state, empty_state),
        (
            lax.all_gather(key_states, "ctx", axis=1, tiled=True),
            lax.all_gather(value_states, "ctx", axis=1, tiled=True),
        ),
        jnp.int32(0),
    )
    first_out = finish(final_sets[0], half_rows, KV_HEADS, group_size, HD)
    second_out = finish(final_sets[1], half_rows, KV_HEADS, group_size, HD)
    attention = jnp.concatenate([first_out, second_out], axis=0)
    summed = residual[0].astype(jnp.float32) + lax.optimization_barrier(attention).astype(
        jnp.float32
    )
    normed = (
        summed * lax.rsqrt(jnp.mean(summed * summed, axis=-1, keepdims=True) + epsilon)
    ).astype(jnp.bfloat16)
    width_model = normed.shape[1]
    experts_each = ctx_count // PIECES
    expert_total = experts_each * exp_count
    pair_count = tok_rows * TOPK
    capacity = max(2, 2 * tok_rows * TOPK // expert_total)
    flat_ids = expert_ids[0].reshape(pair_count)
    onehot = (flat_ids[:, None] == jnp.arange(expert_total, dtype=jnp.int32)[None, :]).astype(
        jnp.int32
    )
    earlier = jnp.cumsum(onehot, axis=0) - onehot
    slot_index = jnp.sum(earlier * onehot, axis=1)
    owner_index = flat_ids // experts_each
    local_expert = flat_ids % experts_each
    target = (local_expert * exp_count + owner_index) * capacity + slot_index
    pair_token = jnp.arange(pair_count, dtype=jnp.int32) // TOPK
    slot_total = expert_total * capacity
    slot_table = jnp.full((slot_total,), tok_rows, jnp.int32).at[target].set(pair_token)
    padded = jnp.concatenate([normed, jnp.zeros((1, width_model), jnp.bfloat16)], axis=0)
    outgoing = padded[slot_table].reshape(experts_each, exp_count, capacity, width_model)
    arrived = lax.all_to_all(outgoing, "exp", split_axis=1, concat_axis=1, tiled=True)
    copies = jnp.broadcast_to(
        arrived[:, None], (experts_each, PIECES, exp_count, capacity, width_model)
    ).reshape(ctx_count, exp_count * capacity, width_model)
    gate_piece = gate_weight[0, 0]
    up_piece = up_weight[0, 0]
    down_piece = down_weight[0, 0]
    received = lax.all_to_all(copies, "ctx", split_axis=0, concat_axis=0, tiled=True)
    sources = received.shape[0]
    item_count = received.shape[1]
    flat_rows = received.reshape(sources * item_count, width_model)
    gate_part = contract_rows(flat_rows, gate_piece)
    up_part = contract_rows(flat_rows, up_piece)
    active = (jax.nn.silu(gate_part) * up_part).astype(jnp.bfloat16)
    partial_out = jnp.dot(active, down_piece, preferred_element_type=jnp.float32).astype(
        jnp.bfloat16
    )
    returned = lax.all_to_all(
        partial_out.reshape(sources, item_count, width_model),
        "ctx",
        split_axis=0,
        concat_axis=0,
        tiled=True,
    )
    piece_sum = jnp.sum(
        returned.reshape(experts_each, PIECES, exp_count, capacity, width_model).astype(
            jnp.float32
        ),
        axis=1,
    ).astype(jnp.bfloat16)
    arrived_back = lax.all_to_all(piece_sum, "exp", split_axis=1, concat_axis=1, tiled=True)
    gathered = arrived_back.reshape(slot_total, width_model)[target].astype(jnp.float32)
    weighted = gathered * route_weight[0]
    mixture = jnp.sum(weighted.reshape(tok_rows, TOPK, width_model), axis=1)
    return (summed + mixture).astype(jnp.bfloat16)[None]


AXES = ("ctx", "exp")


def spot(flat):
    ctx, exp = divmod(flat, 4)
    return ctx // 2, ctx % 2, exp // 2, exp % 2


def flat_of(z, x, y, core):
    return (z * 2 + x) * 4 + y * 2 + core


def move(array, rule):
    pairs = []
    for flat in range(32):
        there = rule(*spot(flat))
        if there is not None:
            pairs.append((flat, flat_of(*there)))
    return lax.ppermute(array, AXES, pairs)


def gather_pieces(weights):
    def first(z, x, y, core):
        return (z, x, y, 1 - core) if core == z % 2 else (z ^ 1, x, y, core)

    def over_x(z, x, y, core):
        return z, x ^ 1, y, core

    def to_core(z, x, y, core):
        return z, x, y, 1 - core

    near = [move(w, first) for w in weights]
    far = [move(w, over_x) for w in near]
    near_twin = [move(w, to_core) for w in near]
    far_twin = [move(w, to_core) for w in far]
    return near, near_twin, far, far_twin


def slot_targets(ids_row, z_here, y_here, capacity):
    expert_count = 8
    token_count = ids_row.shape[1]
    lanes = lax.broadcasted_iota(jnp.int32, (expert_count, token_count), 0)
    onehot = (lanes == ids_row).astype(jnp.float32)
    before = (
        lax.broadcasted_iota(jnp.int32, (token_count, token_count), 0)
        < lax.broadcasted_iota(jnp.int32, (token_count, token_count), 1)
    ).astype(jnp.bfloat16)
    earlier = jnp.dot(onehot.astype(jnp.bfloat16), before, preferred_element_type=jnp.float32)
    slot = jnp.sum(earlier * onehot, axis=0, keepdims=True).astype(jnp.int32)
    owner = lax.shift_right_logical(ids_row, 1)
    z_there = (ids_row & 1) * 2 + (owner & 1)
    y_there = lax.shift_right_logical(owner, 1)
    relative = (z_there ^ z_here) * 2 + (y_there ^ y_here)
    return relative * capacity + slot


def slot_matrix(ids_row, z_here, y_here, capacity):
    target = slot_targets(ids_row, z_here, y_here, capacity)
    rows = lax.broadcasted_iota(jnp.int32, (8 * capacity, ids_row.shape[1]), 0)
    return (rows == target).astype(jnp.bfloat16)


def attend_kernel(where_ref, ids_ref, queries_ref, residual_ref, *refs):
    kv_refs, summed_ref, out_refs = refs[:8], refs[8], refs[9:17]
    keys_ref, values_ref, bias_ref, mixed_ref = refs[17:]
    tokens = queries_ref.shape[0]
    group = HEADS // KV_HEADS
    ctx_here = where_ref[0]
    row = lax.broadcasted_iota(jnp.int32, (tokens, tokens), 0)
    column = lax.broadcasted_iota(jnp.int32, (tokens, tokens), 1)
    for k in range(8):
        span = slice(k * tokens, (k + 1) * tokens)
        block = kv_refs[k][...]
        keys_ref[span, :] = block[:, : KV_HEADS * HD]
        values_ref[span, :] = block[:, KV_HEADS * HD :]
        if k == 0:
            bias_ref[:, span] = jnp.where(column <= row, 0.0, negative_fill)
        else:
            bias_ref[:, span] = jnp.full(
                (tokens, tokens), jnp.where(ctx_here >= k, 0.0, negative_fill), jnp.float32
            )
    factor = math.log2(math.e) / math.sqrt(HD)
    heads_each = 2
    for first in range(0, HEADS, heads_each):
        kv_head = first // group
        side = slice(kv_head * HD, (kv_head + 1) * HD)
        rows = jnp.concatenate(
            [queries_ref[:, h * HD : (h + 1) * HD] for h in range(first, first + heads_each)], axis=0
        )
        scores = contract_rows(rows, keys_ref[:, side])
        scores = scores + jnp.concatenate([bias_ref[...]] * heads_each, axis=0)
        largest = jnp.max(scores, axis=1, keepdims=True)
        exponent = jnp.exp2((scores - largest) * factor)
        total = jnp.sum(exponent, axis=1, keepdims=True)
        product = jnp.dot(
            exponent.astype(jnp.bfloat16), values_ref[:, side], preferred_element_type=jnp.float32
        )
        result = product / total
        for j in range(heads_each):
            mixed_ref[:, (first + j) * HD : (first + j + 1) * HD] = result[
                j * tokens : (j + 1) * tokens
            ].astype(jnp.bfloat16)
    summed = residual_ref[...].astype(jnp.float32) + mixed_ref[...].astype(jnp.float32)
    summed_ref[...] = summed
    scale = lax.rsqrt(jnp.mean(summed * summed, axis=1, keepdims=True) + epsilon)
    normed = (summed * scale).astype(jnp.bfloat16)
    capacity = out_refs[0].shape[0]
    choose = slot_matrix(ids_ref[...], where_ref[1], where_ref[2], capacity)
    slots = jnp.dot(choose, normed, preferred_element_type=jnp.float32).astype(jnp.bfloat16)
    for k in range(8):
        out_refs[k][...] = slots[k * capacity : (k + 1) * capacity]


def expert_kernel(*refs):
    row_refs, weight_refs, out_refs = refs[:8], refs[8:20], refs[20:28]
    gate_ref, up_ref, down_ref, semaphores = refs[28:]
    piece = weight_refs[0].shape[0]
    copies = []
    for kind, target in enumerate((gate_ref, up_ref, down_ref)):
        row_of = []
        for j in range(PIECES):
            copy = pltpu.make_async_copy(
                weight_refs[kind * PIECES + j],
                target.at[pl.ds(j * piece, piece)],
                semaphores.at[kind, j],
            )
            row_of.append(copy)
        copies.append(row_of)
    for j in range(PIECES):
        copies[0][j].start()
        copies[1][j].start()
    for j in range(PIECES):
        copies[2][j].start()
    rows = jnp.concatenate([ref[...] for ref in row_refs], axis=0)
    actives = []
    for half in range(2):
        span = slice(half * 2 * piece, (half + 1) * 2 * piece)
        for j in (2 * half, 2 * half + 1):
            copies[0][j].wait()
            copies[1][j].wait()
        gate_part = contract_rows(rows, gate_ref[span, :])
        up_part = contract_rows(rows, up_ref[span, :])
        silu = gate_part / (1.0 + jnp.exp(-gate_part))
        actives.append((silu * up_part).astype(jnp.bfloat16))
    for j in range(PIECES):
        copies[2][j].wait()
    active = jnp.concatenate(actives, axis=1)
    capacity = out_refs[0].shape[0]
    result = jnp.dot(active, down_ref[...], preferred_element_type=jnp.float32).astype(jnp.bfloat16)
    for k in range(8):
        out_refs[k][...] = result[k * capacity : (k + 1) * capacity]


def combine_kernel(where_ref, ids_ref, route_ref, summed_ref, *refs):
    row_refs, out_ref = refs[:8], refs[8]
    capacity = row_refs[0].shape[0]
    choose = slot_matrix(ids_ref[...], where_ref[1], where_ref[2], capacity)
    rows = jnp.concatenate([ref[...] for ref in row_refs], axis=0)
    picked = lax.dot_general(
        choose, rows, (((0,), (0,)), ((), ())), preferred_element_type=jnp.float32
    )
    out_ref[...] = (summed_ref[...] + picked * route_ref[...]).astype(jnp.bfloat16)


IN_VMEM = pl.BlockSpec(memory_space=pltpu.VMEM)
IN_SMEM = pl.BlockSpec(memory_space=pltpu.SMEM)
ANYWHERE = pl.BlockSpec(memory_space=pl.ANY)


def shards_cube(
    residual,
    queries,
    key_states,
    value_states,
    expert_ids,
    route_weight,
    gate_weight,
    up_weight,
    down_weight,
):
    ctx_here = lax.axis_index("ctx")
    exp_here = lax.axis_index("exp")
    where = jnp.stack([ctx_here, ctx_here // 2, exp_here // 2]).astype(jnp.int32)
    tokens, width = residual.shape[1:]
    piece = gate_weight.shape[2]
    capacity = max(2, 2 * tokens * TOPK // 8)
    ids_row = expert_ids[0].reshape(1, tokens)
    kv_own = jnp.concatenate([key_states[0], value_states[0]], axis=1)
    kv_blocks = [kv_own]
    for k in range(1, 8):
        def later(z, x, y, core, k=k):
            ctx = 2 * z + x + k
            return (ctx // 2, ctx % 2, y, core) if ctx < 8 else None

        kv_blocks.append(move(kv_own, later))
    near, near_twin, far, far_twin = gather_pieces([gate_weight[0, 0], up_weight[0, 0], down_weight[0, 0]])
    slot_shape = jax.ShapeDtypeStruct((capacity, width), jnp.bfloat16)
    keys_all = 8 * tokens
    first_out = pl.pallas_call(
        attend_kernel,
        out_shape=[jax.ShapeDtypeStruct((tokens, width), jnp.float32)] + [slot_shape] * 8,
        in_specs=[IN_SMEM] + [IN_VMEM] * 11,
        out_specs=[IN_VMEM] * 9,
        scratch_shapes=[
            pltpu.VMEM((keys_all, KV_HEADS * HD), jnp.bfloat16),
            pltpu.VMEM((keys_all, KV_HEADS * HD), jnp.bfloat16),
            pltpu.VMEM((tokens, keys_all), jnp.float32),
            pltpu.VMEM((tokens, width), jnp.bfloat16),
        ],
        compiler_params=pltpu.CompilerParams(vmem_limit_bytes=40 << 20),
        cost_estimate=pl.CostEstimate(
            flops=4 * tokens * keys_all * HEADS * HD,
            bytes_accessed=8 * tokens * width,
            transcendentals=tokens * keys_all * HEADS,
        ),
        name="attend",
    )(where, ids_row, queries[0], residual[0], *kv_blocks)
    summed, outgoing = first_out[0], first_out[1:]

    def swap(array, k):
        if k == 0:
            return array
        return move(array, lambda z, x, y, core: (z ^ (k >> 1), x, y ^ (k & 1), core))

    arrived = [swap(outgoing[k], k) for k in range(8)]
    pieces = []
    for kind in range(3):
        pieces += [near[kind], near_twin[kind], far[kind], far_twin[kind]]
    results = pl.pallas_call(
        expert_kernel,
        out_shape=[slot_shape] * 8,
        in_specs=[IN_VMEM] * 8 + [ANYWHERE] * 12,
        out_specs=[IN_VMEM] * 8,
        scratch_shapes=[
            pltpu.VMEM((PIECES * piece, width), jnp.bfloat16),
            pltpu.VMEM((PIECES * piece, width), jnp.bfloat16),
            pltpu.VMEM((PIECES * piece, width), jnp.bfloat16),
            pltpu.SemaphoreType.DMA((3, PIECES)),
        ],
        compiler_params=pltpu.CompilerParams(vmem_limit_bytes=48 << 20),
        cost_estimate=pl.CostEstimate(
            flops=6 * 8 * capacity * PIECES * piece * width,
            bytes_accessed=6 * PIECES * piece * width,
            transcendentals=8 * capacity * PIECES * piece,
        ),
        name="experts",
    )(*arrived, *pieces)
    returned = [swap(results[k], k) for k in range(8)]
    output = pl.pallas_call(
        combine_kernel,
        out_shape=jax.ShapeDtypeStruct((tokens, width), jnp.bfloat16),
        in_specs=[IN_SMEM] + [IN_VMEM] * 11,
        out_specs=IN_VMEM,
        compiler_params=pltpu.CompilerParams(vmem_limit_bytes=24 << 20),
        cost_estimate=pl.CostEstimate(
            flops=2 * tokens * 8 * capacity * width,
            bytes_accessed=12 * tokens * width,
            transcendentals=0,
        ),
        name="combine",
    )(where, ids_row, route_weight[0], summed, *returned)
    return output[None]


def solution(mesh):
    in_specs = (
        P("exp", "ctx", None),
        P("exp", "ctx", None),
        P("exp", "ctx", None),
        P("exp", "ctx", None),
        P("exp", "ctx", None),
        P("exp", "ctx", None),
        P("exp", "ctx", None, None),
        P("exp", "ctx", None, None),
        P("exp", "ctx", None, None),
    )
    out_specs = P("exp", "ctx", None)
    cube = mesh.shape["ctx"] == 8 and mesh.shape["exp"] == 4
    body = shards_cube if cube else shards
    return jax.shard_map(body, mesh=mesh, in_specs=in_specs, out_specs=out_specs, check_vma=False)
```

```python
from functools import partial
import math

import jax
import jax.numpy as jnp
from jax import lax
from jax.experimental import pallas as pl
from jax.experimental.pallas import tpu as pltpu
from jax.sharding import PartitionSpec as P

HD = 128
HEADS = 16
KV_HEADS = 2
PIECES = 4
TOPK = 1


negative_fill = -1e30
epsilon = 1e-06


def contract_rows(left_rows, weight_rows):
    return lax.dot_general(
        left_rows, weight_rows, (((1,), (1,)), ((), ())), preferred_element_type=jnp.float32
    )


def to_groups(half_block, heads_kv, group_size, head_dim):
    token_count = half_block.shape[0]
    shaped = half_block.reshape(token_count, heads_kv, group_size, head_dim)
    return jnp.transpose(shaped, (1, 0, 2, 3)).reshape(heads_kv, token_count * group_size, head_dim)


def keep_current(current):
    return current


def block_update(current, query_rows, query_pos, key_block, value_block, key_start, score_scale):
    running_max, running_total, accumulated = current
    scores = (
        jnp.einsum("gqd,kgd->gqk", query_rows, key_block, preferred_element_type=jnp.float32)
        * score_scale
    )
    key_pos = key_start + jnp.arange(key_block.shape[0], dtype=jnp.int32)
    allowed = key_pos[None, None, :] <= query_pos[None, :, None]
    scores = jnp.where(allowed, scores, negative_fill)
    new_max = jnp.maximum(running_max, jnp.max(scores, axis=-1))
    rescale = jnp.exp(running_max - new_max)
    exponent = jnp.where(allowed, jnp.exp(scores - new_max[..., None]), 0.0)
    new_total = running_total * rescale + jnp.sum(exponent, axis=-1)
    product = jnp.einsum(
        "gqk,kgd->gqd",
        exponent.astype(jnp.bfloat16),
        value_block,
        preferred_element_type=jnp.float32,
    )
    return (new_max, new_total, accumulated * rescale[..., None] + product)


def make_folder(query_sets, position_sets, last_positions, heads_kv, head_dim, score_scale):

    def fold_keys(running, key_piece, first_key):
        key_part, value_part = key_piece
        key_count = key_part.shape[1]
        key_width = math.gcd(key_count, 512)
        key_rows = key_part.reshape(key_count, heads_kv, head_dim)
        value_rows = value_part.reshape(key_count, heads_kv, head_dim)

        def one_block(block_index, current_sets):
            offset = block_index * key_width
            key_block = lax.dynamic_slice_in_dim(key_rows, offset, key_width, 0)
            value_block = lax.dynamic_slice_in_dim(value_rows, offset, key_width, 0)
            updated = []
            for current, query_rows, query_pos, last_pos in zip(
                current_sets, query_sets, position_sets, last_positions
            ):
                step_fn = partial(
                    block_update,
                    query_rows=query_rows,
                    query_pos=query_pos,
                    key_block=key_block,
                    value_block=value_block,
                    key_start=offset,
                    score_scale=score_scale,
                )
                updated.append(lax.cond(offset <= last_pos, step_fn, keep_current, current))
            return tuple(updated)

        return lax.fori_loop(0, key_count // key_width, one_block, running)

    return fold_keys


def finish(current, token_count, heads_kv, group_size, head_dim):
    running_max, running_total, accumulated = current
    result = accumulated / running_total[..., None]
    shaped = result.reshape(heads_kv, token_count, group_size, head_dim)
    return (
        jnp.transpose(shaped, (1, 0, 2, 3))
        .reshape(token_count, heads_kv * group_size * head_dim)
        .astype(jnp.bfloat16)
    )


def shards(
    residual,
    queries,
    key_states,
    value_states,
    expert_ids,
    route_weight,
    gate_weight,
    up_weight,
    down_weight,
):
    ctx_count = lax.axis_size("ctx")
    exp_count = lax.axis_size("exp")
    ctx_rank = lax.axis_index("ctx")
    tok_rows = residual.shape[1]
    half_rows = tok_rows // 2
    group_size = HEADS // KV_HEADS
    score_scale = 1.0 / math.sqrt(HD)
    local_queries = queries[0]
    first_half = local_queries[:half_rows]
    second_half = local_queries[half_rows:]
    first_start = ctx_rank * tok_rows
    second_start = first_start + half_rows
    offsets = jnp.repeat(jnp.arange(half_rows, dtype=jnp.int32), group_size)
    query_sets = (
        to_groups(first_half, KV_HEADS, group_size, HD),
        to_groups(second_half, KV_HEADS, group_size, HD),
    )
    position_sets = (first_start + offsets, second_start + offsets)
    last_positions = (first_start + half_rows - 1, second_start + half_rows - 1)
    row_total = half_rows * group_size
    empty_state = (
        jnp.full((KV_HEADS, row_total), negative_fill, jnp.float32),
        jnp.zeros((KV_HEADS, row_total), jnp.float32),
        jnp.zeros((KV_HEADS, row_total, HD), jnp.float32),
    )
    folder = make_folder(query_sets, position_sets, last_positions, KV_HEADS, HD, score_scale)
    final_sets = folder(
        (empty_state, empty_state),
        (
            lax.all_gather(key_states, "ctx", axis=1, tiled=True),
            lax.all_gather(value_states, "ctx", axis=1, tiled=True),
        ),
        jnp.int32(0),
    )
    first_out = finish(final_sets[0], half_rows, KV_HEADS, group_size, HD)
    second_out = finish(final_sets[1], half_rows, KV_HEADS, group_size, HD)
    attention = jnp.concatenate([first_out, second_out], axis=0)
    summed = residual[0].astype(jnp.float32) + lax.optimization_barrier(attention).astype(
        jnp.float32
    )
    normed = (
        summed * lax.rsqrt(jnp.mean(summed * summed, axis=-1, keepdims=True) + epsilon)
    ).astype(jnp.bfloat16)
    width_model = normed.shape[1]
    experts_each = ctx_count // PIECES
    expert_total = experts_each * exp_count
    pair_count = tok_rows * TOPK
    capacity = max(2, 2 * tok_rows * TOPK // expert_total)
    flat_ids = expert_ids[0].reshape(pair_count)
    onehot = (flat_ids[:, None] == jnp.arange(expert_total, dtype=jnp.int32)[None, :]).astype(
        jnp.int32
    )
    earlier = jnp.cumsum(onehot, axis=0) - onehot
    slot_index = jnp.sum(earlier * onehot, axis=1)
    owner_index = flat_ids // experts_each
    local_expert = flat_ids % experts_each
    target = (local_expert * exp_count + owner_index) * capacity + slot_index
    pair_token = jnp.arange(pair_count, dtype=jnp.int32) // TOPK
    slot_total = expert_total * capacity
    slot_table = jnp.full((slot_total,), tok_rows, jnp.int32).at[target].set(pair_token)
    padded = jnp.concatenate([normed, jnp.zeros((1, width_model), jnp.bfloat16)], axis=0)
    outgoing = padded[slot_table].reshape(experts_each, exp_count, capacity, width_model)
    arrived = lax.all_to_all(outgoing, "exp", split_axis=1, concat_axis=1, tiled=True)
    copies = jnp.broadcast_to(
        arrived[:, None], (experts_each, PIECES, exp_count, capacity, width_model)
    ).reshape(ctx_count, exp_count * capacity, width_model)
    gate_piece = gate_weight[0, 0]
    up_piece = up_weight[0, 0]
    down_piece = down_weight[0, 0]
    received = lax.all_to_all(copies, "ctx", split_axis=0, concat_axis=0, tiled=True)
    sources = received.shape[0]
    item_count = received.shape[1]
    flat_rows = received.reshape(sources * item_count, width_model)
    gate_part = contract_rows(flat_rows, gate_piece)
    up_part = contract_rows(flat_rows, up_piece)
    active = (jax.nn.silu(gate_part) * up_part).astype(jnp.bfloat16)
    partial_out = jnp.dot(active, down_piece, preferred_element_type=jnp.float32).astype(
        jnp.bfloat16
    )
    returned = lax.all_to_all(
        partial_out.reshape(sources, item_count, width_model),
        "ctx",
        split_axis=0,
        concat_axis=0,
        tiled=True,
    )
    piece_sum = jnp.sum(
        returned.reshape(experts_each, PIECES, exp_count, capacity, width_model).astype(
            jnp.float32
        ),
        axis=1,
    ).astype(jnp.bfloat16)
    arrived_back = lax.all_to_all(piece_sum, "exp", split_axis=1, concat_axis=1, tiled=True)
    gathered = arrived_back.reshape(slot_total, width_model)[target].astype(jnp.float32)
    weighted = gathered * route_weight[0]
    mixture = jnp.sum(weighted.reshape(tok_rows, TOPK, width_model), axis=1)
    return (summed + mixture).astype(jnp.bfloat16)[None]


AXES = ("ctx", "exp")


def spot(flat):
    ctx, exp = divmod(flat, 4)
    return ctx // 2, ctx % 2, exp // 2, exp % 2


def flat_of(z, x, y, core):
    return (z * 2 + x) * 4 + y * 2 + core


def move(array, rule):
    pairs = []
    for flat in range(32):
        there = rule(*spot(flat))
        if there is not None:
            pairs.append((flat, flat_of(*there)))
    return lax.ppermute(array, AXES, pairs)


def is_home(z, core):
    return core == z % 2


def to_twin(z, x, y, core):
    return z, x, y, 1 - core


def first_hop(z, x, y, core):
    return (z, x ^ 1, y, 1 - core) if is_home(z, core) else (z ^ 1, x, y, core)


def second_hop(z, x, y, core):
    return (z, x ^ 1, y, core) if is_home(z, core) else None


def home_to_twin(z, x, y, core):
    return (z, x, y, 1 - core) if is_home(z, core) else None


def pack_halves(gate, up, down):
    half = gate.shape[0] // 2
    return [
        jnp.concatenate([w[k * half : (k + 1) * half] for w in (gate, up, down)], axis=0)
        for k in range(2)
    ]


def slot_targets(ids_row, z_here, y_here, capacity):
    expert_count = 8
    token_count = ids_row.shape[1]
    lanes = lax.broadcasted_iota(jnp.int32, (expert_count, token_count), 0)
    onehot = (lanes == ids_row).astype(jnp.float32)
    before = (
        lax.broadcasted_iota(jnp.int32, (token_count, token_count), 0)
        < lax.broadcasted_iota(jnp.int32, (token_count, token_count), 1)
    ).astype(jnp.bfloat16)
    earlier = jnp.dot(onehot.astype(jnp.bfloat16), before, preferred_element_type=jnp.float32)
    slot = jnp.sum(earlier * onehot, axis=0, keepdims=True).astype(jnp.int32)
    owner = lax.shift_right_logical(ids_row, 1)
    z_there = (ids_row & 1) * 2 + (owner & 1)
    y_there = lax.shift_right_logical(owner, 1)
    relative = (z_there ^ z_here) * 2 + (y_there ^ y_here)
    return relative * capacity + slot


def slot_matrix(ids_row, z_here, y_here, capacity):
    target = slot_targets(ids_row, z_here, y_here, capacity)
    rows = lax.broadcasted_iota(jnp.int32, (8 * capacity, ids_row.shape[1]), 0)
    return (rows == target).astype(jnp.bfloat16)


def attend_kernel(where_ref, ids_ref, queries_ref, residual_ref, *refs):
    kv_refs, summed_ref, out_refs = refs[:8], refs[8], refs[9:17]
    keys_ref, values_ref, bias_ref, mixed_ref = refs[17:]
    tokens = queries_ref.shape[0]
    group = HEADS // KV_HEADS
    ctx_here = where_ref[0]
    row = lax.broadcasted_iota(jnp.int32, (tokens, tokens), 0)
    column = lax.broadcasted_iota(jnp.int32, (tokens, tokens), 1)
    for k in range(8):
        span = slice(k * tokens, (k + 1) * tokens)
        block = kv_refs[k][...]
        keys_ref[span, :] = block[:, : KV_HEADS * HD]
        values_ref[span, :] = block[:, KV_HEADS * HD :]
        if k == 0:
            bias_ref[:, span] = jnp.where(column <= row, 0.0, negative_fill)
        else:
            bias_ref[:, span] = jnp.full(
                (tokens, tokens), jnp.where(ctx_here >= k, 0.0, negative_fill), jnp.float32
            )
    factor = math.log2(math.e) / math.sqrt(HD)
    heads_each = 2
    for first in range(0, HEADS, heads_each):
        kv_head = first // group
        side = slice(kv_head * HD, (kv_head + 1) * HD)
        rows = jnp.concatenate(
            [queries_ref[:, h * HD : (h + 1) * HD] for h in range(first, first + heads_each)], axis=0
        )
        scores = contract_rows(rows, keys_ref[:, side])
        scores = scores + jnp.concatenate([bias_ref[...]] * heads_each, axis=0)
        largest = jnp.max(scores, axis=1, keepdims=True)
        exponent = jnp.exp2((scores - largest) * factor)
        total = jnp.sum(exponent, axis=1, keepdims=True)
        product = jnp.dot(
            exponent.astype(jnp.bfloat16), values_ref[:, side], preferred_element_type=jnp.float32
        )
        result = product / total
        for j in range(heads_each):
            mixed_ref[:, (first + j) * HD : (first + j + 1) * HD] = result[
                j * tokens : (j + 1) * tokens
            ].astype(jnp.bfloat16)
    summed = residual_ref[...].astype(jnp.float32) + mixed_ref[...].astype(jnp.float32)
    summed_ref[...] = summed
    scale = lax.rsqrt(jnp.mean(summed * summed, axis=1, keepdims=True) + epsilon)
    normed = (summed * scale).astype(jnp.bfloat16)
    capacity = out_refs[0].shape[0]
    choose = slot_matrix(ids_ref[...], where_ref[1], where_ref[2], capacity)
    slots = jnp.dot(choose, normed, preferred_element_type=jnp.float32).astype(jnp.bfloat16)
    for k in range(8):
        out_refs[k][...] = slots[k * capacity : (k + 1) * capacity]


def expert_kernel(where_ref, *refs):
    row_refs, pack_refs, out_refs = refs[:8], refs[8:20], refs[20:28]
    gate_ref, up_ref, down_ref, semaphores = refs[28:]
    own, own_twin, one, one_twin, last, last_twin = [pack_refs[2 * i : 2 * i + 2] for i in range(6)]
    at_home = where_ref[3] == 1
    away = jnp.logical_not(at_home)
    strip = pack_refs[0].shape[0] // 3
    targets = (gate_ref, up_ref, down_ref)

    def copies_of(pair, place, kinds):
        return [
            pltpu.make_async_copy(
                pair[h].at[pl.ds(kind * strip, strip)],
                targets[kind].at[pl.ds((2 * place + h) * strip, strip)],
                semaphores.at[kind, place, h],
            )
            for kind in kinds
            for h in range(2)
        ]

    def start(pair, place):
        for copy in copies_of(pair, place, range(3)):
            copy.start()

    def wait(pair, place, kinds):
        for copy in copies_of(pair, place, kinds):
            copy.wait()

    @pl.when(at_home)
    def _():
        start(own, 0)

    @pl.when(away)
    def _():
        start(own_twin, 0)

    start(one, 1)
    start(one_twin, 2)

    @pl.when(at_home)
    def _():
        start(last, 3)

    @pl.when(away)
    def _():
        start(last_twin, 3)

    rows = jnp.concatenate([ref[...] for ref in row_refs], axis=0)
    sources = (own, one, one_twin, last)
    actives = []
    for half in range(2):
        span = slice(half * 4 * strip, (half + 1) * 4 * strip)
        for place in (2 * half, 2 * half + 1):
            wait(sources[place], place, (0, 1))
        gate_part = contract_rows(rows, gate_ref[span, :])
        up_part = contract_rows(rows, up_ref[span, :])
        silu = gate_part / (1.0 + jnp.exp(-gate_part))
        actives.append((silu * up_part).astype(jnp.bfloat16))
    for place in range(PIECES):
        wait(sources[place], place, (2,))
    active = jnp.concatenate(actives, axis=1)
    capacity = out_refs[0].shape[0]
    result = jnp.dot(active, down_ref[...], preferred_element_type=jnp.float32).astype(jnp.bfloat16)
    for k in range(8):
        out_refs[k][...] = result[k * capacity : (k + 1) * capacity]


def combine_kernel(where_ref, ids_ref, route_ref, summed_ref, *refs):
    row_refs, out_ref = refs[:8], refs[8]
    capacity = row_refs[0].shape[0]
    choose = slot_matrix(ids_ref[...], where_ref[1], where_ref[2], capacity)
    rows = jnp.concatenate([ref[...] for ref in row_refs], axis=0)
    picked = lax.dot_general(
        choose, rows, (((0,), (0,)), ((), ())), preferred_element_type=jnp.float32
    )
    out_ref[...] = (summed_ref[...] + picked * route_ref[...]).astype(jnp.bfloat16)


IN_VMEM = pl.BlockSpec(memory_space=pltpu.VMEM)
IN_SMEM = pl.BlockSpec(memory_space=pltpu.SMEM)
ANYWHERE = pl.BlockSpec(memory_space=pl.ANY)


def shards_cube(
    residual,
    queries,
    key_states,
    value_states,
    expert_ids,
    route_weight,
    gate_weight,
    up_weight,
    down_weight,
):
    ctx_here = lax.axis_index("ctx")
    exp_here = lax.axis_index("exp")
    home = ((ctx_here // 2) % 2 == exp_here % 2).astype(jnp.int32)
    where = jnp.stack([ctx_here, ctx_here // 2, exp_here // 2, home]).astype(jnp.int32)
    tokens, width = residual.shape[1:]
    piece = gate_weight.shape[2]
    capacity = max(2, 2 * tokens * TOPK // 8)
    ids_row = expert_ids[0].reshape(1, tokens)
    kv_own = jnp.concatenate([key_states[0], value_states[0]], axis=1)
    kv_blocks = {0: kv_own}

    def send_keys(block, k):
        def later(z, x, y, core):
            ctx = 2 * z + x + k
            return (ctx // 2, ctx % 2, y, core) if ctx < 8 else None

        kv_blocks[k] = move(block, later)

    own = pack_halves(gate_weight[0, 0], up_weight[0, 0], down_weight[0, 0])
    for k in (7, 6):
        send_keys(kv_own, k)
    own[0], own[1], kv_blocks[7], kv_blocks[6], kv_next = lax.optimization_barrier(
        (own[0], own[1], kv_blocks[7], kv_blocks[6], kv_own)
    )
    one_first = move(own[0], first_hop)
    for k in (4, 5, 3, 2, 1):
        send_keys(kv_next, k)
    kv_list = [kv_blocks[k] for k in range(1, 8)]
    one_first, own[0], own[1], *kv_list = lax.optimization_barrier(
        (one_first, own[0], own[1], *kv_list)
    )
    one_second = move(own[1], first_hop)
    own_twin = [move(w, home_to_twin) for w in own]
    twin_first = move(one_first, to_twin)
    slot_shape = jax.ShapeDtypeStruct((capacity, width), jnp.bfloat16)
    keys_all = 8 * tokens
    first_out = pl.pallas_call(
        attend_kernel,
        out_shape=[jax.ShapeDtypeStruct((tokens, width), jnp.float32)] + [slot_shape] * 8,
        in_specs=[IN_SMEM] + [IN_VMEM] * 11,
        out_specs=[IN_VMEM] * 9,
        scratch_shapes=[
            pltpu.VMEM((keys_all, KV_HEADS * HD), jnp.bfloat16),
            pltpu.VMEM((keys_all, KV_HEADS * HD), jnp.bfloat16),
            pltpu.VMEM((tokens, keys_all), jnp.float32),
            pltpu.VMEM((tokens, width), jnp.bfloat16),
        ],
        compiler_params=pltpu.CompilerParams(vmem_limit_bytes=16 << 20),
        cost_estimate=pl.CostEstimate(
            flops=4 * tokens * keys_all * HEADS * HD,
            bytes_accessed=8 * tokens * width,
            transcendentals=tokens * keys_all * HEADS,
        ),
        name="attend",
    )(where, ids_row, queries[0], residual[0], kv_own, *kv_list)
    summed, outgoing = first_out[0], list(first_out[1:])

    def swap(array, k):
        if k == 0:
            return array
        return move(array, lambda z, x, y, core: (z ^ (k >> 1), x, y ^ (k & 1), core))

    early, late = (4, 2, 3, 1), (5, 6, 7)
    held = lax.optimization_barrier((*outgoing, *own_twin, twin_first))
    outgoing, own_twin, twin_first = list(held[:8]), list(held[8:10]), held[10]
    arrived = [swap(outgoing[k], k) if k in early else outgoing[k] for k in range(8)]
    one_first, one_second, *arrived = lax.optimization_barrier((one_first, one_second, *arrived))
    one = [one_first, one_second]
    last = [move(w, second_hop) for w in one]
    arrived = [swap(arrived[k], k) if k in late else arrived[k] for k in range(8)]
    last[0], one[1], *arrived = lax.optimization_barrier((last[0], one[1], *arrived))
    one_twin = [twin_first, move(one[1], to_twin)]
    last_twin = [move(w, home_to_twin) for w in last]
    packs = own + own_twin + one + one_twin + last + last_twin
    results = pl.pallas_call(
        expert_kernel,
        out_shape=[slot_shape] * 8,
        in_specs=[IN_SMEM] + [IN_VMEM] * 8 + [ANYWHERE] * 12,
        out_specs=[IN_VMEM] * 8,
        scratch_shapes=[
            pltpu.VMEM((PIECES * piece, width), jnp.bfloat16),
            pltpu.VMEM((PIECES * piece, width), jnp.bfloat16),
            pltpu.VMEM((PIECES * piece, width), jnp.bfloat16),
            pltpu.SemaphoreType.DMA((3, PIECES, 2)),
        ],
        compiler_params=pltpu.CompilerParams(vmem_limit_bytes=24 << 20),
        cost_estimate=pl.CostEstimate(
            flops=6 * 8 * capacity * PIECES * piece * width,
            bytes_accessed=6 * PIECES * piece * width,
            transcendentals=8 * capacity * PIECES * piece,
        ),
        name="experts",
    )(where, *[arrived[k] for k in range(8)], *packs)
    returned = [swap(results[k], k) for k in range(8)]
    output = pl.pallas_call(
        combine_kernel,
        out_shape=jax.ShapeDtypeStruct((tokens, width), jnp.bfloat16),
        in_specs=[IN_SMEM] + [IN_VMEM] * 11,
        out_specs=IN_VMEM,
        compiler_params=pltpu.CompilerParams(vmem_limit_bytes=10 << 20),
        cost_estimate=pl.CostEstimate(
            flops=2 * tokens * 8 * capacity * width,
            bytes_accessed=12 * tokens * width,
            transcendentals=0,
        ),
        name="combine",
    )(where, ids_row, route_weight[0], summed, *returned)
    return output[None]


def solution(mesh):
    in_specs = (
        P("exp", "ctx", None),
        P("exp", "ctx", None),
        P("exp", "ctx", None),
        P("exp", "ctx", None),
        P("exp", "ctx", None),
        P("exp", "ctx", None),
        P("exp", "ctx", None, None),
        P("exp", "ctx", None, None),
        P("exp", "ctx", None, None),
    )
    out_specs = P("exp", "ctx", None)
    cube = mesh.shape["ctx"] == 8 and mesh.shape["exp"] == 4
    body = shards_cube if cube else shards
    return jax.shard_map(body, mesh=mesh, in_specs=in_specs, out_specs=out_specs, check_vma=False)
```

```python
from functools import partial
import math

import jax
import jax.numpy as jnp
from jax import lax
from jax.experimental import pallas as pl
from jax.experimental.pallas import tpu as pltpu
from jax.sharding import PartitionSpec as P

HD = 128
HEADS = 16
KV_HEADS = 2
PIECES = 4
TOPK = 1


negative_fill = -1e30
epsilon = 1e-06


def contract_rows(left_rows, weight_rows):
    return lax.dot_general(
        left_rows, weight_rows, (((1,), (1,)), ((), ())), preferred_element_type=jnp.float32
    )


def to_groups(half_block, heads_kv, group_size, head_dim):
    token_count = half_block.shape[0]
    shaped = half_block.reshape(token_count, heads_kv, group_size, head_dim)
    return jnp.transpose(shaped, (1, 0, 2, 3)).reshape(heads_kv, token_count * group_size, head_dim)


def keep_current(current):
    return current


def block_update(current, query_rows, query_pos, key_block, value_block, key_start, score_scale):
    running_max, running_total, accumulated = current
    scores = (
        jnp.einsum("gqd,kgd->gqk", query_rows, key_block, preferred_element_type=jnp.float32)
        * score_scale
    )
    key_pos = key_start + jnp.arange(key_block.shape[0], dtype=jnp.int32)
    allowed = key_pos[None, None, :] <= query_pos[None, :, None]
    scores = jnp.where(allowed, scores, negative_fill)
    new_max = jnp.maximum(running_max, jnp.max(scores, axis=-1))
    rescale = jnp.exp(running_max - new_max)
    exponent = jnp.where(allowed, jnp.exp(scores - new_max[..., None]), 0.0)
    new_total = running_total * rescale + jnp.sum(exponent, axis=-1)
    product = jnp.einsum(
        "gqk,kgd->gqd",
        exponent.astype(jnp.bfloat16),
        value_block,
        preferred_element_type=jnp.float32,
    )
    return (new_max, new_total, accumulated * rescale[..., None] + product)


def make_folder(query_sets, position_sets, last_positions, heads_kv, head_dim, score_scale):

    def fold_keys(running, key_piece, first_key):
        key_part, value_part = key_piece
        key_count = key_part.shape[1]
        key_width = math.gcd(key_count, 512)
        key_rows = key_part.reshape(key_count, heads_kv, head_dim)
        value_rows = value_part.reshape(key_count, heads_kv, head_dim)

        def one_block(block_index, current_sets):
            offset = block_index * key_width
            key_block = lax.dynamic_slice_in_dim(key_rows, offset, key_width, 0)
            value_block = lax.dynamic_slice_in_dim(value_rows, offset, key_width, 0)
            updated = []
            for current, query_rows, query_pos, last_pos in zip(
                current_sets, query_sets, position_sets, last_positions
            ):
                step_fn = partial(
                    block_update,
                    query_rows=query_rows,
                    query_pos=query_pos,
                    key_block=key_block,
                    value_block=value_block,
                    key_start=offset,
                    score_scale=score_scale,
                )
                updated.append(lax.cond(offset <= last_pos, step_fn, keep_current, current))
            return tuple(updated)

        return lax.fori_loop(0, key_count // key_width, one_block, running)

    return fold_keys


def finish(current, token_count, heads_kv, group_size, head_dim):
    running_max, running_total, accumulated = current
    result = accumulated / running_total[..., None]
    shaped = result.reshape(heads_kv, token_count, group_size, head_dim)
    return (
        jnp.transpose(shaped, (1, 0, 2, 3))
        .reshape(token_count, heads_kv * group_size * head_dim)
        .astype(jnp.bfloat16)
    )


def shards(
    residual,
    queries,
    key_states,
    value_states,
    expert_ids,
    route_weight,
    gate_weight,
    up_weight,
    down_weight,
):
    ctx_count = lax.axis_size("ctx")
    exp_count = lax.axis_size("exp")
    ctx_rank = lax.axis_index("ctx")
    tok_rows = residual.shape[1]
    half_rows = tok_rows // 2
    group_size = HEADS // KV_HEADS
    score_scale = 1.0 / math.sqrt(HD)
    local_queries = queries[0]
    first_half = local_queries[:half_rows]
    second_half = local_queries[half_rows:]
    first_start = ctx_rank * tok_rows
    second_start = first_start + half_rows
    offsets = jnp.repeat(jnp.arange(half_rows, dtype=jnp.int32), group_size)
    query_sets = (
        to_groups(first_half, KV_HEADS, group_size, HD),
        to_groups(second_half, KV_HEADS, group_size, HD),
    )
    position_sets = (first_start + offsets, second_start + offsets)
    last_positions = (first_start + half_rows - 1, second_start + half_rows - 1)
    row_total = half_rows * group_size
    empty_state = (
        jnp.full((KV_HEADS, row_total), negative_fill, jnp.float32),
        jnp.zeros((KV_HEADS, row_total), jnp.float32),
        jnp.zeros((KV_HEADS, row_total, HD), jnp.float32),
    )
    folder = make_folder(query_sets, position_sets, last_positions, KV_HEADS, HD, score_scale)
    final_sets = folder(
        (empty_state, empty_state),
        (
            lax.all_gather(key_states, "ctx", axis=1, tiled=True),
            lax.all_gather(value_states, "ctx", axis=1, tiled=True),
        ),
        jnp.int32(0),
    )
    first_out = finish(final_sets[0], half_rows, KV_HEADS, group_size, HD)
    second_out = finish(final_sets[1], half_rows, KV_HEADS, group_size, HD)
    attention = jnp.concatenate([first_out, second_out], axis=0)
    summed = residual[0].astype(jnp.float32) + lax.optimization_barrier(attention).astype(
        jnp.float32
    )
    normed = (
        summed * lax.rsqrt(jnp.mean(summed * summed, axis=-1, keepdims=True) + epsilon)
    ).astype(jnp.bfloat16)
    width_model = normed.shape[1]
    experts_each = ctx_count // PIECES
    expert_total = experts_each * exp_count
    pair_count = tok_rows * TOPK
    capacity = max(2, 2 * tok_rows * TOPK // expert_total)
    flat_ids = expert_ids[0].reshape(pair_count)
    onehot = (flat_ids[:, None] == jnp.arange(expert_total, dtype=jnp.int32)[None, :]).astype(
        jnp.int32
    )
    earlier = jnp.cumsum(onehot, axis=0) - onehot
    slot_index = jnp.sum(earlier * onehot, axis=1)
    owner_index = flat_ids // experts_each
    local_expert = flat_ids % experts_each
    target = (local_expert * exp_count + owner_index) * capacity + slot_index
    pair_token = jnp.arange(pair_count, dtype=jnp.int32) // TOPK
    slot_total = expert_total * capacity
    slot_table = jnp.full((slot_total,), tok_rows, jnp.int32).at[target].set(pair_token)
    padded = jnp.concatenate([normed, jnp.zeros((1, width_model), jnp.bfloat16)], axis=0)
    outgoing = padded[slot_table].reshape(experts_each, exp_count, capacity, width_model)
    arrived = lax.all_to_all(outgoing, "exp", split_axis=1, concat_axis=1, tiled=True)
    copies = jnp.broadcast_to(
        arrived[:, None], (experts_each, PIECES, exp_count, capacity, width_model)
    ).reshape(ctx_count, exp_count * capacity, width_model)
    gate_piece = gate_weight[0, 0]
    up_piece = up_weight[0, 0]
    down_piece = down_weight[0, 0]
    received = lax.all_to_all(copies, "ctx", split_axis=0, concat_axis=0, tiled=True)
    sources = received.shape[0]
    item_count = received.shape[1]
    flat_rows = received.reshape(sources * item_count, width_model)
    gate_part = contract_rows(flat_rows, gate_piece)
    up_part = contract_rows(flat_rows, up_piece)
    active = (jax.nn.silu(gate_part) * up_part).astype(jnp.bfloat16)
    partial_out = jnp.dot(active, down_piece, preferred_element_type=jnp.float32).astype(
        jnp.bfloat16
    )
    returned = lax.all_to_all(
        partial_out.reshape(sources, item_count, width_model),
        "ctx",
        split_axis=0,
        concat_axis=0,
        tiled=True,
    )
    piece_sum = jnp.sum(
        returned.reshape(experts_each, PIECES, exp_count, capacity, width_model).astype(
            jnp.float32
        ),
        axis=1,
    ).astype(jnp.bfloat16)
    arrived_back = lax.all_to_all(piece_sum, "exp", split_axis=1, concat_axis=1, tiled=True)
    gathered = arrived_back.reshape(slot_total, width_model)[target].astype(jnp.float32)
    weighted = gathered * route_weight[0]
    mixture = jnp.sum(weighted.reshape(tok_rows, TOPK, width_model), axis=1)
    return (summed + mixture).astype(jnp.bfloat16)[None]


AXES = ("ctx", "exp")


def spot(flat):
    ctx, exp = divmod(flat, 4)
    return ctx // 2, ctx % 2, exp // 2, exp % 2


def flat_of(z, x, y, core):
    return (z * 2 + x) * 4 + y * 2 + core


def move(array, rule):
    pairs = []
    for flat in range(32):
        there = rule(*spot(flat))
        if there is not None:
            pairs.append((flat, flat_of(*there)))
    return lax.ppermute(array, AXES, pairs)


def is_home(z, core):
    return core == z % 2


def to_twin(z, x, y, core):
    return z, x, y, 1 - core


def first_hop(z, x, y, core):
    return (z, x ^ 1, y, 1 - core) if is_home(z, core) else (z ^ 1, x, y, core)


def second_hop(z, x, y, core):
    return (z, x ^ 1, y, core) if is_home(z, core) else None


def home_to_twin(z, x, y, core):
    return (z, x, y, 1 - core) if is_home(z, core) else None


def slot_targets(ids_row, z_here, y_here, capacity):
    expert_count = 8
    token_count = ids_row.shape[1]
    lanes = lax.broadcasted_iota(jnp.int32, (expert_count, token_count), 0)
    onehot = (lanes == ids_row).astype(jnp.float32)
    before = (
        lax.broadcasted_iota(jnp.int32, (token_count, token_count), 0)
        < lax.broadcasted_iota(jnp.int32, (token_count, token_count), 1)
    ).astype(jnp.bfloat16)
    earlier = jnp.dot(onehot.astype(jnp.bfloat16), before, preferred_element_type=jnp.float32)
    slot = jnp.sum(earlier * onehot, axis=0, keepdims=True).astype(jnp.int32)
    owner = lax.shift_right_logical(ids_row, 1)
    z_there = (ids_row & 1) * 2 + (owner & 1)
    y_there = lax.shift_right_logical(owner, 1)
    relative = (z_there ^ z_here) * 2 + (y_there ^ y_here)
    return relative * capacity + slot


def slot_matrix(ids_row, z_here, y_here, capacity):
    target = slot_targets(ids_row, z_here, y_here, capacity)
    rows = lax.broadcasted_iota(jnp.int32, (8 * capacity, ids_row.shape[1]), 0)
    return (rows == target).astype(jnp.bfloat16)


def fetch_all(pairs, semaphores):
    copies = [
        pltpu.make_async_copy(source, target, semaphores.at[i])
        for i, (source, target) in enumerate(pairs)
    ]
    for copy in copies:
        copy.start()
    return copies


def attend_kernel(where_ref, ids_ref, queries_from, residual_from, *refs):
    kv_from, summed_to, out_refs = refs[:8], refs[8], refs[9:17]
    queries_ref, residual_ref, kv_ref, bias_ref, mixed_ref, summed_ref, semaphores = refs[17:]
    tokens = queries_ref.shape[0]
    group = HEADS // KV_HEADS
    ctx_here = where_ref[0]
    copies = fetch_all(
        [(queries_from, queries_ref), (residual_from, residual_ref)]
        + [(kv_from[k], kv_ref.at[pl.ds(k * tokens, tokens)]) for k in range(8)],
        semaphores,
    )
    row = lax.broadcasted_iota(jnp.int32, (tokens, tokens), 0)
    column = lax.broadcasted_iota(jnp.int32, (tokens, tokens), 1)
    for k in range(8):
        span = slice(k * tokens, (k + 1) * tokens)
        if k == 0:
            bias_ref[:, span] = jnp.where(column <= row, 0.0, negative_fill)
        else:
            bias_ref[:, span] = jnp.full(
                (tokens, tokens), jnp.where(ctx_here >= k, 0.0, negative_fill), jnp.float32
            )
    for copy in copies[2:] + copies[:1]:
        copy.wait()
    factor = math.log2(math.e) / math.sqrt(HD)
    heads_each = 2
    for first in range(0, HEADS, heads_each):
        kv_head = first // group
        key_side = slice(kv_head * HD, (kv_head + 1) * HD)
        value_side = slice((KV_HEADS + kv_head) * HD, (KV_HEADS + kv_head + 1) * HD)
        rows = jnp.concatenate(
            [queries_ref[:, h * HD : (h + 1) * HD] for h in range(first, first + heads_each)], axis=0
        )
        scores = contract_rows(rows, kv_ref[:, key_side])
        scores = scores + jnp.concatenate([bias_ref[...]] * heads_each, axis=0)
        largest = jnp.max(scores, axis=1, keepdims=True)
        exponent = jnp.exp2((scores - largest) * factor)
        total = jnp.sum(exponent, axis=1, keepdims=True)
        product = jnp.dot(
            exponent.astype(jnp.bfloat16), kv_ref[:, value_side], preferred_element_type=jnp.float32
        )
        result = product / total
        for j in range(heads_each):
            mixed_ref[:, (first + j) * HD : (first + j + 1) * HD] = result[
                j * tokens : (j + 1) * tokens
            ].astype(jnp.bfloat16)
    copies[1].wait()
    summed = residual_ref[...].astype(jnp.float32) + mixed_ref[...].astype(jnp.float32)
    summed_ref[...] = summed
    keep = pltpu.make_async_copy(summed_ref, summed_to, semaphores.at[10])
    keep.start()
    scale = lax.rsqrt(jnp.mean(summed * summed, axis=1, keepdims=True) + epsilon)
    normed = (summed * scale).astype(jnp.bfloat16)
    capacity = out_refs[0].shape[0]
    choose = slot_matrix(ids_ref[...], where_ref[1], where_ref[2], capacity)
    slots = jnp.dot(choose, normed, preferred_element_type=jnp.float32).astype(jnp.bfloat16)
    for k in range(8):
        out_refs[k][...] = slots[k * capacity : (k + 1) * capacity]
    keep.wait()


def load_pack(pack, place, strip, targets, semaphores):
    return [
        pltpu.make_async_copy(
            pack.at[pl.ds(kind * strip, strip)],
            targets[kind].at[pl.ds(place * strip, strip)],
            semaphores.at[place, kind],
        )
        for kind in range(3)
    ]


def active_of(rows, gate, up):
    gate_part = contract_rows(rows, gate)
    up_part = contract_rows(rows, up)
    silu = gate_part / (1.0 + jnp.exp(-gate_part))
    return (silu * up_part).astype(jnp.bfloat16)


def expert_kernel(places, where_ref, *refs):
    row_from, pack_from, rest = refs[:8], refs[8 : 9 + places], refs[9 + places :]
    continued = places == 1
    if continued:
        before_from, rest = rest[0], rest[1:]
        out_refs, rest = rest[:8], rest[8:]
    else:
        out_refs, rest = rest[:1], rest[1:]
    rows_ref, before_ref, gate_ref, up_ref, down_ref, row_semaphores, semaphores = rest
    at_home = where_ref[3] == 1
    away = jnp.logical_not(at_home)
    strip = pack_from[0].shape[0] // 3
    capacity = row_from[0].shape[0]
    targets = (gate_ref, up_ref, down_ref)
    loads = [(row_from[k], rows_ref.at[pl.ds(k * capacity, capacity)]) for k in range(8)]
    if continued:
        loads.append((before_from, before_ref))
    row_copies = fetch_all(loads, row_semaphores)

    @pl.when(at_home)
    def _():
        for copy in load_pack(pack_from[0], 0, strip, targets, semaphores):
            copy.start()

    @pl.when(away)
    def _():
        for copy in load_pack(pack_from[1], 0, strip, targets, semaphores):
            copy.start()

    waits = [load_pack(pack_from[0], 0, strip, targets, semaphores)]
    for place in range(1, places):
        waits.append(load_pack(pack_from[place + 1], place, strip, targets, semaphores))
        for copy in waits[place]:
            copy.start()
    for copy in row_copies:
        copy.wait()
    rows = rows_ref[...]
    actives = []
    for place in range(places):
        for copy in waits[place][:2]:
            copy.wait()
        span = slice(place * strip, (place + 1) * strip)
        actives.append(active_of(rows, gate_ref[span, :], up_ref[span, :]))
    for place in range(places):
        for copy in waits[place][2:]:
            copy.wait()
    active = actives[0] if continued else jnp.concatenate(actives, axis=1)
    result = jnp.dot(active, down_ref[...], preferred_element_type=jnp.float32)
    if continued:
        result = (result + before_ref[...]).astype(jnp.bfloat16)
        for k in range(8):
            out_refs[k][...] = result[k * capacity : (k + 1) * capacity]
    else:
        out_refs[0][...] = result


def combine_kernel(where_ref, ids_ref, route_ref, summed_from, *refs):
    row_from, out_ref, rows_ref, summed_ref, semaphores = refs[:8], *refs[8:]
    capacity = row_from[0].shape[0]
    copies = fetch_all(
        [(row_from[k], rows_ref.at[pl.ds(k * capacity, capacity)]) for k in range(8)]
        + [(summed_from, summed_ref)],
        semaphores,
    )
    choose = slot_matrix(ids_ref[...], where_ref[1], where_ref[2], capacity)
    for copy in copies:
        copy.wait()
    picked = lax.dot_general(
        choose, rows_ref[...], (((0,), (0,)), ((), ())), preferred_element_type=jnp.float32
    )
    out_ref[...] = (summed_ref[...] + picked * route_ref[...]).astype(jnp.bfloat16)


IN_VMEM = pl.BlockSpec(memory_space=pltpu.VMEM)
IN_SMEM = pl.BlockSpec(memory_space=pltpu.SMEM)
IN_HBM = pl.BlockSpec(memory_space=pltpu.HBM)


def shards_cube(
    residual,
    queries,
    key_states,
    value_states,
    expert_ids,
    route_weight,
    gate_weight,
    up_weight,
    down_weight,
):
    ctx_here = lax.axis_index("ctx")
    exp_here = lax.axis_index("exp")
    home = ((ctx_here // 2) % 2 == exp_here % 2).astype(jnp.int32)
    where = jnp.stack([ctx_here, ctx_here // 2, exp_here // 2, home]).astype(jnp.int32)
    tokens, width = residual.shape[1:]
    piece = gate_weight.shape[2]
    capacity = max(2, 2 * tokens * TOPK // 8)
    ids_row = expert_ids[0].reshape(1, tokens)
    kv_own = jnp.concatenate([key_states[0], value_states[0]], axis=1)
    kv_blocks = {0: kv_own}

    def send_keys(block, k):
        def later(z, x, y, core):
            ctx = 2 * z + x + k
            return (ctx // 2, ctx % 2, y, core) if ctx < 8 else None

        kv_blocks[k] = move(block, later)

    own = jnp.concatenate([gate_weight[0, 0], up_weight[0, 0], down_weight[0, 0]], axis=0)
    send_keys(kv_own, 7)
    own, kv_blocks[7], kv_next = lax.optimization_barrier((own, kv_blocks[7], kv_own))
    one = move(own, first_hop)
    for k in (4, 6, 5, 3, 2, 1):
        send_keys(kv_next, k)
    kv_list = [kv_blocks[k] for k in range(1, 8)]
    one, own, *kv_list = lax.optimization_barrier((one, own, *kv_list))
    last = move(one, second_hop)
    own_twin = move(own, home_to_twin)
    one_twin = move(one, to_twin)
    slot_shape = jax.ShapeDtypeStruct((capacity, width), jnp.bfloat16)
    keys_all = 8 * tokens
    rows_all = 8 * capacity
    first_out = pl.pallas_call(
        attend_kernel,
        out_shape=[jax.ShapeDtypeStruct((tokens, width), jnp.float32)] + [slot_shape] * 8,
        in_specs=[IN_SMEM, IN_VMEM] + [IN_HBM] * 10,
        out_specs=[IN_HBM] + [IN_VMEM] * 8,
        scratch_shapes=[
            pltpu.VMEM((tokens, width), jnp.bfloat16),
            pltpu.VMEM((tokens, width), jnp.bfloat16),
            pltpu.VMEM((keys_all, 2 * KV_HEADS * HD), jnp.bfloat16),
            pltpu.VMEM((tokens, keys_all), jnp.float32),
            pltpu.VMEM((tokens, width), jnp.bfloat16),
            pltpu.VMEM((tokens, width), jnp.float32),
            pltpu.SemaphoreType.DMA((11,)),
        ],
        compiler_params=pltpu.CompilerParams(vmem_limit_bytes=58 << 20),
        cost_estimate=pl.CostEstimate(
            flops=4 * tokens * keys_all * HEADS * HD,
            bytes_accessed=8 * tokens * width,
            transcendentals=tokens * keys_all * HEADS,
        ),
        name="attend",
    )(where, ids_row, queries[0], residual[0], kv_own, *kv_list)
    summed, outgoing = first_out[0], list(first_out[1:])

    def swap(array, k):
        if k == 0:
            return array
        return move(array, lambda z, x, y, core: (z ^ (k >> 1), x, y ^ (k & 1), core))

    own_twin, one_twin, *outgoing = lax.optimization_barrier((own_twin, one_twin, *outgoing))
    arrived = [outgoing[0]] + [swap(outgoing[k], k) for k in range(1, 8)]
    def run_expert(places, rows, packs, before):
        total = jax.ShapeDtypeStruct((rows_all, width), jnp.float32)
        inner = places * piece
        return pl.pallas_call(
            partial(expert_kernel, places),
            out_shape=[slot_shape] * 8 if before else [total],
            in_specs=[IN_SMEM] + [IN_HBM] * (8 + len(packs) + len(before)),
            out_specs=[IN_VMEM] * (8 if before else 1),
            scratch_shapes=[
                pltpu.VMEM((rows_all, width), jnp.bfloat16),
                pltpu.VMEM((rows_all if before else 8, width), jnp.float32),
                pltpu.VMEM((inner, width), jnp.bfloat16),
                pltpu.VMEM((inner, width), jnp.bfloat16),
                pltpu.VMEM((inner, width), jnp.bfloat16),
                pltpu.SemaphoreType.DMA((9,)),
                pltpu.SemaphoreType.DMA((places, 3)),
            ],
            compiler_params=pltpu.CompilerParams(vmem_limit_bytes=24 << 20),
            cost_estimate=pl.CostEstimate(
                flops=6 * rows_all * inner * width,
                bytes_accessed=6 * inner * width,
                transcendentals=rows_all * inner,
            ),
            name="experts_%d" % places,
        )(where, *rows, *packs, *before)

    most = run_expert(3, arrived, [own, own_twin, one, one_twin], [])
    last, *most = lax.optimization_barrier((last, *most))
    last_twin = move(last, home_to_twin)
    results = run_expert(1, arrived, [last, last_twin], most)
    returned = [swap(results[k], k) for k in range(8)]
    output = pl.pallas_call(
        combine_kernel,
        out_shape=jax.ShapeDtypeStruct((tokens, width), jnp.bfloat16),
        in_specs=[IN_SMEM, IN_VMEM, IN_VMEM] + [IN_HBM] * 9,
        out_specs=IN_VMEM,
        scratch_shapes=[
            pltpu.VMEM((rows_all, width), jnp.bfloat16),
            pltpu.VMEM((tokens, width), jnp.float32),
            pltpu.SemaphoreType.DMA((9,)),
        ],
        compiler_params=pltpu.CompilerParams(vmem_limit_bytes=12 << 20),
        cost_estimate=pl.CostEstimate(
            flops=2 * tokens * 8 * capacity * width,
            bytes_accessed=12 * tokens * width,
            transcendentals=0,
        ),
        name="combine",
    )(where, ids_row, route_weight[0], summed, *returned)
    return output[None]


def solution(mesh):
    in_specs = (
        P("exp", "ctx", None),
        P("exp", "ctx", None),
        P("exp", "ctx", None),
        P("exp", "ctx", None),
        P("exp", "ctx", None),
        P("exp", "ctx", None),
        P("exp", "ctx", None, None),
        P("exp", "ctx", None, None),
        P("exp", "ctx", None, None),
    )
    out_specs = P("exp", "ctx", None)
    cube = mesh.shape["ctx"] == 8 and mesh.shape["exp"] == 4
    body = shards_cube if cube else shards
    return jax.shard_map(body, mesh=mesh, in_specs=in_specs, out_specs=out_specs, check_vma=False)
```

```python
from functools import partial
import math

import jax
import jax.numpy as jnp
from jax import lax
from jax.experimental import pallas as pl
from jax.experimental.pallas import tpu as pltpu
from jax.sharding import PartitionSpec as P

HD = 128
HEADS = 16
KV_HEADS = 2
PIECES = 4
TOPK = 1


negative_fill = -1e30
epsilon = 1e-06


def contract_rows(left_rows, weight_rows):
    return lax.dot_general(
        left_rows, weight_rows, (((1,), (1,)), ((), ())), preferred_element_type=jnp.float32
    )


def to_groups(half_block, heads_kv, group_size, head_dim):
    token_count = half_block.shape[0]
    shaped = half_block.reshape(token_count, heads_kv, group_size, head_dim)
    return jnp.transpose(shaped, (1, 0, 2, 3)).reshape(heads_kv, token_count * group_size, head_dim)


def keep_current(current):
    return current


def block_update(current, query_rows, query_pos, key_block, value_block, key_start, score_scale):
    running_max, running_total, accumulated = current
    scores = (
        jnp.einsum("gqd,kgd->gqk", query_rows, key_block, preferred_element_type=jnp.float32)
        * score_scale
    )
    key_pos = key_start + jnp.arange(key_block.shape[0], dtype=jnp.int32)
    allowed = key_pos[None, None, :] <= query_pos[None, :, None]
    scores = jnp.where(allowed, scores, negative_fill)
    new_max = jnp.maximum(running_max, jnp.max(scores, axis=-1))
    rescale = jnp.exp(running_max - new_max)
    exponent = jnp.where(allowed, jnp.exp(scores - new_max[..., None]), 0.0)
    new_total = running_total * rescale + jnp.sum(exponent, axis=-1)
    product = jnp.einsum(
        "gqk,kgd->gqd",
        exponent.astype(jnp.bfloat16),
        value_block,
        preferred_element_type=jnp.float32,
    )
    return (new_max, new_total, accumulated * rescale[..., None] + product)


def make_folder(query_sets, position_sets, last_positions, heads_kv, head_dim, score_scale):

    def fold_keys(running, key_piece, first_key):
        key_part, value_part = key_piece
        key_count = key_part.shape[1]
        key_width = math.gcd(key_count, 512)
        key_rows = key_part.reshape(key_count, heads_kv, head_dim)
        value_rows = value_part.reshape(key_count, heads_kv, head_dim)

        def one_block(block_index, current_sets):
            offset = block_index * key_width
            key_block = lax.dynamic_slice_in_dim(key_rows, offset, key_width, 0)
            value_block = lax.dynamic_slice_in_dim(value_rows, offset, key_width, 0)
            updated = []
            for current, query_rows, query_pos, last_pos in zip(
                current_sets, query_sets, position_sets, last_positions
            ):
                step_fn = partial(
                    block_update,
                    query_rows=query_rows,
                    query_pos=query_pos,
                    key_block=key_block,
                    value_block=value_block,
                    key_start=offset,
                    score_scale=score_scale,
                )
                updated.append(lax.cond(offset <= last_pos, step_fn, keep_current, current))
            return tuple(updated)

        return lax.fori_loop(0, key_count // key_width, one_block, running)

    return fold_keys


def finish(current, token_count, heads_kv, group_size, head_dim):
    running_max, running_total, accumulated = current
    result = accumulated / running_total[..., None]
    shaped = result.reshape(heads_kv, token_count, group_size, head_dim)
    return (
        jnp.transpose(shaped, (1, 0, 2, 3))
        .reshape(token_count, heads_kv * group_size * head_dim)
        .astype(jnp.bfloat16)
    )


def shards(
    residual,
    queries,
    key_states,
    value_states,
    expert_ids,
    route_weight,
    gate_weight,
    up_weight,
    down_weight,
):
    ctx_count = lax.axis_size("ctx")
    exp_count = lax.axis_size("exp")
    ctx_rank = lax.axis_index("ctx")
    tok_rows = residual.shape[1]
    half_rows = tok_rows // 2
    group_size = HEADS // KV_HEADS
    score_scale = 1.0 / math.sqrt(HD)
    local_queries = queries[0]
    first_half = local_queries[:half_rows]
    second_half = local_queries[half_rows:]
    first_start = ctx_rank * tok_rows
    second_start = first_start + half_rows
    offsets = jnp.repeat(jnp.arange(half_rows, dtype=jnp.int32), group_size)
    query_sets = (
        to_groups(first_half, KV_HEADS, group_size, HD),
        to_groups(second_half, KV_HEADS, group_size, HD),
    )
    position_sets = (first_start + offsets, second_start + offsets)
    last_positions = (first_start + half_rows - 1, second_start + half_rows - 1)
    row_total = half_rows * group_size
    empty_state = (
        jnp.full((KV_HEADS, row_total), negative_fill, jnp.float32),
        jnp.zeros((KV_HEADS, row_total), jnp.float32),
        jnp.zeros((KV_HEADS, row_total, HD), jnp.float32),
    )
    folder = make_folder(query_sets, position_sets, last_positions, KV_HEADS, HD, score_scale)
    final_sets = folder(
        (empty_state, empty_state),
        (
            lax.all_gather(key_states, "ctx", axis=1, tiled=True),
            lax.all_gather(value_states, "ctx", axis=1, tiled=True),
        ),
        jnp.int32(0),
    )
    first_out = finish(final_sets[0], half_rows, KV_HEADS, group_size, HD)
    second_out = finish(final_sets[1], half_rows, KV_HEADS, group_size, HD)
    attention = jnp.concatenate([first_out, second_out], axis=0)
    summed = residual[0].astype(jnp.float32) + lax.optimization_barrier(attention).astype(
        jnp.float32
    )
    normed = (
        summed * lax.rsqrt(jnp.mean(summed * summed, axis=-1, keepdims=True) + epsilon)
    ).astype(jnp.bfloat16)
    width_model = normed.shape[1]
    experts_each = ctx_count // PIECES
    expert_total = experts_each * exp_count
    pair_count = tok_rows * TOPK
    capacity = max(2, 2 * tok_rows * TOPK // expert_total)
    flat_ids = expert_ids[0].reshape(pair_count)
    onehot = (flat_ids[:, None] == jnp.arange(expert_total, dtype=jnp.int32)[None, :]).astype(
        jnp.int32
    )
    earlier = jnp.cumsum(onehot, axis=0) - onehot
    slot_index = jnp.sum(earlier * onehot, axis=1)
    owner_index = flat_ids // experts_each
    local_expert = flat_ids % experts_each
    target = (local_expert * exp_count + owner_index) * capacity + slot_index
    pair_token = jnp.arange(pair_count, dtype=jnp.int32) // TOPK
    slot_total = expert_total * capacity
    slot_table = jnp.full((slot_total,), tok_rows, jnp.int32).at[target].set(pair_token)
    padded = jnp.concatenate([normed, jnp.zeros((1, width_model), jnp.bfloat16)], axis=0)
    outgoing = padded[slot_table].reshape(experts_each, exp_count, capacity, width_model)
    arrived = lax.all_to_all(outgoing, "exp", split_axis=1, concat_axis=1, tiled=True)
    copies = jnp.broadcast_to(
        arrived[:, None], (experts_each, PIECES, exp_count, capacity, width_model)
    ).reshape(ctx_count, exp_count * capacity, width_model)
    gate_piece = gate_weight[0, 0]
    up_piece = up_weight[0, 0]
    down_piece = down_weight[0, 0]
    received = lax.all_to_all(copies, "ctx", split_axis=0, concat_axis=0, tiled=True)
    sources = received.shape[0]
    item_count = received.shape[1]
    flat_rows = received.reshape(sources * item_count, width_model)
    gate_part = contract_rows(flat_rows, gate_piece)
    up_part = contract_rows(flat_rows, up_piece)
    active = (jax.nn.silu(gate_part) * up_part).astype(jnp.bfloat16)
    partial_out = jnp.dot(active, down_piece, preferred_element_type=jnp.float32).astype(
        jnp.bfloat16
    )
    returned = lax.all_to_all(
        partial_out.reshape(sources, item_count, width_model),
        "ctx",
        split_axis=0,
        concat_axis=0,
        tiled=True,
    )
    piece_sum = jnp.sum(
        returned.reshape(experts_each, PIECES, exp_count, capacity, width_model).astype(
            jnp.float32
        ),
        axis=1,
    ).astype(jnp.bfloat16)
    arrived_back = lax.all_to_all(piece_sum, "exp", split_axis=1, concat_axis=1, tiled=True)
    gathered = arrived_back.reshape(slot_total, width_model)[target].astype(jnp.float32)
    weighted = gathered * route_weight[0]
    mixture = jnp.sum(weighted.reshape(tok_rows, TOPK, width_model), axis=1)
    return (summed + mixture).astype(jnp.bfloat16)[None]


AXES = ("ctx", "exp")


def spot(flat):
    ctx, exp = divmod(flat, 4)
    return ctx // 2, ctx % 2, exp // 2, exp % 2


def flat_of(z, x, y, core):
    return (z * 2 + x) * 4 + y * 2 + core


def move(array, rule):
    pairs = []
    for flat in range(32):
        there = rule(*spot(flat))
        if there is not None:
            pairs.append((flat, flat_of(*there)))
    return lax.ppermute(array, AXES, pairs)


def is_home(z, core):
    return core == z % 2


def to_twin(z, x, y, core):
    return z, x, y, 1 - core


def first_hop(z, x, y, core):
    return (z, x ^ 1, y, 1 - core) if is_home(z, core) else (z ^ 1, x, y, core)


def second_hop(z, x, y, core):
    return (z, x ^ 1, y, 1 - core) if is_home(z, core) else None


def pack_half(half, *weights):
    rows = weights[0].shape[0] // 2
    return jnp.concatenate([w[half * rows : (half + 1) * rows] for w in weights], axis=0)


def slot_targets(ids_row, z_here, y_here, capacity):
    expert_count = 8
    token_count = ids_row.shape[1]
    lanes = lax.broadcasted_iota(jnp.int32, (expert_count, token_count), 0)
    onehot = (lanes == ids_row).astype(jnp.float32)
    before = (
        lax.broadcasted_iota(jnp.int32, (token_count, token_count), 0)
        < lax.broadcasted_iota(jnp.int32, (token_count, token_count), 1)
    ).astype(jnp.bfloat16)
    earlier = jnp.dot(onehot.astype(jnp.bfloat16), before, preferred_element_type=jnp.float32)
    slot = jnp.sum(earlier * onehot, axis=0, keepdims=True).astype(jnp.int32)
    owner = lax.shift_right_logical(ids_row, 1)
    z_there = (ids_row & 1) * 2 + (owner & 1)
    y_there = lax.shift_right_logical(owner, 1)
    relative = (z_there ^ z_here) * 2 + (y_there ^ y_here)
    return relative * capacity + slot


def slot_matrix(ids_row, z_here, y_here, capacity):
    target = slot_targets(ids_row, z_here, y_here, capacity)
    rows = lax.broadcasted_iota(jnp.int32, (8 * capacity, ids_row.shape[1]), 0)
    return (rows == target).astype(jnp.bfloat16)


def fetch_all(pairs, semaphores):
    copies = [
        pltpu.make_async_copy(source, target, semaphores.at[i])
        for i, (source, target) in enumerate(pairs)
    ]
    for copy in copies:
        copy.start()
    return copies


def attend_kernel(where_ref, ids_ref, queries_from, residual_from, *refs):
    kv_from, summed_to, out_refs = refs[:8], refs[8], refs[9:17]
    queries_ref, residual_ref, kv_ref, bias_ref, mixed_ref, summed_ref, semaphores = refs[17:]
    tokens = queries_ref.shape[0]
    group = HEADS // KV_HEADS
    ctx_here = where_ref[0]
    copies = fetch_all(
        [(queries_from, queries_ref), (residual_from, residual_ref)]
        + [(kv_from[k], kv_ref.at[pl.ds(k * tokens, tokens)]) for k in range(8)],
        semaphores,
    )
    row = lax.broadcasted_iota(jnp.int32, (tokens, tokens), 0)
    column = lax.broadcasted_iota(jnp.int32, (tokens, tokens), 1)
    for k in range(8):
        span = slice(k * tokens, (k + 1) * tokens)
        if k == 0:
            bias_ref[:, span] = jnp.where(column <= row, 0.0, negative_fill)
        else:
            bias_ref[:, span] = jnp.full(
                (tokens, tokens), jnp.where(ctx_here >= k, 0.0, negative_fill), jnp.float32
            )
    for copy in copies[2:] + copies[:1]:
        copy.wait()
    factor = math.log2(math.e) / math.sqrt(HD)
    heads_each = 2
    for first in range(0, HEADS, heads_each):
        kv_head = first // group
        key_side = slice(kv_head * HD, (kv_head + 1) * HD)
        value_side = slice((KV_HEADS + kv_head) * HD, (KV_HEADS + kv_head + 1) * HD)
        rows = jnp.concatenate(
            [queries_ref[:, h * HD : (h + 1) * HD] for h in range(first, first + heads_each)], axis=0
        )
        scores = contract_rows(rows, kv_ref[:, key_side])
        scores = scores + jnp.concatenate([bias_ref[...]] * heads_each, axis=0)
        largest = jnp.max(scores, axis=1, keepdims=True)
        exponent = jnp.exp2((scores - largest) * factor)
        total = jnp.sum(exponent, axis=1, keepdims=True)
        product = jnp.dot(
            exponent.astype(jnp.bfloat16), kv_ref[:, value_side], preferred_element_type=jnp.float32
        )
        result = product / total
        for j in range(heads_each):
            mixed_ref[:, (first + j) * HD : (first + j + 1) * HD] = result[
                j * tokens : (j + 1) * tokens
            ].astype(jnp.bfloat16)
    copies[1].wait()
    summed = residual_ref[...].astype(jnp.float32) + mixed_ref[...].astype(jnp.float32)
    summed_ref[...] = summed
    keep = pltpu.make_async_copy(summed_ref, summed_to, semaphores.at[10])
    keep.start()
    scale = lax.rsqrt(jnp.mean(summed * summed, axis=1, keepdims=True) + epsilon)
    normed = (summed * scale).astype(jnp.bfloat16)
    capacity = out_refs[0].shape[0]
    choose = slot_matrix(ids_ref[...], where_ref[1], where_ref[2], capacity)
    slots = jnp.dot(choose, normed, preferred_element_type=jnp.float32).astype(jnp.bfloat16)
    for k in range(8):
        out_refs[k][...] = slots[k * capacity : (k + 1) * capacity]
    keep.wait()


def load_pack(pair, strip, targets, semaphores):
    return [
        pltpu.make_async_copy(
            pair[half].at[pl.ds(kind * strip, strip)],
            targets[kind].at[pl.ds(half * strip, strip)],
            semaphores.at[kind, half],
        )
        for kind in range(3)
        for half in range(2)
    ]


def active_of(rows, gate, up):
    gate_part = contract_rows(rows, gate)
    up_part = contract_rows(rows, up)
    silu = gate_part / (1.0 + jnp.exp(-gate_part))
    return (silu * up_part).astype(jnp.bfloat16)


def expert_kernel(row_count, where_ref, *refs):
    row_from, refs = refs[:row_count], refs[row_count:]
    first_piece = len(refs) == 10
    if first_piece:
        pairs, (total_ref,), rest = [refs[:2]], refs[2:3], refs[3:]
    else:
        pairs, before_from, (mine_ref, twins_ref), rest = (
            [refs[:2], refs[2:4]],
            refs[4],
            refs[5:7],
            refs[7:],
        )
    rows_ref, before_ref, gate_ref, up_ref, down_ref, row_semaphores, semaphores = rest
    strip = pairs[0][0].shape[0] // 3
    targets = (gate_ref, up_ref, down_ref)
    loads = []
    place = 0
    for ref in row_from:
        loads.append((ref, rows_ref.at[pl.ds(place, ref.shape[0])]))
        place += ref.shape[0]
    if not first_piece:
        loads.append((before_from, before_ref))
    row_copies = fetch_all(loads, row_semaphores)
    weight_copies = load_pack(pairs[0], strip, targets, semaphores)
    if first_piece:
        for copy in weight_copies:
            copy.start()
    else:
        at_home = where_ref[3] == 1

        @pl.when(at_home)
        def _():
            for copy in load_pack(pairs[0], strip, targets, semaphores):
                copy.start()

        @pl.when(jnp.logical_not(at_home))
        def _():
            for copy in load_pack(pairs[1], strip, targets, semaphores):
                copy.start()

    for copy in row_copies + weight_copies[:4]:
        copy.wait()
    active = active_of(rows_ref[...], gate_ref[...], up_ref[...])
    for copy in weight_copies[4:]:
        copy.wait()
    result = jnp.dot(active, down_ref[...], preferred_element_type=jnp.float32)
    if first_piece:
        total_ref[...] = result
    else:
        result = result + before_ref[...]
        half = result.shape[0] // 2
        mine_ref[...] = result[:half]
        twins_ref[...] = result[half:].astype(jnp.bfloat16)


def join_kernel(mine_from, other_from, *refs):
    out_refs, (mine_ref, other_ref, semaphores) = refs[:8], refs[8:]
    capacity = out_refs[0].shape[0]
    for copy in fetch_all([(mine_from, mine_ref), (other_from, other_ref)], semaphores):
        copy.wait()
    result = (mine_ref[...] + other_ref[...].astype(jnp.float32)).astype(jnp.bfloat16)
    for k in range(8):
        out_refs[k][...] = result[k * capacity : (k + 1) * capacity]


def combine_kernel(where_ref, ids_ref, route_ref, summed_from, *refs):
    row_from, out_ref, rows_ref, summed_ref, semaphores = refs[:8], *refs[8:]
    capacity = row_from[0].shape[0]
    copies = fetch_all(
        [(row_from[k], rows_ref.at[pl.ds(k * capacity, capacity)]) for k in range(8)]
        + [(summed_from, summed_ref)],
        semaphores,
    )
    choose = slot_matrix(ids_ref[...], where_ref[1], where_ref[2], capacity)
    for copy in copies:
        copy.wait()
    picked = lax.dot_general(
        choose, rows_ref[...], (((0,), (0,)), ((), ())), preferred_element_type=jnp.float32
    )
    out_ref[...] = (summed_ref[...] + picked * route_ref[...]).astype(jnp.bfloat16)


IN_VMEM = pl.BlockSpec(memory_space=pltpu.VMEM)
IN_SMEM = pl.BlockSpec(memory_space=pltpu.SMEM)
IN_HBM = pl.BlockSpec(memory_space=pltpu.HBM)


def shards_cube(
    residual,
    queries,
    key_states,
    value_states,
    expert_ids,
    route_weight,
    gate_weight,
    up_weight,
    down_weight,
):
    ctx_here = lax.axis_index("ctx")
    exp_here = lax.axis_index("exp")
    home = ((ctx_here // 2) % 2 == exp_here % 2).astype(jnp.int32)
    where = jnp.stack([ctx_here, ctx_here // 2, exp_here // 2, home]).astype(jnp.int32)
    tokens, width = residual.shape[1:]
    piece = gate_weight.shape[2]
    capacity = max(2, 2 * tokens * TOPK // 8)
    ids_row = expert_ids[0].reshape(1, tokens)
    kv_own = jnp.concatenate([key_states[0], value_states[0]], axis=1)
    kv_blocks = {0: kv_own}

    def send_keys(block, k):
        def later(z, x, y, core):
            ctx = 2 * z + x + k
            return (ctx // 2, ctx % 2, y, core) if ctx < 8 else None

        kv_blocks[k] = move(block, later)

    own = [pack_half(half, gate_weight[0, 0], up_weight[0, 0], down_weight[0, 0]) for half in range(2)]
    one_first = move(own[0], first_hop)
    for k in (4, 5, 3, 2, 6, 1, 7):
        send_keys(kv_own, k)
    kv_list = [kv_blocks[k] for k in range(1, 8)]
    one_first, own[0], own[1], *kv_list = lax.optimization_barrier((one_first, *own, *kv_list))
    one_second = move(own[1], first_hop)
    last_first = move(one_first, second_hop)
    slot_shape = jax.ShapeDtypeStruct((capacity, width), jnp.bfloat16)
    keys_all = 8 * tokens
    rows_all = 8 * capacity
    first_out = pl.pallas_call(
        attend_kernel,
        out_shape=[jax.ShapeDtypeStruct((tokens, width), jnp.float32)] + [slot_shape] * 8,
        in_specs=[IN_SMEM, IN_VMEM] + [IN_HBM] * 10,
        out_specs=[IN_HBM] + [IN_VMEM] * 8,
        scratch_shapes=[
            pltpu.VMEM((tokens, width), jnp.bfloat16),
            pltpu.VMEM((tokens, width), jnp.bfloat16),
            pltpu.VMEM((keys_all, 2 * KV_HEADS * HD), jnp.bfloat16),
            pltpu.VMEM((tokens, keys_all), jnp.float32),
            pltpu.VMEM((tokens, width), jnp.bfloat16),
            pltpu.VMEM((tokens, width), jnp.float32),
            pltpu.SemaphoreType.DMA((11,)),
        ],
        compiler_params=pltpu.CompilerParams(vmem_limit_bytes=58 << 20),
        cost_estimate=pl.CostEstimate(
            flops=4 * tokens * keys_all * HEADS * HD,
            bytes_accessed=8 * tokens * width,
            transcendentals=tokens * keys_all * HEADS,
        ),
        name="attend",
    )(where, ids_row, queries[0], residual[0], kv_own, *kv_list)
    summed, outgoing = first_out[0], list(first_out[1:])

    def swap(array, k):
        if k == 0:
            return array
        return move(array, lambda z, x, y, core: (z ^ (k >> 1), x, y ^ (k & 1), core))

    early, late = (4, 6, 2), (5, 7, 3, 1)
    arrived = [swap(outgoing[k], k) if k in early else outgoing[k] for k in range(8)]
    one_second, *held = lax.optimization_barrier((one_second, *[arrived[k] for k in late]))
    for k, array in zip(late, held):
        arrived[k] = swap(array, k)
    last_second = move(one_second, second_hop)
    order = (0, *early, *late)
    row_parts = [jnp.concatenate([arrived[k] for k in group]) for group in (order[:4], order[4:])]
    row_parts += [move(part, to_twin) for part in row_parts]
    half_rows = row_parts[0].shape[0]

    def run_expert(packs, before):
        row_total = 2 * rows_all
        mine = jax.ShapeDtypeStruct((rows_all, width), jnp.float32)
        twins = jax.ShapeDtypeStruct((rows_all, width), jnp.bfloat16)
        total = jax.ShapeDtypeStruct((row_total, width), jnp.float32)
        return pl.pallas_call(
            partial(expert_kernel, len(row_parts)),
            out_shape=[mine, twins] if before else [total],
            in_specs=[IN_SMEM] + [IN_HBM] * (len(row_parts) + len(packs) + len(before)),
            out_specs=[IN_VMEM] * (2 if before else 1),
            scratch_shapes=[
                pltpu.VMEM((row_total, width), jnp.bfloat16),
                pltpu.VMEM((row_total if before else 8, width), jnp.float32),
                pltpu.VMEM((piece, width), jnp.bfloat16),
                pltpu.VMEM((piece, width), jnp.bfloat16),
                pltpu.VMEM((piece, width), jnp.bfloat16),
                pltpu.SemaphoreType.DMA((5,)),
                pltpu.SemaphoreType.DMA((3, 2)),
            ],
            compiler_params=pltpu.CompilerParams(vmem_limit_bytes=32 << 20),
            cost_estimate=pl.CostEstimate(
                flops=6 * row_total * piece * width,
                bytes_accessed=6 * piece * width,
                transcendentals=row_total * piece,
            ),
            name="experts_rest" if before else "experts_first",
        )(where, *row_parts, *packs, *before)

    first_total = run_expert([one_first, one_second], [])
    last_first, last_second, *first_total = lax.optimization_barrier(
        (last_first, last_second, *first_total)
    )
    mine, twins = run_expert([*own, last_first, last_second], first_total)
    joined = pl.pallas_call(
        join_kernel,
        out_shape=[slot_shape] * 8,
        in_specs=[IN_HBM] * 2,
        out_specs=[IN_VMEM] * 8,
        scratch_shapes=[
            pltpu.VMEM((rows_all, width), jnp.float32),
            pltpu.VMEM((rows_all, width), jnp.bfloat16),
            pltpu.SemaphoreType.DMA((2,)),
        ],
        compiler_params=pltpu.CompilerParams(vmem_limit_bytes=16 << 20),
        cost_estimate=pl.CostEstimate(
            flops=rows_all * width, bytes_accessed=8 * rows_all * width, transcendentals=0
        ),
        name="join",
    )(mine, move(twins, to_twin))
    results = [joined[order.index(k)] for k in range(8)]
    returned = [swap(results[k], k) for k in range(8)]
    output = pl.pallas_call(
        combine_kernel,
        out_shape=jax.ShapeDtypeStruct((tokens, width), jnp.bfloat16),
        in_specs=[IN_SMEM, IN_VMEM, IN_VMEM] + [IN_HBM] * 9,
        out_specs=IN_VMEM,
        scratch_shapes=[
            pltpu.VMEM((rows_all, width), jnp.bfloat16),
            pltpu.VMEM((tokens, width), jnp.float32),
            pltpu.SemaphoreType.DMA((9,)),
        ],
        compiler_params=pltpu.CompilerParams(vmem_limit_bytes=12 << 20),
        cost_estimate=pl.CostEstimate(
            flops=2 * tokens * 8 * capacity * width,
            bytes_accessed=12 * tokens * width,
            transcendentals=0,
        ),
        name="combine",
    )(where, ids_row, route_weight[0], summed, *returned)
    return output[None]


def solution(mesh):
    in_specs = (
        P("exp", "ctx", None),
        P("exp", "ctx", None),
        P("exp", "ctx", None),
        P("exp", "ctx", None),
        P("exp", "ctx", None),
        P("exp", "ctx", None),
        P("exp", "ctx", None, None),
        P("exp", "ctx", None, None),
        P("exp", "ctx", None, None),
    )
    out_specs = P("exp", "ctx", None)
    cube = mesh.shape["ctx"] == 8 and mesh.shape["exp"] == 4
    body = shards_cube if cube else shards
    return jax.shard_map(body, mesh=mesh, in_specs=in_specs, out_specs=out_specs, check_vma=False)
```

```python
from functools import partial
import math

import jax
import jax.numpy as jnp
from jax import lax
from jax.experimental import pallas as pl
from jax.experimental.pallas import tpu as pltpu
from jax.sharding import PartitionSpec as P

HD = 128
HEADS = 16
KV_HEADS = 2
PIECES = 4
TOPK = 1


negative_fill = -1e30
epsilon = 1e-06


def contract_rows(left_rows, weight_rows):
    return lax.dot_general(
        left_rows, weight_rows, (((1,), (1,)), ((), ())), preferred_element_type=jnp.float32
    )


def to_groups(half_block, heads_kv, group_size, head_dim):
    token_count = half_block.shape[0]
    shaped = half_block.reshape(token_count, heads_kv, group_size, head_dim)
    return jnp.transpose(shaped, (1, 0, 2, 3)).reshape(heads_kv, token_count * group_size, head_dim)


def keep_current(current):
    return current


def block_update(current, query_rows, query_pos, key_block, value_block, key_start, score_scale):
    running_max, running_total, accumulated = current
    scores = (
        jnp.einsum("gqd,kgd->gqk", query_rows, key_block, preferred_element_type=jnp.float32)
        * score_scale
    )
    key_pos = key_start + jnp.arange(key_block.shape[0], dtype=jnp.int32)
    allowed = key_pos[None, None, :] <= query_pos[None, :, None]
    scores = jnp.where(allowed, scores, negative_fill)
    new_max = jnp.maximum(running_max, jnp.max(scores, axis=-1))
    rescale = jnp.exp(running_max - new_max)
    exponent = jnp.where(allowed, jnp.exp(scores - new_max[..., None]), 0.0)
    new_total = running_total * rescale + jnp.sum(exponent, axis=-1)
    product = jnp.einsum(
        "gqk,kgd->gqd",
        exponent.astype(jnp.bfloat16),
        value_block,
        preferred_element_type=jnp.float32,
    )
    return (new_max, new_total, accumulated * rescale[..., None] + product)


def make_folder(query_sets, position_sets, last_positions, heads_kv, head_dim, score_scale):

    def fold_keys(running, key_piece, first_key):
        key_part, value_part = key_piece
        key_count = key_part.shape[1]
        key_width = math.gcd(key_count, 512)
        key_rows = key_part.reshape(key_count, heads_kv, head_dim)
        value_rows = value_part.reshape(key_count, heads_kv, head_dim)

        def one_block(block_index, current_sets):
            offset = block_index * key_width
            key_block = lax.dynamic_slice_in_dim(key_rows, offset, key_width, 0)
            value_block = lax.dynamic_slice_in_dim(value_rows, offset, key_width, 0)
            updated = []
            for current, query_rows, query_pos, last_pos in zip(
                current_sets, query_sets, position_sets, last_positions
            ):
                step_fn = partial(
                    block_update,
                    query_rows=query_rows,
                    query_pos=query_pos,
                    key_block=key_block,
                    value_block=value_block,
                    key_start=offset,
                    score_scale=score_scale,
                )
                updated.append(lax.cond(offset <= last_pos, step_fn, keep_current, current))
            return tuple(updated)

        return lax.fori_loop(0, key_count // key_width, one_block, running)

    return fold_keys


def finish(current, token_count, heads_kv, group_size, head_dim):
    running_max, running_total, accumulated = current
    result = accumulated / running_total[..., None]
    shaped = result.reshape(heads_kv, token_count, group_size, head_dim)
    return (
        jnp.transpose(shaped, (1, 0, 2, 3))
        .reshape(token_count, heads_kv * group_size * head_dim)
        .astype(jnp.bfloat16)
    )


def shards(
    residual,
    queries,
    key_states,
    value_states,
    expert_ids,
    route_weight,
    gate_weight,
    up_weight,
    down_weight,
):
    ctx_count = lax.axis_size("ctx")
    exp_count = lax.axis_size("exp")
    ctx_rank = lax.axis_index("ctx")
    tok_rows = residual.shape[1]
    half_rows = tok_rows // 2
    group_size = HEADS // KV_HEADS
    score_scale = 1.0 / math.sqrt(HD)
    local_queries = queries[0]
    first_half = local_queries[:half_rows]
    second_half = local_queries[half_rows:]
    first_start = ctx_rank * tok_rows
    second_start = first_start + half_rows
    offsets = jnp.repeat(jnp.arange(half_rows, dtype=jnp.int32), group_size)
    query_sets = (
        to_groups(first_half, KV_HEADS, group_size, HD),
        to_groups(second_half, KV_HEADS, group_size, HD),
    )
    position_sets = (first_start + offsets, second_start + offsets)
    last_positions = (first_start + half_rows - 1, second_start + half_rows - 1)
    row_total = half_rows * group_size
    empty_state = (
        jnp.full((KV_HEADS, row_total), negative_fill, jnp.float32),
        jnp.zeros((KV_HEADS, row_total), jnp.float32),
        jnp.zeros((KV_HEADS, row_total, HD), jnp.float32),
    )
    folder = make_folder(query_sets, position_sets, last_positions, KV_HEADS, HD, score_scale)
    final_sets = folder(
        (empty_state, empty_state),
        (
            lax.all_gather(key_states, "ctx", axis=1, tiled=True),
            lax.all_gather(value_states, "ctx", axis=1, tiled=True),
        ),
        jnp.int32(0),
    )
    first_out = finish(final_sets[0], half_rows, KV_HEADS, group_size, HD)
    second_out = finish(final_sets[1], half_rows, KV_HEADS, group_size, HD)
    attention = jnp.concatenate([first_out, second_out], axis=0)
    summed = residual[0].astype(jnp.float32) + lax.optimization_barrier(attention).astype(
        jnp.float32
    )
    normed = (
        summed * lax.rsqrt(jnp.mean(summed * summed, axis=-1, keepdims=True) + epsilon)
    ).astype(jnp.bfloat16)
    width_model = normed.shape[1]
    experts_each = ctx_count // PIECES
    expert_total = experts_each * exp_count
    pair_count = tok_rows * TOPK
    capacity = max(2, 2 * tok_rows * TOPK // expert_total)
    flat_ids = expert_ids[0].reshape(pair_count)
    onehot = (flat_ids[:, None] == jnp.arange(expert_total, dtype=jnp.int32)[None, :]).astype(
        jnp.int32
    )
    earlier = jnp.cumsum(onehot, axis=0) - onehot
    slot_index = jnp.sum(earlier * onehot, axis=1)
    owner_index = flat_ids // experts_each
    local_expert = flat_ids % experts_each
    target = (local_expert * exp_count + owner_index) * capacity + slot_index
    pair_token = jnp.arange(pair_count, dtype=jnp.int32) // TOPK
    slot_total = expert_total * capacity
    slot_table = jnp.full((slot_total,), tok_rows, jnp.int32).at[target].set(pair_token)
    padded = jnp.concatenate([normed, jnp.zeros((1, width_model), jnp.bfloat16)], axis=0)
    outgoing = padded[slot_table].reshape(experts_each, exp_count, capacity, width_model)
    arrived = lax.all_to_all(outgoing, "exp", split_axis=1, concat_axis=1, tiled=True)
    copies = jnp.broadcast_to(
        arrived[:, None], (experts_each, PIECES, exp_count, capacity, width_model)
    ).reshape(ctx_count, exp_count * capacity, width_model)
    gate_piece = gate_weight[0, 0]
    up_piece = up_weight[0, 0]
    down_piece = down_weight[0, 0]
    received = lax.all_to_all(copies, "ctx", split_axis=0, concat_axis=0, tiled=True)
    sources = received.shape[0]
    item_count = received.shape[1]
    flat_rows = received.reshape(sources * item_count, width_model)
    gate_part = contract_rows(flat_rows, gate_piece)
    up_part = contract_rows(flat_rows, up_piece)
    active = (jax.nn.silu(gate_part) * up_part).astype(jnp.bfloat16)
    partial_out = jnp.dot(active, down_piece, preferred_element_type=jnp.float32).astype(
        jnp.bfloat16
    )
    returned = lax.all_to_all(
        partial_out.reshape(sources, item_count, width_model),
        "ctx",
        split_axis=0,
        concat_axis=0,
        tiled=True,
    )
    piece_sum = jnp.sum(
        returned.reshape(experts_each, PIECES, exp_count, capacity, width_model).astype(
            jnp.float32
        ),
        axis=1,
    ).astype(jnp.bfloat16)
    arrived_back = lax.all_to_all(piece_sum, "exp", split_axis=1, concat_axis=1, tiled=True)
    gathered = arrived_back.reshape(slot_total, width_model)[target].astype(jnp.float32)
    weighted = gathered * route_weight[0]
    mixture = jnp.sum(weighted.reshape(tok_rows, TOPK, width_model), axis=1)
    return (summed + mixture).astype(jnp.bfloat16)[None]


AXES = ("ctx", "exp")


def spot(flat):
    ctx, exp = divmod(flat, 4)
    return ctx // 2, ctx % 2, exp // 2, exp % 2


def flat_of(z, x, y, core):
    return (z * 2 + x) * 4 + y * 2 + core


def move(array, rule):
    pairs = []
    for flat in range(32):
        there = rule(*spot(flat))
        if there is not None:
            pairs.append((flat, flat_of(*there)))
    return lax.ppermute(array, AXES, pairs)


def is_home(z, core):
    return core == z % 2


def to_twin(z, x, y, core):
    return z, x, y, 1 - core


def first_hop(z, x, y, core):
    return (z, x ^ 1, y, 1 - core) if is_home(z, core) else (z ^ 1, x, y, core)


def second_hop(z, x, y, core):
    return (z, x ^ 1, y, 1 - core) if is_home(z, core) else None


def slot_targets(ids_row, z_here, y_here, capacity):
    expert_count = 8
    token_count = ids_row.shape[1]
    lanes = lax.broadcasted_iota(jnp.int32, (expert_count, token_count), 0)
    onehot = (lanes == ids_row).astype(jnp.float32)
    before = (
        lax.broadcasted_iota(jnp.int32, (token_count, token_count), 0)
        < lax.broadcasted_iota(jnp.int32, (token_count, token_count), 1)
    ).astype(jnp.bfloat16)
    earlier = jnp.dot(onehot.astype(jnp.bfloat16), before, preferred_element_type=jnp.float32)
    slot = jnp.sum(earlier * onehot, axis=0, keepdims=True).astype(jnp.int32)
    owner = lax.shift_right_logical(ids_row, 1)
    z_there = (ids_row & 1) * 2 + (owner & 1)
    y_there = lax.shift_right_logical(owner, 1)
    relative = (z_there ^ z_here) * 2 + (y_there ^ y_here)
    return relative * capacity + slot


def slot_matrix(ids_row, z_here, y_here, capacity):
    target = slot_targets(ids_row, z_here, y_here, capacity)
    rows = lax.broadcasted_iota(jnp.int32, (8 * capacity, ids_row.shape[1]), 0)
    return (rows == target).astype(jnp.bfloat16)


def fetch_all(pairs, semaphores):
    copies = [
        pltpu.make_async_copy(source, target, semaphores.at[i])
        for i, (source, target) in enumerate(pairs)
    ]
    for copy in copies:
        copy.start()
    return copies


def attend_kernel(where_ref, ids_ref, queries_from, residual_from, *refs):
    kv_from, summed_to, out_refs = refs[:8], refs[8], refs[9:17]
    queries_ref, residual_ref, kv_ref, bias_ref, mixed_ref, summed_ref, semaphores = refs[17:]
    tokens = queries_ref.shape[0]
    group = HEADS // KV_HEADS
    ctx_here = where_ref[0]
    copies = fetch_all(
        [(queries_from, queries_ref), (residual_from, residual_ref)]
        + [(kv_from[k], kv_ref.at[pl.ds(k * tokens, tokens)]) for k in range(8)],
        semaphores,
    )
    row = lax.broadcasted_iota(jnp.int32, (tokens, tokens), 0)
    column = lax.broadcasted_iota(jnp.int32, (tokens, tokens), 1)
    for k in range(8):
        span = slice(k * tokens, (k + 1) * tokens)
        if k == 0:
            bias_ref[:, span] = jnp.where(column <= row, 0.0, negative_fill)
        else:
            bias_ref[:, span] = jnp.full(
                (tokens, tokens), jnp.where(ctx_here >= k, 0.0, negative_fill), jnp.float32
            )
    for copy in copies[2:] + copies[:1]:
        copy.wait()
    factor = math.log2(math.e) / math.sqrt(HD)
    heads_each = 2
    for first in range(0, HEADS, heads_each):
        kv_head = first // group
        key_side = slice(kv_head * HD, (kv_head + 1) * HD)
        value_side = slice((KV_HEADS + kv_head) * HD, (KV_HEADS + kv_head + 1) * HD)
        rows = jnp.concatenate(
            [queries_ref[:, h * HD : (h + 1) * HD] for h in range(first, first + heads_each)], axis=0
        )
        scores = contract_rows(rows, kv_ref[:, key_side])
        scores = scores + jnp.concatenate([bias_ref[...]] * heads_each, axis=0)
        largest = jnp.max(scores, axis=1, keepdims=True)
        exponent = jnp.exp2((scores - largest) * factor)
        total = jnp.sum(exponent, axis=1, keepdims=True)
        product = jnp.dot(
            exponent.astype(jnp.bfloat16), kv_ref[:, value_side], preferred_element_type=jnp.float32
        )
        result = product / total
        for j in range(heads_each):
            mixed_ref[:, (first + j) * HD : (first + j + 1) * HD] = result[
                j * tokens : (j + 1) * tokens
            ].astype(jnp.bfloat16)
    copies[1].wait()
    summed = residual_ref[...].astype(jnp.float32) + mixed_ref[...].astype(jnp.float32)
    summed_ref[...] = summed
    keep = pltpu.make_async_copy(summed_ref, summed_to, semaphores.at[10])
    keep.start()
    scale = lax.rsqrt(jnp.mean(summed * summed, axis=1, keepdims=True) + epsilon)
    normed = (summed * scale).astype(jnp.bfloat16)
    capacity = out_refs[0].shape[0]
    choose = slot_matrix(ids_ref[...], where_ref[1], where_ref[2], capacity)
    slots = jnp.dot(choose, normed, preferred_element_type=jnp.float32).astype(jnp.bfloat16)
    for k in range(8):
        out_refs[k][...] = slots[k * capacity : (k + 1) * capacity]
    keep.wait()


def load_pack(pack, strip, targets, semaphores):
    return [
        pltpu.make_async_copy(
            pack.at[pl.ds(kind * strip, strip)], targets[kind], semaphores.at[kind]
        )
        for kind in range(3)
    ]


def active_of(rows, gate, up):
    gate_part = contract_rows(rows, gate)
    up_part = contract_rows(rows, up)
    silu = gate_part / (1.0 + jnp.exp(-gate_part))
    return (silu * up_part).astype(jnp.bfloat16)


def expert_kernel(row_count, where_ref, *refs):
    row_from, refs = refs[:row_count], refs[row_count:]
    first_piece = len(refs) == 9
    if first_piece:
        packs, (total_ref,), rest = refs[:1], refs[1:2], refs[2:]
    else:
        packs, before_from, (mine_ref, twins_ref), rest = refs[:2], refs[2], refs[3:5], refs[5:]
    rows_ref, before_ref, gate_ref, up_ref, down_ref, row_semaphores, semaphores = rest
    strip = packs[0].shape[0] // 3
    targets = (gate_ref, up_ref, down_ref)
    loads = []
    place = 0
    for ref in row_from:
        loads.append((ref, rows_ref.at[pl.ds(place, ref.shape[0])]))
        place += ref.shape[0]
    if not first_piece:
        loads.append((before_from, before_ref))
    row_copies = fetch_all(loads, row_semaphores)
    weight_copies = load_pack(packs[0], strip, targets, semaphores)
    if first_piece:
        for copy in weight_copies:
            copy.start()
    else:
        at_home = where_ref[3] == 1

        @pl.when(at_home)
        def _():
            for copy in load_pack(packs[0], strip, targets, semaphores):
                copy.start()

        @pl.when(jnp.logical_not(at_home))
        def _():
            for copy in load_pack(packs[1], strip, targets, semaphores):
                copy.start()

    for copy in row_copies + weight_copies[:2]:
        copy.wait()
    active = active_of(rows_ref[...], gate_ref[...], up_ref[...])
    for copy in weight_copies[2:]:
        copy.wait()
    result = jnp.dot(active, down_ref[...], preferred_element_type=jnp.float32)
    if first_piece:
        total_ref[...] = result
    else:
        result = result + before_ref[...]
        half = result.shape[0] // 2
        mine_ref[...] = result[:half]
        twins_ref[...] = result[half:].astype(jnp.bfloat16)


def join_kernel(mine_from, other_from, *refs):
    out_refs, (mine_ref, other_ref, semaphores) = refs[:8], refs[8:]
    capacity = out_refs[0].shape[0]
    for copy in fetch_all([(mine_from, mine_ref), (other_from, other_ref)], semaphores):
        copy.wait()
    result = (mine_ref[...] + other_ref[...].astype(jnp.float32)).astype(jnp.bfloat16)
    for k in range(8):
        out_refs[k][...] = result[k * capacity : (k + 1) * capacity]


def combine_kernel(where_ref, ids_ref, route_ref, summed_ref, *refs):
    row_refs, out_ref = refs[:8], refs[8]
    capacity = row_refs[0].shape[0]
    choose = slot_matrix(ids_ref[...], where_ref[1], where_ref[2], capacity)
    rows = jnp.concatenate([ref[...] for ref in row_refs], axis=0)
    picked = lax.dot_general(
        choose, rows, (((0,), (0,)), ((), ())), preferred_element_type=jnp.float32
    )
    out_ref[...] = (summed_ref[...] + picked * route_ref[...]).astype(jnp.bfloat16)


IN_VMEM = pl.BlockSpec(memory_space=pltpu.VMEM)
IN_SMEM = pl.BlockSpec(memory_space=pltpu.SMEM)
IN_HBM = pl.BlockSpec(memory_space=pltpu.HBM)


def shards_cube(
    residual,
    queries,
    key_states,
    value_states,
    expert_ids,
    route_weight,
    gate_weight,
    up_weight,
    down_weight,
):
    ctx_here = lax.axis_index("ctx")
    exp_here = lax.axis_index("exp")
    home = ((ctx_here // 2) % 2 == exp_here % 2).astype(jnp.int32)
    where = jnp.stack([ctx_here, ctx_here // 2, exp_here // 2, home]).astype(jnp.int32)
    tokens, width = residual.shape[1:]
    piece = gate_weight.shape[2]
    capacity = max(2, 2 * tokens * TOPK // 8)
    ids_row = expert_ids[0].reshape(1, tokens)
    kv_own = jnp.concatenate([key_states[0], value_states[0]], axis=1)
    kv_blocks = {0: kv_own}

    def send_keys(block, k):
        def later(z, x, y, core):
            ctx = 2 * z + x + k
            return (ctx // 2, ctx % 2, y, core) if ctx < 8 else None

        kv_blocks[k] = move(block, later)

    own = jnp.concatenate([gate_weight[0, 0], up_weight[0, 0], down_weight[0, 0]], axis=0)
    one = move(own, first_hop)
    for k in (4, 5, 3, 2, 6, 1, 7):
        send_keys(kv_own, k)
    kv_list = [kv_blocks[k] for k in range(1, 8)]
    one, *kv_list = lax.optimization_barrier((one, *kv_list))
    last = move(one, second_hop)
    slot_shape = jax.ShapeDtypeStruct((capacity, width), jnp.bfloat16)
    keys_all = 8 * tokens
    rows_all = 8 * capacity
    first_out = pl.pallas_call(
        attend_kernel,
        out_shape=[jax.ShapeDtypeStruct((tokens, width), jnp.float32)] + [slot_shape] * 8,
        in_specs=[IN_SMEM, IN_VMEM] + [IN_HBM] * 10,
        out_specs=[IN_HBM] + [IN_VMEM] * 8,
        scratch_shapes=[
            pltpu.VMEM((tokens, width), jnp.bfloat16),
            pltpu.VMEM((tokens, width), jnp.bfloat16),
            pltpu.VMEM((keys_all, 2 * KV_HEADS * HD), jnp.bfloat16),
            pltpu.VMEM((tokens, keys_all), jnp.float32),
            pltpu.VMEM((tokens, width), jnp.bfloat16),
            pltpu.VMEM((tokens, width), jnp.float32),
            pltpu.SemaphoreType.DMA((11,)),
        ],
        compiler_params=pltpu.CompilerParams(vmem_limit_bytes=58 << 20),
        cost_estimate=pl.CostEstimate(
            flops=4 * tokens * keys_all * HEADS * HD,
            bytes_accessed=8 * tokens * width,
            transcendentals=tokens * keys_all * HEADS,
        ),
        name="attend",
    )(where, ids_row, queries[0], residual[0], kv_own, *kv_list)
    summed, outgoing = first_out[0], list(first_out[1:])

    def swap(array, k):
        if k == 0:
            return array
        return move(array, lambda z, x, y, core: (z ^ (k >> 1), x, y ^ (k & 1), core))

    arrived = {0: outgoing[0]}
    for k in (4, 6, 5, 7, 2, 3, 1):
        arrived[k] = swap(outgoing[k], k)
    order = (0, 2, 3, 1, 4, 6, 5, 7)
    row_parts = [jnp.concatenate([arrived[k] for k in group]) for group in (order[:4], order[4:])]
    row_parts += [move(part, to_twin) for part in row_parts]

    def run_expert(packs, before):
        row_total = 2 * rows_all
        mine = jax.ShapeDtypeStruct((rows_all, width), jnp.float32)
        twins = jax.ShapeDtypeStruct((rows_all, width), jnp.bfloat16)
        total = jax.ShapeDtypeStruct((row_total, width), jnp.float32)
        return pl.pallas_call(
            partial(expert_kernel, len(row_parts)),
            out_shape=[mine, twins] if before else [total],
            in_specs=[IN_SMEM] + [IN_HBM] * (len(row_parts) + len(packs) + len(before)),
            out_specs=[IN_VMEM] * (2 if before else 1),
            scratch_shapes=[
                pltpu.VMEM((row_total, width), jnp.bfloat16),
                pltpu.VMEM((row_total if before else 8, width), jnp.float32),
                pltpu.VMEM((piece, width), jnp.bfloat16),
                pltpu.VMEM((piece, width), jnp.bfloat16),
                pltpu.VMEM((piece, width), jnp.bfloat16),
                pltpu.SemaphoreType.DMA((5,)),
                pltpu.SemaphoreType.DMA((3,)),
            ],
            compiler_params=pltpu.CompilerParams(vmem_limit_bytes=32 << 20),
            cost_estimate=pl.CostEstimate(
                flops=6 * row_total * piece * width,
                bytes_accessed=6 * piece * width,
                transcendentals=row_total * piece,
            ),
            name="experts_rest" if before else "experts_first",
        )(where, *row_parts, *packs, *before)

    first_total = run_expert([one], [])
    last, *first_total = lax.optimization_barrier((last, *first_total))
    mine, twins = run_expert([own, last], first_total)
    joined = pl.pallas_call(
        join_kernel,
        out_shape=[slot_shape] * 8,
        in_specs=[IN_HBM] * 2,
        out_specs=[IN_VMEM] * 8,
        scratch_shapes=[
            pltpu.VMEM((rows_all, width), jnp.float32),
            pltpu.VMEM((rows_all, width), jnp.bfloat16),
            pltpu.SemaphoreType.DMA((2,)),
        ],
        compiler_params=pltpu.CompilerParams(vmem_limit_bytes=16 << 20),
        cost_estimate=pl.CostEstimate(
            flops=rows_all * width, bytes_accessed=8 * rows_all * width, transcendentals=0
        ),
        name="join",
    )(mine, move(twins, to_twin))
    results = [joined[order.index(k)] for k in range(8)]
    returned = [swap(results[k], k) for k in range(8)]
    output = pl.pallas_call(
        combine_kernel,
        out_shape=jax.ShapeDtypeStruct((tokens, width), jnp.bfloat16),
        in_specs=[IN_SMEM] + [IN_VMEM] * 11,
        out_specs=IN_VMEM,
        compiler_params=pltpu.CompilerParams(vmem_limit_bytes=12 << 20),
        cost_estimate=pl.CostEstimate(
            flops=2 * tokens * 8 * capacity * width,
            bytes_accessed=12 * tokens * width,
            transcendentals=0,
        ),
        name="combine",
    )(where, ids_row, route_weight[0], summed, *returned)
    return output[None]


def solution(mesh):
    in_specs = (
        P("exp", "ctx", None),
        P("exp", "ctx", None),
        P("exp", "ctx", None),
        P("exp", "ctx", None),
        P("exp", "ctx", None),
        P("exp", "ctx", None),
        P("exp", "ctx", None, None),
        P("exp", "ctx", None, None),
        P("exp", "ctx", None, None),
    )
    out_specs = P("exp", "ctx", None)
    cube = mesh.shape["ctx"] == 8 and mesh.shape["exp"] == 4
    body = shards_cube if cube else shards
    return jax.shard_map(body, mesh=mesh, in_specs=in_specs, out_specs=out_specs, check_vma=False)
```

```python
from functools import partial
import math

import jax
import jax.numpy as jnp
from jax import lax
from jax.experimental import pallas as pl
from jax.experimental.pallas import tpu as pltpu
from jax.sharding import PartitionSpec as P

HD = 128
HEADS = 16
KV_HEADS = 2
PIECES = 4
TOPK = 1


negative_fill = -1e30
epsilon = 1e-06


def contract_rows(left_rows, weight_rows):
    return lax.dot_general(
        left_rows, weight_rows, (((1,), (1,)), ((), ())), preferred_element_type=jnp.float32
    )


def to_groups(half_block, heads_kv, group_size, head_dim):
    token_count = half_block.shape[0]
    shaped = half_block.reshape(token_count, heads_kv, group_size, head_dim)
    return jnp.transpose(shaped, (1, 0, 2, 3)).reshape(heads_kv, token_count * group_size, head_dim)


def keep_current(current):
    return current


def block_update(current, query_rows, query_pos, key_block, value_block, key_start, score_scale):
    running_max, running_total, accumulated = current
    scores = (
        jnp.einsum("gqd,kgd->gqk", query_rows, key_block, preferred_element_type=jnp.float32)
        * score_scale
    )
    key_pos = key_start + jnp.arange(key_block.shape[0], dtype=jnp.int32)
    allowed = key_pos[None, None, :] <= query_pos[None, :, None]
    scores = jnp.where(allowed, scores, negative_fill)
    new_max = jnp.maximum(running_max, jnp.max(scores, axis=-1))
    rescale = jnp.exp(running_max - new_max)
    exponent = jnp.where(allowed, jnp.exp(scores - new_max[..., None]), 0.0)
    new_total = running_total * rescale + jnp.sum(exponent, axis=-1)
    product = jnp.einsum(
        "gqk,kgd->gqd",
        exponent.astype(jnp.bfloat16),
        value_block,
        preferred_element_type=jnp.float32,
    )
    return (new_max, new_total, accumulated * rescale[..., None] + product)


def make_folder(query_sets, position_sets, last_positions, heads_kv, head_dim, score_scale):

    def fold_keys(running, key_piece, first_key):
        key_part, value_part = key_piece
        key_count = key_part.shape[1]
        key_width = math.gcd(key_count, 512)
        key_rows = key_part.reshape(key_count, heads_kv, head_dim)
        value_rows = value_part.reshape(key_count, heads_kv, head_dim)

        def one_block(block_index, current_sets):
            offset = block_index * key_width
            key_block = lax.dynamic_slice_in_dim(key_rows, offset, key_width, 0)
            value_block = lax.dynamic_slice_in_dim(value_rows, offset, key_width, 0)
            updated = []
            for current, query_rows, query_pos, last_pos in zip(
                current_sets, query_sets, position_sets, last_positions
            ):
                step_fn = partial(
                    block_update,
                    query_rows=query_rows,
                    query_pos=query_pos,
                    key_block=key_block,
                    value_block=value_block,
                    key_start=offset,
                    score_scale=score_scale,
                )
                updated.append(lax.cond(offset <= last_pos, step_fn, keep_current, current))
            return tuple(updated)

        return lax.fori_loop(0, key_count // key_width, one_block, running)

    return fold_keys


def finish(current, token_count, heads_kv, group_size, head_dim):
    running_max, running_total, accumulated = current
    result = accumulated / running_total[..., None]
    shaped = result.reshape(heads_kv, token_count, group_size, head_dim)
    return (
        jnp.transpose(shaped, (1, 0, 2, 3))
        .reshape(token_count, heads_kv * group_size * head_dim)
        .astype(jnp.bfloat16)
    )


def shards(
    residual,
    queries,
    key_states,
    value_states,
    expert_ids,
    route_weight,
    gate_weight,
    up_weight,
    down_weight,
):
    ctx_count = lax.axis_size("ctx")
    exp_count = lax.axis_size("exp")
    ctx_rank = lax.axis_index("ctx")
    tok_rows = residual.shape[1]
    half_rows = tok_rows // 2
    group_size = HEADS // KV_HEADS
    score_scale = 1.0 / math.sqrt(HD)
    local_queries = queries[0]
    first_half = local_queries[:half_rows]
    second_half = local_queries[half_rows:]
    first_start = ctx_rank * tok_rows
    second_start = first_start + half_rows
    offsets = jnp.repeat(jnp.arange(half_rows, dtype=jnp.int32), group_size)
    query_sets = (
        to_groups(first_half, KV_HEADS, group_size, HD),
        to_groups(second_half, KV_HEADS, group_size, HD),
    )
    position_sets = (first_start + offsets, second_start + offsets)
    last_positions = (first_start + half_rows - 1, second_start + half_rows - 1)
    row_total = half_rows * group_size
    empty_state = (
        jnp.full((KV_HEADS, row_total), negative_fill, jnp.float32),
        jnp.zeros((KV_HEADS, row_total), jnp.float32),
        jnp.zeros((KV_HEADS, row_total, HD), jnp.float32),
    )
    folder = make_folder(query_sets, position_sets, last_positions, KV_HEADS, HD, score_scale)
    final_sets = folder(
        (empty_state, empty_state),
        (
            lax.all_gather(key_states, "ctx", axis=1, tiled=True),
            lax.all_gather(value_states, "ctx", axis=1, tiled=True),
        ),
        jnp.int32(0),
    )
    first_out = finish(final_sets[0], half_rows, KV_HEADS, group_size, HD)
    second_out = finish(final_sets[1], half_rows, KV_HEADS, group_size, HD)
    attention = jnp.concatenate([first_out, second_out], axis=0)
    summed = residual[0].astype(jnp.float32) + lax.optimization_barrier(attention).astype(
        jnp.float32
    )
    normed = (
        summed * lax.rsqrt(jnp.mean(summed * summed, axis=-1, keepdims=True) + epsilon)
    ).astype(jnp.bfloat16)
    width_model = normed.shape[1]
    experts_each = ctx_count // PIECES
    expert_total = experts_each * exp_count
    pair_count = tok_rows * TOPK
    capacity = max(2, 2 * tok_rows * TOPK // expert_total)
    flat_ids = expert_ids[0].reshape(pair_count)
    onehot = (flat_ids[:, None] == jnp.arange(expert_total, dtype=jnp.int32)[None, :]).astype(
        jnp.int32
    )
    earlier = jnp.cumsum(onehot, axis=0) - onehot
    slot_index = jnp.sum(earlier * onehot, axis=1)
    owner_index = flat_ids // experts_each
    local_expert = flat_ids % experts_each
    target = (local_expert * exp_count + owner_index) * capacity + slot_index
    pair_token = jnp.arange(pair_count, dtype=jnp.int32) // TOPK
    slot_total = expert_total * capacity
    slot_table = jnp.full((slot_total,), tok_rows, jnp.int32).at[target].set(pair_token)
    padded = jnp.concatenate([normed, jnp.zeros((1, width_model), jnp.bfloat16)], axis=0)
    outgoing = padded[slot_table].reshape(experts_each, exp_count, capacity, width_model)
    arrived = lax.all_to_all(outgoing, "exp", split_axis=1, concat_axis=1, tiled=True)
    copies = jnp.broadcast_to(
        arrived[:, None], (experts_each, PIECES, exp_count, capacity, width_model)
    ).reshape(ctx_count, exp_count * capacity, width_model)
    gate_piece = gate_weight[0, 0]
    up_piece = up_weight[0, 0]
    down_piece = down_weight[0, 0]
    received = lax.all_to_all(copies, "ctx", split_axis=0, concat_axis=0, tiled=True)
    sources = received.shape[0]
    item_count = received.shape[1]
    flat_rows = received.reshape(sources * item_count, width_model)
    gate_part = contract_rows(flat_rows, gate_piece)
    up_part = contract_rows(flat_rows, up_piece)
    active = (jax.nn.silu(gate_part) * up_part).astype(jnp.bfloat16)
    partial_out = jnp.dot(active, down_piece, preferred_element_type=jnp.float32).astype(
        jnp.bfloat16
    )
    returned = lax.all_to_all(
        partial_out.reshape(sources, item_count, width_model),
        "ctx",
        split_axis=0,
        concat_axis=0,
        tiled=True,
    )
    piece_sum = jnp.sum(
        returned.reshape(experts_each, PIECES, exp_count, capacity, width_model).astype(
            jnp.float32
        ),
        axis=1,
    ).astype(jnp.bfloat16)
    arrived_back = lax.all_to_all(piece_sum, "exp", split_axis=1, concat_axis=1, tiled=True)
    gathered = arrived_back.reshape(slot_total, width_model)[target].astype(jnp.float32)
    weighted = gathered * route_weight[0]
    mixture = jnp.sum(weighted.reshape(tok_rows, TOPK, width_model), axis=1)
    return (summed + mixture).astype(jnp.bfloat16)[None]


AXES = ("ctx", "exp")


def spot(flat):
    ctx, exp = divmod(flat, 4)
    return ctx // 2, ctx % 2, exp // 2, exp % 2


def flat_of(z, x, y, core):
    return (z * 2 + x) * 4 + y * 2 + core


def move(array, rule):
    pairs = []
    for flat in range(32):
        there = rule(*spot(flat))
        if there is not None:
            pairs.append((flat, flat_of(*there)))
    return lax.ppermute(array, AXES, pairs)


def is_home(z, core):
    return core == z % 2


def to_twin(z, x, y, core):
    return z, x, y, 1 - core


def first_hop(z, x, y, core):
    return (z, x ^ 1, y, 1 - core) if is_home(z, core) else (z ^ 1, x, y, core)


def second_hop(z, x, y, core):
    return (z, x ^ 1, y, 1 - core) if is_home(z, core) else None


def slot_targets(ids_row, z_here, y_here, capacity):
    expert_count = 8
    token_count = ids_row.shape[1]
    lanes = lax.broadcasted_iota(jnp.int32, (expert_count, token_count), 0)
    onehot = (lanes == ids_row).astype(jnp.float32)
    before = (
        lax.broadcasted_iota(jnp.int32, (token_count, token_count), 0)
        < lax.broadcasted_iota(jnp.int32, (token_count, token_count), 1)
    ).astype(jnp.bfloat16)
    earlier = jnp.dot(onehot.astype(jnp.bfloat16), before, preferred_element_type=jnp.float32)
    slot = jnp.sum(earlier * onehot, axis=0, keepdims=True).astype(jnp.int32)
    owner = lax.shift_right_logical(ids_row, 1)
    z_there = (ids_row & 1) * 2 + (owner & 1)
    y_there = lax.shift_right_logical(owner, 1)
    relative = (z_there ^ z_here) * 2 + (y_there ^ y_here)
    return relative * capacity + slot


def slot_matrix(ids_row, z_here, y_here, capacity):
    target = slot_targets(ids_row, z_here, y_here, capacity)
    rows = lax.broadcasted_iota(jnp.int32, (8 * capacity, ids_row.shape[1]), 0)
    return (rows == target).astype(jnp.bfloat16)


def fetch_all(pairs, semaphores):
    copies = [
        pltpu.make_async_copy(source, target, semaphores.at[i])
        for i, (source, target) in enumerate(pairs)
    ]
    for copy in copies:
        copy.start()
    return copies


def attend_kernel(where_ref, ids_ref, queries_from, residual_from, *refs):
    kv_from, summed_to, out_refs = refs[:8], refs[8], refs[9:17]
    queries_ref, residual_ref, kv_ref, bias_ref, mixed_ref, summed_ref, semaphores = refs[17:]
    tokens = queries_ref.shape[0]
    group = HEADS // KV_HEADS
    copies = fetch_all(
        [(queries_from, queries_ref), (residual_from, residual_ref)]
        + [(kv_from[k], kv_ref.at[pl.ds(k * tokens, tokens)]) for k in range(8)],
        semaphores,
    )
    row = lax.broadcasted_iota(jnp.int32, (tokens, tokens), 0)
    column = lax.broadcasted_iota(jnp.int32, (tokens, tokens), 1)
    for k in range(8):
        span = slice(k * tokens, (k + 1) * tokens)
        if k == 0:
            bias_ref[:, span] = jnp.where(column <= row, 0.0, negative_fill)
        else:
            seen = where_ref[0] == 1 if k == 1 else where_ref[1] >= k // 2
            bias_ref[:, span] = jnp.full(
                (tokens, tokens), jnp.where(seen, 0.0, negative_fill), jnp.float32
            )
    for copy in copies[2:] + copies[:1]:
        copy.wait()
    factor = math.log2(math.e) / math.sqrt(HD)
    heads_each = 2
    for first in range(0, HEADS, heads_each):
        kv_head = first // group
        key_side = slice(kv_head * HD, (kv_head + 1) * HD)
        value_side = slice((KV_HEADS + kv_head) * HD, (KV_HEADS + kv_head + 1) * HD)
        rows = jnp.concatenate(
            [queries_ref[:, h * HD : (h + 1) * HD] for h in range(first, first + heads_each)], axis=0
        )
        scores = contract_rows(rows, kv_ref[:, key_side])
        scores = scores + jnp.concatenate([bias_ref[...]] * heads_each, axis=0)
        largest = jnp.max(scores, axis=1, keepdims=True)
        exponent = jnp.exp2((scores - largest) * factor)
        total = jnp.sum(exponent, axis=1, keepdims=True)
        product = jnp.dot(
            exponent.astype(jnp.bfloat16), kv_ref[:, value_side], preferred_element_type=jnp.float32
        )
        result = product / total
        for j in range(heads_each):
            mixed_ref[:, (first + j) * HD : (first + j + 1) * HD] = result[
                j * tokens : (j + 1) * tokens
            ].astype(jnp.bfloat16)
    copies[1].wait()
    summed = residual_ref[...].astype(jnp.float32) + mixed_ref[...].astype(jnp.float32)
    summed_ref[...] = summed
    keep = pltpu.make_async_copy(summed_ref, summed_to, semaphores.at[10])
    keep.start()
    scale = lax.rsqrt(jnp.mean(summed * summed, axis=1, keepdims=True) + epsilon)
    normed = (summed * scale).astype(jnp.bfloat16)
    capacity = out_refs[0].shape[0]
    choose = slot_matrix(ids_ref[...], where_ref[1], where_ref[2], capacity)
    slots = jnp.dot(choose, normed, preferred_element_type=jnp.float32).astype(jnp.bfloat16)
    for k in range(8):
        out_refs[k][...] = slots[k * capacity : (k + 1) * capacity]
    keep.wait()


def load_pack(pack, strip, targets, semaphores):
    return [
        pltpu.make_async_copy(
            pack.at[pl.ds(kind * strip, strip)], targets[kind], semaphores.at[kind]
        )
        for kind in range(3)
    ]


def active_of(rows, gate, up):
    gate_part = contract_rows(rows, gate)
    up_part = contract_rows(rows, up)
    silu = gate_part / (1.0 + jnp.exp(-gate_part))
    return (silu * up_part).astype(jnp.bfloat16)


def expert_kernel(row_count, where_ref, *refs):
    row_from, refs = refs[:row_count], refs[row_count:]
    first_piece = len(refs) == 9
    if first_piece:
        packs, (total_ref,), rest = refs[:1], refs[1:2], refs[2:]
    else:
        packs, own_from, before_from = refs[:1], refs[1:4], refs[4]
        (mine_ref, twins_ref), rest = refs[5:7], refs[7:]
    rows_ref, before_ref, gate_ref, up_ref, down_ref, row_semaphores, semaphores = rest
    strip = packs[0].shape[0] // 3
    targets = (gate_ref, up_ref, down_ref)
    loads = []
    place = 0
    for ref in row_from:
        loads.append((ref, rows_ref.at[pl.ds(place, ref.shape[0])]))
        place += ref.shape[0]
    if not first_piece:
        loads.append((before_from, before_ref))
    row_copies = fetch_all(loads, row_semaphores)
    weight_copies = load_pack(packs[0], strip, targets, semaphores)
    if first_piece:
        for copy in weight_copies:
            copy.start()
    else:
        at_home = where_ref[3] == 1

        @pl.when(at_home)
        def _():
            for kind in range(3):
                pltpu.make_async_copy(own_from[kind], targets[kind], semaphores.at[kind]).start()

        @pl.when(jnp.logical_not(at_home))
        def _():
            for copy in weight_copies:
                copy.start()

    for copy in row_copies + weight_copies[:2]:
        copy.wait()
    active = active_of(rows_ref[...], gate_ref[...], up_ref[...])
    for copy in weight_copies[2:]:
        copy.wait()
    result = jnp.dot(active, down_ref[...], preferred_element_type=jnp.float32)
    if first_piece:
        total_ref[...] = result
    else:
        result = result + before_ref[...]
        half = result.shape[0] // 2
        mine_ref[...] = result[:half]
        twins_ref[...] = result[half:].astype(jnp.bfloat16)


def join_kernel(mine_from, other_from, *refs):
    out_refs, (mine_ref, other_ref, semaphores) = refs[:8], refs[8:]
    capacity = out_refs[0].shape[0]
    for copy in fetch_all([(mine_from, mine_ref), (other_from, other_ref)], semaphores):
        copy.wait()
    result = (mine_ref[...] + other_ref[...].astype(jnp.float32)).astype(jnp.bfloat16)
    for k in range(8):
        out_refs[k][...] = result[k * capacity : (k + 1) * capacity]


def combine_kernel(where_ref, ids_ref, route_ref, summed_ref, *refs):
    row_refs, out_ref = refs[:8], refs[8]
    capacity = row_refs[0].shape[0]
    choose = slot_matrix(ids_ref[...], where_ref[1], where_ref[2], capacity)
    rows = jnp.concatenate([ref[...] for ref in row_refs], axis=0)
    picked = lax.dot_general(
        choose, rows, (((0,), (0,)), ((), ())), preferred_element_type=jnp.float32
    )
    out_ref[...] = (summed_ref[...] + picked * route_ref[...]).astype(jnp.bfloat16)


IN_VMEM = pl.BlockSpec(memory_space=pltpu.VMEM)
IN_SMEM = pl.BlockSpec(memory_space=pltpu.SMEM)
IN_HBM = pl.BlockSpec(memory_space=pltpu.HBM)


def shards_cube(
    residual,
    queries,
    key_states,
    value_states,
    expert_ids,
    route_weight,
    gate_weight,
    up_weight,
    down_weight,
):
    ctx_here = lax.axis_index("ctx")
    exp_here = lax.axis_index("exp")
    home = ((ctx_here // 2) % 2 == exp_here % 2).astype(jnp.int32)
    where = jnp.stack([ctx_here % 2, ctx_here // 2, exp_here // 2, home]).astype(jnp.int32)
    tokens, width = residual.shape[1:]
    piece = gate_weight.shape[2]
    capacity = max(2, 2 * tokens * TOPK // 8)
    ids_row = expert_ids[0].reshape(1, tokens)
    kv_own = jnp.concatenate([key_states[0], value_states[0]], axis=1)
    weights = (gate_weight[0, 0], up_weight[0, 0], down_weight[0, 0])
    own_first = jnp.concatenate([weights[0], weights[1]], axis=0)
    own_second = weights[2]

    def along_z(steps):
        return move(
            kv_own, lambda z, x, y, core: (z + steps, x, y, core) if z + steps < 4 else None
        )

    def over_x(block, steps):
        def rule(z, x, y, core):
            return (z, 1 - x, y, core) if z >= steps and (steps or x == 0) else None

        return move(block, rule)

    one_first = move(own_first, first_hop)
    kv_along = [kv_own] + [along_z(steps) for steps in (1, 2, 3)]
    kv_list = []
    for steps in range(4):
        kv_list += [kv_along[steps], over_x(kv_along[steps], steps)]
    one_first, own_second, *kv_list = lax.optimization_barrier((one_first, own_second, *kv_list))
    one_second = move(own_second, first_hop)
    slot_shape = jax.ShapeDtypeStruct((capacity, width), jnp.bfloat16)
    keys_all = 8 * tokens
    rows_all = 8 * capacity
    first_out = pl.pallas_call(
        attend_kernel,
        out_shape=[jax.ShapeDtypeStruct((tokens, width), jnp.float32)] + [slot_shape] * 8,
        in_specs=[IN_SMEM, IN_VMEM] + [IN_HBM] * 10,
        out_specs=[IN_HBM] + [IN_VMEM] * 8,
        scratch_shapes=[
            pltpu.VMEM((tokens, width), jnp.bfloat16),
            pltpu.VMEM((tokens, width), jnp.bfloat16),
            pltpu.VMEM((keys_all, 2 * KV_HEADS * HD), jnp.bfloat16),
            pltpu.VMEM((tokens, keys_all), jnp.float32),
            pltpu.VMEM((tokens, width), jnp.bfloat16),
            pltpu.VMEM((tokens, width), jnp.float32),
            pltpu.SemaphoreType.DMA((11,)),
        ],
        compiler_params=pltpu.CompilerParams(vmem_limit_bytes=58 << 20),
        cost_estimate=pl.CostEstimate(
            flops=4 * tokens * keys_all * HEADS * HD,
            bytes_accessed=8 * tokens * width,
            transcendentals=tokens * keys_all * HEADS,
        ),
        name="attend",
    )(where, ids_row, queries[0], residual[0], *kv_list)
    summed, outgoing = first_out[0], list(first_out[1:])

    def swap(array, k):
        if k == 0:
            return array
        return move(array, lambda z, x, y, core: (z ^ (k >> 1), x, y ^ (k & 1), core))

    one_second, *outgoing = lax.optimization_barrier((one_second, *outgoing))
    one = jnp.concatenate([one_first, one_second], axis=0)
    last = move(one, second_hop)
    arrived = {0: outgoing[0]}
    for k in (4, 6, 5, 7, 2, 3, 1):
        arrived[k] = swap(outgoing[k], k)
    order = (0, 2, 3, 1, 4, 6, 5, 7)
    row_parts = [jnp.concatenate([arrived[k] for k in group]) for group in (order[:4], order[4:])]
    row_parts += [move(part, to_twin) for part in row_parts]

    def run_expert(packs, before):
        row_total = 2 * rows_all
        mine = jax.ShapeDtypeStruct((rows_all, width), jnp.float32)
        twins = jax.ShapeDtypeStruct((rows_all, width), jnp.bfloat16)
        total = jax.ShapeDtypeStruct((row_total, width), jnp.float32)
        return pl.pallas_call(
            partial(expert_kernel, len(row_parts)),
            out_shape=[mine, twins] if before else [total],
            in_specs=[IN_SMEM] + [IN_HBM] * (len(row_parts) + len(packs) + len(before)),
            out_specs=[IN_VMEM] * (2 if before else 1),
            scratch_shapes=[
                pltpu.VMEM((row_total, width), jnp.bfloat16),
                pltpu.VMEM((row_total if before else 8, width), jnp.float32),
                pltpu.VMEM((piece, width), jnp.bfloat16),
                pltpu.VMEM((piece, width), jnp.bfloat16),
                pltpu.VMEM((piece, width), jnp.bfloat16),
                pltpu.SemaphoreType.DMA((5,)),
                pltpu.SemaphoreType.DMA((3,)),
            ],
            compiler_params=pltpu.CompilerParams(vmem_limit_bytes=32 << 20),
            cost_estimate=pl.CostEstimate(
                flops=6 * row_total * piece * width,
                bytes_accessed=6 * piece * width,
                transcendentals=row_total * piece,
            ),
            name="experts_rest" if before else "experts_first",
        )(where, *row_parts, *packs, *before)

    first_total = run_expert([one], [])
    last, *first_total = lax.optimization_barrier((last, *first_total))
    mine, twins = run_expert([last, *weights], first_total)
    joined = pl.pallas_call(
        join_kernel,
        out_shape=[slot_shape] * 8,
        in_specs=[IN_HBM] * 2,
        out_specs=[IN_VMEM] * 8,
        scratch_shapes=[
            pltpu.VMEM((rows_all, width), jnp.float32),
            pltpu.VMEM((rows_all, width), jnp.bfloat16),
            pltpu.SemaphoreType.DMA((2,)),
        ],
        compiler_params=pltpu.CompilerParams(vmem_limit_bytes=16 << 20),
        cost_estimate=pl.CostEstimate(
            flops=rows_all * width, bytes_accessed=8 * rows_all * width, transcendentals=0
        ),
        name="join",
    )(mine, move(twins, to_twin))
    results = [joined[order.index(k)] for k in range(8)]
    returned = [swap(results[k], k) for k in range(8)]
    output = pl.pallas_call(
        combine_kernel,
        out_shape=jax.ShapeDtypeStruct((tokens, width), jnp.bfloat16),
        in_specs=[IN_SMEM] + [IN_VMEM] * 11,
        out_specs=IN_VMEM,
        compiler_params=pltpu.CompilerParams(vmem_limit_bytes=12 << 20),
        cost_estimate=pl.CostEstimate(
            flops=2 * tokens * 8 * capacity * width,
            bytes_accessed=12 * tokens * width,
            transcendentals=0,
        ),
        name="combine",
    )(where, ids_row, route_weight[0], summed, *returned)
    return output[None]


def solution(mesh):
    in_specs = (
        P("exp", "ctx", None),
        P("exp", "ctx", None),
        P("exp", "ctx", None),
        P("exp", "ctx", None),
        P("exp", "ctx", None),
        P("exp", "ctx", None),
        P("exp", "ctx", None, None),
        P("exp", "ctx", None, None),
        P("exp", "ctx", None, None),
    )
    out_specs = P("exp", "ctx", None)
    cube = mesh.shape["ctx"] == 8 and mesh.shape["exp"] == 4
    body = shards_cube if cube else shards
    return jax.shard_map(body, mesh=mesh, in_specs=in_specs, out_specs=out_specs, check_vma=False)
```

```python
from functools import partial
import math

import jax
import jax.numpy as jnp
from jax import lax
from jax.experimental import pallas as pl
from jax.experimental.pallas import tpu as pltpu
from jax.sharding import PartitionSpec as P

HD = 128
HEADS = 16
KV_HEADS = 2
PIECES = 4
TOPK = 1


negative_fill = -1e30
epsilon = 1e-06


def contract_rows(left_rows, weight_rows):
    return lax.dot_general(
        left_rows, weight_rows, (((1,), (1,)), ((), ())), preferred_element_type=jnp.float32
    )


def to_groups(half_block, heads_kv, group_size, head_dim):
    token_count = half_block.shape[0]
    shaped = half_block.reshape(token_count, heads_kv, group_size, head_dim)
    return jnp.transpose(shaped, (1, 0, 2, 3)).reshape(heads_kv, token_count * group_size, head_dim)


def keep_current(current):
    return current


def block_update(current, query_rows, query_pos, key_block, value_block, key_start, score_scale):
    running_max, running_total, accumulated = current
    scores = (
        jnp.einsum("gqd,kgd->gqk", query_rows, key_block, preferred_element_type=jnp.float32)
        * score_scale
    )
    key_pos = key_start + jnp.arange(key_block.shape[0], dtype=jnp.int32)
    allowed = key_pos[None, None, :] <= query_pos[None, :, None]
    scores = jnp.where(allowed, scores, negative_fill)
    new_max = jnp.maximum(running_max, jnp.max(scores, axis=-1))
    rescale = jnp.exp(running_max - new_max)
    exponent = jnp.where(allowed, jnp.exp(scores - new_max[..., None]), 0.0)
    new_total = running_total * rescale + jnp.sum(exponent, axis=-1)
    product = jnp.einsum(
        "gqk,kgd->gqd",
        exponent.astype(jnp.bfloat16),
        value_block,
        preferred_element_type=jnp.float32,
    )
    return (new_max, new_total, accumulated * rescale[..., None] + product)


def make_folder(query_sets, position_sets, last_positions, heads_kv, head_dim, score_scale):

    def fold_keys(running, key_piece, first_key):
        key_part, value_part = key_piece
        key_count = key_part.shape[1]
        key_width = math.gcd(key_count, 512)
        key_rows = key_part.reshape(key_count, heads_kv, head_dim)
        value_rows = value_part.reshape(key_count, heads_kv, head_dim)

        def one_block(block_index, current_sets):
            offset = block_index * key_width
            key_block = lax.dynamic_slice_in_dim(key_rows, offset, key_width, 0)
            value_block = lax.dynamic_slice_in_dim(value_rows, offset, key_width, 0)
            updated = []
            for current, query_rows, query_pos, last_pos in zip(
                current_sets, query_sets, position_sets, last_positions
            ):
                step_fn = partial(
                    block_update,
                    query_rows=query_rows,
                    query_pos=query_pos,
                    key_block=key_block,
                    value_block=value_block,
                    key_start=offset,
                    score_scale=score_scale,
                )
                updated.append(lax.cond(offset <= last_pos, step_fn, keep_current, current))
            return tuple(updated)

        return lax.fori_loop(0, key_count // key_width, one_block, running)

    return fold_keys


def finish(current, token_count, heads_kv, group_size, head_dim):
    running_max, running_total, accumulated = current
    result = accumulated / running_total[..., None]
    shaped = result.reshape(heads_kv, token_count, group_size, head_dim)
    return (
        jnp.transpose(shaped, (1, 0, 2, 3))
        .reshape(token_count, heads_kv * group_size * head_dim)
        .astype(jnp.bfloat16)
    )


def shards(
    residual,
    queries,
    key_states,
    value_states,
    expert_ids,
    route_weight,
    gate_weight,
    up_weight,
    down_weight,
):
    ctx_count = lax.axis_size("ctx")
    exp_count = lax.axis_size("exp")
    ctx_rank = lax.axis_index("ctx")
    tok_rows = residual.shape[1]
    half_rows = tok_rows // 2
    group_size = HEADS // KV_HEADS
    score_scale = 1.0 / math.sqrt(HD)
    local_queries = queries[0]
    first_half = local_queries[:half_rows]
    second_half = local_queries[half_rows:]
    first_start = ctx_rank * tok_rows
    second_start = first_start + half_rows
    offsets = jnp.repeat(jnp.arange(half_rows, dtype=jnp.int32), group_size)
    query_sets = (
        to_groups(first_half, KV_HEADS, group_size, HD),
        to_groups(second_half, KV_HEADS, group_size, HD),
    )
    position_sets = (first_start + offsets, second_start + offsets)
    last_positions = (first_start + half_rows - 1, second_start + half_rows - 1)
    row_total = half_rows * group_size
    empty_state = (
        jnp.full((KV_HEADS, row_total), negative_fill, jnp.float32),
        jnp.zeros((KV_HEADS, row_total), jnp.float32),
        jnp.zeros((KV_HEADS, row_total, HD), jnp.float32),
    )
    folder = make_folder(query_sets, position_sets, last_positions, KV_HEADS, HD, score_scale)
    final_sets = folder(
        (empty_state, empty_state),
        (
            lax.all_gather(key_states, "ctx", axis=1, tiled=True),
            lax.all_gather(value_states, "ctx", axis=1, tiled=True),
        ),
        jnp.int32(0),
    )
    first_out = finish(final_sets[0], half_rows, KV_HEADS, group_size, HD)
    second_out = finish(final_sets[1], half_rows, KV_HEADS, group_size, HD)
    attention = jnp.concatenate([first_out, second_out], axis=0)
    summed = residual[0].astype(jnp.float32) + lax.optimization_barrier(attention).astype(
        jnp.float32
    )
    normed = (
        summed * lax.rsqrt(jnp.mean(summed * summed, axis=-1, keepdims=True) + epsilon)
    ).astype(jnp.bfloat16)
    width_model = normed.shape[1]
    experts_each = ctx_count // PIECES
    expert_total = experts_each * exp_count
    pair_count = tok_rows * TOPK
    capacity = max(2, 2 * tok_rows * TOPK // expert_total)
    flat_ids = expert_ids[0].reshape(pair_count)
    onehot = (flat_ids[:, None] == jnp.arange(expert_total, dtype=jnp.int32)[None, :]).astype(
        jnp.int32
    )
    earlier = jnp.cumsum(onehot, axis=0) - onehot
    slot_index = jnp.sum(earlier * onehot, axis=1)
    owner_index = flat_ids // experts_each
    local_expert = flat_ids % experts_each
    target = (local_expert * exp_count + owner_index) * capacity + slot_index
    pair_token = jnp.arange(pair_count, dtype=jnp.int32) // TOPK
    slot_total = expert_total * capacity
    slot_table = jnp.full((slot_total,), tok_rows, jnp.int32).at[target].set(pair_token)
    padded = jnp.concatenate([normed, jnp.zeros((1, width_model), jnp.bfloat16)], axis=0)
    outgoing = padded[slot_table].reshape(experts_each, exp_count, capacity, width_model)
    arrived = lax.all_to_all(outgoing, "exp", split_axis=1, concat_axis=1, tiled=True)
    copies = jnp.broadcast_to(
        arrived[:, None], (experts_each, PIECES, exp_count, capacity, width_model)
    ).reshape(ctx_count, exp_count * capacity, width_model)
    gate_piece = gate_weight[0, 0]
    up_piece = up_weight[0, 0]
    down_piece = down_weight[0, 0]
    received = lax.all_to_all(copies, "ctx", split_axis=0, concat_axis=0, tiled=True)
    sources = received.shape[0]
    item_count = received.shape[1]
    flat_rows = received.reshape(sources * item_count, width_model)
    gate_part = contract_rows(flat_rows, gate_piece)
    up_part = contract_rows(flat_rows, up_piece)
    active = (jax.nn.silu(gate_part) * up_part).astype(jnp.bfloat16)
    partial_out = jnp.dot(active, down_piece, preferred_element_type=jnp.float32).astype(
        jnp.bfloat16
    )
    returned = lax.all_to_all(
        partial_out.reshape(sources, item_count, width_model),
        "ctx",
        split_axis=0,
        concat_axis=0,
        tiled=True,
    )
    piece_sum = jnp.sum(
        returned.reshape(experts_each, PIECES, exp_count, capacity, width_model).astype(
            jnp.float32
        ),
        axis=1,
    ).astype(jnp.bfloat16)
    arrived_back = lax.all_to_all(piece_sum, "exp", split_axis=1, concat_axis=1, tiled=True)
    gathered = arrived_back.reshape(slot_total, width_model)[target].astype(jnp.float32)
    weighted = gathered * route_weight[0]
    mixture = jnp.sum(weighted.reshape(tok_rows, TOPK, width_model), axis=1)
    return (summed + mixture).astype(jnp.bfloat16)[None]


AXES = ("ctx", "exp")


def spot(flat):
    ctx, exp = divmod(flat, 4)
    return ctx // 2, ctx % 2, exp // 2, exp % 2


def flat_of(z, x, y, core):
    return (z * 2 + x) * 4 + y * 2 + core


def move(array, rule):
    pairs = []
    for flat in range(32):
        there = rule(*spot(flat))
        if there is not None:
            pairs.append((flat, flat_of(*there)))
    return lax.ppermute(array, AXES, pairs)


def is_home(z, core):
    return core == z % 2


def to_twin(z, x, y, core):
    return z, x, y, 1 - core


def aside(z, x, y, core):
    return (z, x ^ 1, y, 1 - core) if is_home(z, core) else None


def homeward(z, x, y, core):
    return None if is_home(z, core) else (z ^ 1, x, y, core)


def second_hop(z, x, y, core):
    return (z, x ^ 1, y, 1 - core) if is_home(z, core) else None


def slot_targets(ids_row, z_here, y_here, capacity):
    expert_count = 8
    token_count = ids_row.shape[1]
    lanes = lax.broadcasted_iota(jnp.int32, (expert_count, token_count), 0)
    onehot = (lanes == ids_row).astype(jnp.float32)
    before = (
        lax.broadcasted_iota(jnp.int32, (token_count, token_count), 0)
        < lax.broadcasted_iota(jnp.int32, (token_count, token_count), 1)
    ).astype(jnp.bfloat16)
    earlier = jnp.dot(onehot.astype(jnp.bfloat16), before, preferred_element_type=jnp.float32)
    slot = jnp.sum(earlier * onehot, axis=0, keepdims=True).astype(jnp.int32)
    owner = lax.shift_right_logical(ids_row, 1)
    z_there = (ids_row & 1) * 2 + (owner & 1)
    y_there = lax.shift_right_logical(owner, 1)
    relative = (z_there ^ z_here) * 2 + (y_there ^ y_here)
    return relative * capacity + slot


def slot_matrix(ids_row, z_here, y_here, capacity):
    target = slot_targets(ids_row, z_here, y_here, capacity)
    rows = lax.broadcasted_iota(jnp.int32, (8 * capacity, ids_row.shape[1]), 0)
    return (rows == target).astype(jnp.bfloat16)


def fetch_all(pairs, semaphores):
    copies = [
        pltpu.make_async_copy(source, target, semaphores.at[i])
        for i, (source, target) in enumerate(pairs)
    ]
    for copy in copies:
        copy.start()
    return copies


def attend_kernel(where_ref, ids_ref, queries_from, residual_from, *refs):
    kv_from, summed_to, out_refs = refs[:8], refs[8], refs[9:17]
    queries_ref, residual_ref, kv_ref, bias_ref, mixed_ref, summed_ref, semaphores = refs[17:]
    tokens = queries_ref.shape[0]
    group = HEADS // KV_HEADS
    copies = fetch_all(
        [(kv_from[k], kv_ref.at[pl.ds(k * tokens, tokens)]) for k in range(8)]
        + [(queries_from, queries_ref), (residual_from, residual_ref)],
        semaphores,
    )
    row = lax.broadcasted_iota(jnp.int32, (tokens, tokens), 0)
    column = lax.broadcasted_iota(jnp.int32, (tokens, tokens), 1)
    for k in range(8):
        span = slice(k * tokens, (k + 1) * tokens)
        if k == 0:
            bias_ref[:, span] = jnp.where(column <= row, 0.0, negative_fill)
        else:
            seen = where_ref[0] == 1 if k == 1 else where_ref[1] >= k // 2
            bias_ref[:, span] = jnp.full(
                (tokens, tokens), jnp.where(seen, 0.0, negative_fill), jnp.float32
            )
    for copy in copies[:9]:
        copy.wait()
    factor = math.log2(math.e) / math.sqrt(HD)
    heads_each = 4
    for first in range(0, HEADS, heads_each):
        kv_head = first // group
        key_side = slice(kv_head * HD, (kv_head + 1) * HD)
        value_side = slice((KV_HEADS + kv_head) * HD, (KV_HEADS + kv_head + 1) * HD)
        rows = jnp.concatenate(
            [queries_ref[:, h * HD : (h + 1) * HD] for h in range(first, first + heads_each)], axis=0
        )
        scores = contract_rows(rows, kv_ref[:, key_side])
        scores = scores + jnp.concatenate([bias_ref[...]] * heads_each, axis=0)
        largest = jnp.max(scores, axis=1, keepdims=True)
        exponent = jnp.exp2((scores - largest) * factor)
        total = jnp.sum(exponent, axis=1, keepdims=True)
        product = jnp.dot(
            exponent.astype(jnp.bfloat16), kv_ref[:, value_side], preferred_element_type=jnp.float32
        )
        result = product / total
        for j in range(heads_each):
            mixed_ref[:, (first + j) * HD : (first + j + 1) * HD] = result[
                j * tokens : (j + 1) * tokens
            ].astype(jnp.bfloat16)
    copies[9].wait()
    summed = residual_ref[...].astype(jnp.float32) + mixed_ref[...].astype(jnp.float32)
    summed_ref[...] = summed
    keep = pltpu.make_async_copy(summed_ref, summed_to, semaphores.at[10])
    keep.start()
    scale = lax.rsqrt(jnp.mean(summed * summed, axis=1, keepdims=True) + epsilon)
    normed = (summed * scale).astype(jnp.bfloat16)
    capacity = out_refs[0].shape[0]
    choose = slot_matrix(ids_ref[...], where_ref[1], where_ref[2], capacity)
    slots = jnp.dot(choose, normed, preferred_element_type=jnp.float32).astype(jnp.bfloat16)
    for k in range(8):
        out_refs[k][...] = slots[k * capacity : (k + 1) * capacity]
    keep.wait()


def strips(pack, strip, count):
    return [pack.at[pl.ds(i * strip, strip)] for i in range(count)]


def load(sources, targets, semaphores):
    return [
        pltpu.make_async_copy(sources[kind], targets[kind], semaphores.at[kind])
        for kind in range(3)
    ]


def active_of(rows, gate, up):
    gate_part = contract_rows(rows, gate)
    up_part = contract_rows(rows, up)
    silu = gate_part / (1.0 + jnp.exp(-gate_part))
    return (silu * up_part).astype(jnp.bfloat16)


def expert_kernel(row_count, where_ref, *refs):
    row_from, refs = refs[:row_count], refs[row_count:]
    first_piece = len(refs) == 12
    strip = refs[-4].shape[0]
    if first_piece:
        at_home_from = strips(refs[0], strip, 3)
        away_from = refs[1:4]
        (total_ref,), rest = refs[4:5], refs[5:]
    else:
        away_from, at_home_from, before_from = strips(refs[0], strip, 3), refs[1:4], refs[4]
        (mine_ref, twins_ref), rest = refs[5:7], refs[7:]
    rows_ref, before_ref, gate_ref, up_ref, down_ref, row_semaphores, semaphores = rest
    targets = (gate_ref, up_ref, down_ref)
    loads = []
    place = 0
    for ref in row_from:
        loads.append((ref, rows_ref.at[pl.ds(place, ref.shape[0])]))
        place += ref.shape[0]
    if not first_piece:
        loads.append((before_from, before_ref))
    row_copies = fetch_all(loads, row_semaphores)
    weight_copies = load(at_home_from, targets, semaphores)
    at_home = where_ref[3] == 1

    @pl.when(at_home)
    def _():
        for copy in weight_copies:
            copy.start()

    @pl.when(jnp.logical_not(at_home))
    def _():
        for copy in load(away_from, targets, semaphores):
            copy.start()

    for copy in row_copies + weight_copies[:2]:
        copy.wait()
    active = active_of(rows_ref[...], gate_ref[...], up_ref[...])
    for copy in weight_copies[2:]:
        copy.wait()
    result = jnp.dot(active, down_ref[...], preferred_element_type=jnp.float32)
    if first_piece:
        total_ref[...] = result
    else:
        result = result + before_ref[...]
        half = result.shape[0] // 2
        mine_ref[...] = result[:half]
        twins_ref[...] = result[half:].astype(jnp.bfloat16)


def join_kernel(mine_from, other_from, *refs):
    out_refs, (mine_ref, other_ref, semaphores) = refs[:8], refs[8:]
    capacity = out_refs[0].shape[0]
    for copy in fetch_all([(mine_from, mine_ref), (other_from, other_ref)], semaphores):
        copy.wait()
    result = (mine_ref[...] + other_ref[...].astype(jnp.float32)).astype(jnp.bfloat16)
    for k in range(8):
        out_refs[k][...] = result[k * capacity : (k + 1) * capacity]


def combine_kernel(where_ref, ids_ref, route_ref, summed_ref, *refs):
    row_refs, out_ref = refs[:8], refs[8]
    capacity = row_refs[0].shape[0]
    choose = slot_matrix(ids_ref[...], where_ref[1], where_ref[2], capacity)
    rows = jnp.concatenate([ref[...] for ref in row_refs], axis=0)
    picked = lax.dot_general(
        choose, rows, (((0,), (0,)), ((), ())), preferred_element_type=jnp.float32
    )
    out_ref[...] = (summed_ref[...] + picked * route_ref[...]).astype(jnp.bfloat16)


IN_VMEM = pl.BlockSpec(memory_space=pltpu.VMEM)
IN_SMEM = pl.BlockSpec(memory_space=pltpu.SMEM)
IN_HBM = pl.BlockSpec(memory_space=pltpu.HBM)


def shards_cube(
    residual,
    queries,
    key_states,
    value_states,
    expert_ids,
    route_weight,
    gate_weight,
    up_weight,
    down_weight,
):
    ctx_here = lax.axis_index("ctx")
    exp_here = lax.axis_index("exp")
    at_home = ((ctx_here // 2) % 2 == exp_here % 2).astype(jnp.int32)
    where = jnp.stack([ctx_here % 2, ctx_here // 2, exp_here // 2, at_home]).astype(jnp.int32)
    tokens, width = residual.shape[1:]
    piece = gate_weight.shape[2]
    capacity = max(2, 2 * tokens * TOPK // 8)
    ids_row = expert_ids[0].reshape(1, tokens)
    kv_own = jnp.concatenate([key_states[0], value_states[0]], axis=1)
    weights = (gate_weight[0, 0], up_weight[0, 0], down_weight[0, 0])
    def along_z(steps):
        return move(
            kv_own, lambda z, x, y, core: (z + steps, x, y, core) if z + steps < 4 else None
        )

    def over_x(block, steps):
        def rule(z, x, y, core):
            return (z, 1 - x, y, core) if z >= steps and (steps or x == 0) else None

        return move(block, rule)

    beside = [move(w, aside) for w in weights[:2]]
    kv_along = [kv_own] + [along_z(steps) for steps in (1, 2, 3)]
    own = jnp.concatenate(weights, axis=0)
    own, where, beside[0], beside[1], *kv_along = lax.optimization_barrier(
        (own, where, *beside, *kv_along)
    )
    home = move(own, homeward)
    kv_list = []
    for steps in range(4):
        kv_list += [kv_along[steps], over_x(kv_along[steps], steps)]
    rest, *kv_list = lax.optimization_barrier((weights[2], *kv_list))
    beside_rest = move(rest, aside)
    slot_shape = jax.ShapeDtypeStruct((capacity, width), jnp.bfloat16)
    keys_all = 8 * tokens
    rows_all = 8 * capacity
    first_out = pl.pallas_call(
        attend_kernel,
        out_shape=[jax.ShapeDtypeStruct((tokens, width), jnp.float32)] + [slot_shape] * 8,
        in_specs=[IN_SMEM, IN_VMEM] + [IN_HBM] * 10,
        out_specs=[IN_HBM] + [IN_VMEM] * 8,
        scratch_shapes=[
            pltpu.VMEM((tokens, width), jnp.bfloat16),
            pltpu.VMEM((tokens, width), jnp.bfloat16),
            pltpu.VMEM((keys_all, 2 * KV_HEADS * HD), jnp.bfloat16),
            pltpu.VMEM((tokens, keys_all), jnp.float32),
            pltpu.VMEM((tokens, width), jnp.bfloat16),
            pltpu.VMEM((tokens, width), jnp.float32),
            pltpu.SemaphoreType.DMA((11,)),
        ],
        compiler_params=pltpu.CompilerParams(vmem_limit_bytes=58 << 20),
        cost_estimate=pl.CostEstimate(
            flops=4 * tokens * keys_all * HEADS * HD,
            bytes_accessed=8 * tokens * width,
            transcendentals=tokens * keys_all * HEADS,
        ),
        name="attend",
    )(where, ids_row, queries[0], residual[0], *kv_list)
    summed, outgoing = first_out[0], list(first_out[1:])

    def swap(array, k):
        if k == 0:
            return array
        return move(array, lambda z, x, y, core: (z ^ (k >> 1), x, y ^ (k & 1), core))

    last = move(home, second_hop)
    arrived = {0: outgoing[0]}
    beside_rest, *outgoing = lax.optimization_barrier((beside_rest, *outgoing))
    for k in (4, 6, 5, 7, 2, 3, 1):
        arrived[k] = swap(outgoing[k], k)
    order = (0, 2, 3, 1, 4, 6, 5, 7)
    row_parts = [jnp.concatenate([arrived[k] for k in group]) for group in (order[:4], order[4:])]
    row_parts += [move(part, to_twin) for part in row_parts]

    def run_expert(packs, before):
        row_total = 2 * rows_all
        mine = jax.ShapeDtypeStruct((rows_all, width), jnp.float32)
        twins = jax.ShapeDtypeStruct((rows_all, width), jnp.bfloat16)
        total = jax.ShapeDtypeStruct((row_total, width), jnp.float32)
        return pl.pallas_call(
            partial(expert_kernel, len(row_parts)),
            out_shape=[mine, twins] if before else [total],
            in_specs=[IN_SMEM] + [IN_HBM] * (len(row_parts) + len(packs) + len(before)),
            out_specs=[IN_VMEM] * (2 if before else 1),
            scratch_shapes=[
                pltpu.VMEM((row_total, width), jnp.bfloat16),
                pltpu.VMEM((row_total if before else 8, width), jnp.float32),
                pltpu.VMEM((piece, width), jnp.bfloat16),
                pltpu.VMEM((piece, width), jnp.bfloat16),
                pltpu.VMEM((piece, width), jnp.bfloat16),
                pltpu.SemaphoreType.DMA((5,)),
                pltpu.SemaphoreType.DMA((3,)),
            ],
            compiler_params=pltpu.CompilerParams(vmem_limit_bytes=32 << 20),
            cost_estimate=pl.CostEstimate(
                flops=6 * row_total * piece * width,
                bytes_accessed=6 * piece * width,
                transcendentals=row_total * piece,
            ),
            name="experts_rest" if before else "experts_first",
        )(where, *row_parts, *packs, *before)

    first_total = run_expert([home, *beside, beside_rest], [])
    last, *first_total = lax.optimization_barrier((last, *first_total))
    mine, twins = run_expert([last, *weights], first_total)
    joined = pl.pallas_call(
        join_kernel,
        out_shape=[slot_shape] * 8,
        in_specs=[IN_HBM] * 2,
        out_specs=[IN_VMEM] * 8,
        scratch_shapes=[
            pltpu.VMEM((rows_all, width), jnp.float32),
            pltpu.VMEM((rows_all, width), jnp.bfloat16),
            pltpu.SemaphoreType.DMA((2,)),
        ],
        compiler_params=pltpu.CompilerParams(vmem_limit_bytes=16 << 20),
        cost_estimate=pl.CostEstimate(
            flops=rows_all * width, bytes_accessed=8 * rows_all * width, transcendentals=0
        ),
        name="join",
    )(mine, move(twins, to_twin))
    results = [joined[order.index(k)] for k in range(8)]
    returned = [swap(results[k], k) for k in range(8)]
    output = pl.pallas_call(
        combine_kernel,
        out_shape=jax.ShapeDtypeStruct((tokens, width), jnp.bfloat16),
        in_specs=[IN_SMEM] + [IN_VMEM] * 11,
        out_specs=IN_VMEM,
        compiler_params=pltpu.CompilerParams(vmem_limit_bytes=12 << 20),
        cost_estimate=pl.CostEstimate(
            flops=2 * tokens * 8 * capacity * width,
            bytes_accessed=12 * tokens * width,
            transcendentals=0,
        ),
        name="combine",
    )(where, ids_row, route_weight[0], summed, *returned)
    return output[None]


def solution(mesh):
    in_specs = (
        P("exp", "ctx", None),
        P("exp", "ctx", None),
        P("exp", "ctx", None),
        P("exp", "ctx", None),
        P("exp", "ctx", None),
        P("exp", "ctx", None),
        P("exp", "ctx", None, None),
        P("exp", "ctx", None, None),
        P("exp", "ctx", None, None),
    )
    out_specs = P("exp", "ctx", None)
    cube = mesh.shape["ctx"] == 8 and mesh.shape["exp"] == 4
    body = shards_cube if cube else shards
    return jax.shard_map(body, mesh=mesh, in_specs=in_specs, out_specs=out_specs, check_vma=False)
```

```python
from functools import partial
import math

import jax
import jax.numpy as jnp
from jax import lax
from jax.experimental import pallas as pl
from jax.experimental.pallas import tpu as pltpu
from jax.sharding import PartitionSpec as P

HD = 128
HEADS = 16
KV_HEADS = 2
PIECES = 4
TOPK = 1


negative_fill = -1e30
epsilon = 1e-06


def contract_rows(left_rows, weight_rows):
    return lax.dot_general(
        left_rows, weight_rows, (((1,), (1,)), ((), ())), preferred_element_type=jnp.float32
    )


def to_groups(half_block, heads_kv, group_size, head_dim):
    token_count = half_block.shape[0]
    shaped = half_block.reshape(token_count, heads_kv, group_size, head_dim)
    return jnp.transpose(shaped, (1, 0, 2, 3)).reshape(heads_kv, token_count * group_size, head_dim)


def keep_current(current):
    return current


def block_update(current, query_rows, query_pos, key_block, value_block, key_start, score_scale):
    running_max, running_total, accumulated = current
    scores = (
        jnp.einsum("gqd,kgd->gqk", query_rows, key_block, preferred_element_type=jnp.float32)
        * score_scale
    )
    key_pos = key_start + jnp.arange(key_block.shape[0], dtype=jnp.int32)
    allowed = key_pos[None, None, :] <= query_pos[None, :, None]
    scores = jnp.where(allowed, scores, negative_fill)
    new_max = jnp.maximum(running_max, jnp.max(scores, axis=-1))
    rescale = jnp.exp(running_max - new_max)
    exponent = jnp.where(allowed, jnp.exp(scores - new_max[..., None]), 0.0)
    new_total = running_total * rescale + jnp.sum(exponent, axis=-1)
    product = jnp.einsum(
        "gqk,kgd->gqd",
        exponent.astype(jnp.bfloat16),
        value_block,
        preferred_element_type=jnp.float32,
    )
    return (new_max, new_total, accumulated * rescale[..., None] + product)


def make_folder(query_sets, position_sets, last_positions, heads_kv, head_dim, score_scale):

    def fold_keys(running, key_piece, first_key):
        key_part, value_part = key_piece
        key_count = key_part.shape[1]
        key_width = math.gcd(key_count, 512)
        key_rows = key_part.reshape(key_count, heads_kv, head_dim)
        value_rows = value_part.reshape(key_count, heads_kv, head_dim)

        def one_block(block_index, current_sets):
            offset = block_index * key_width
            key_block = lax.dynamic_slice_in_dim(key_rows, offset, key_width, 0)
            value_block = lax.dynamic_slice_in_dim(value_rows, offset, key_width, 0)
            updated = []
            for current, query_rows, query_pos, last_pos in zip(
                current_sets, query_sets, position_sets, last_positions
            ):
                step_fn = partial(
                    block_update,
                    query_rows=query_rows,
                    query_pos=query_pos,
                    key_block=key_block,
                    value_block=value_block,
                    key_start=offset,
                    score_scale=score_scale,
                )
                updated.append(lax.cond(offset <= last_pos, step_fn, keep_current, current))
            return tuple(updated)

        return lax.fori_loop(0, key_count // key_width, one_block, running)

    return fold_keys


def finish(current, token_count, heads_kv, group_size, head_dim):
    running_max, running_total, accumulated = current
    result = accumulated / running_total[..., None]
    shaped = result.reshape(heads_kv, token_count, group_size, head_dim)
    return (
        jnp.transpose(shaped, (1, 0, 2, 3))
        .reshape(token_count, heads_kv * group_size * head_dim)
        .astype(jnp.bfloat16)
    )


def shards(
    residual,
    queries,
    key_states,
    value_states,
    expert_ids,
    route_weight,
    gate_weight,
    up_weight,
    down_weight,
):
    ctx_count = lax.axis_size("ctx")
    exp_count = lax.axis_size("exp")
    ctx_rank = lax.axis_index("ctx")
    tok_rows = residual.shape[1]
    half_rows = tok_rows // 2
    group_size = HEADS // KV_HEADS
    score_scale = 1.0 / math.sqrt(HD)
    local_queries = queries[0]
    first_half = local_queries[:half_rows]
    second_half = local_queries[half_rows:]
    first_start = ctx_rank * tok_rows
    second_start = first_start + half_rows
    offsets = jnp.repeat(jnp.arange(half_rows, dtype=jnp.int32), group_size)
    query_sets = (
        to_groups(first_half, KV_HEADS, group_size, HD),
        to_groups(second_half, KV_HEADS, group_size, HD),
    )
    position_sets = (first_start + offsets, second_start + offsets)
    last_positions = (first_start + half_rows - 1, second_start + half_rows - 1)
    row_total = half_rows * group_size
    empty_state = (
        jnp.full((KV_HEADS, row_total), negative_fill, jnp.float32),
        jnp.zeros((KV_HEADS, row_total), jnp.float32),
        jnp.zeros((KV_HEADS, row_total, HD), jnp.float32),
    )
    folder = make_folder(query_sets, position_sets, last_positions, KV_HEADS, HD, score_scale)
    final_sets = folder(
        (empty_state, empty_state),
        (
            lax.all_gather(key_states, "ctx", axis=1, tiled=True),
            lax.all_gather(value_states, "ctx", axis=1, tiled=True),
        ),
        jnp.int32(0),
    )
    first_out = finish(final_sets[0], half_rows, KV_HEADS, group_size, HD)
    second_out = finish(final_sets[1], half_rows, KV_HEADS, group_size, HD)
    attention = jnp.concatenate([first_out, second_out], axis=0)
    summed = residual[0].astype(jnp.float32) + lax.optimization_barrier(attention).astype(
        jnp.float32
    )
    normed = (
        summed * lax.rsqrt(jnp.mean(summed * summed, axis=-1, keepdims=True) + epsilon)
    ).astype(jnp.bfloat16)
    width_model = normed.shape[1]
    experts_each = ctx_count // PIECES
    expert_total = experts_each * exp_count
    pair_count = tok_rows * TOPK
    capacity = max(2, 2 * tok_rows * TOPK // expert_total)
    flat_ids = expert_ids[0].reshape(pair_count)
    onehot = (flat_ids[:, None] == jnp.arange(expert_total, dtype=jnp.int32)[None, :]).astype(
        jnp.int32
    )
    earlier = jnp.cumsum(onehot, axis=0) - onehot
    slot_index = jnp.sum(earlier * onehot, axis=1)
    owner_index = flat_ids // experts_each
    local_expert = flat_ids % experts_each
    target = (local_expert * exp_count + owner_index) * capacity + slot_index
    pair_token = jnp.arange(pair_count, dtype=jnp.int32) // TOPK
    slot_total = expert_total * capacity
    slot_table = jnp.full((slot_total,), tok_rows, jnp.int32).at[target].set(pair_token)
    padded = jnp.concatenate([normed, jnp.zeros((1, width_model), jnp.bfloat16)], axis=0)
    outgoing = padded[slot_table].reshape(experts_each, exp_count, capacity, width_model)
    arrived = lax.all_to_all(outgoing, "exp", split_axis=1, concat_axis=1, tiled=True)
    copies = jnp.broadcast_to(
        arrived[:, None], (experts_each, PIECES, exp_count, capacity, width_model)
    ).reshape(ctx_count, exp_count * capacity, width_model)
    gate_piece = gate_weight[0, 0]
    up_piece = up_weight[0, 0]
    down_piece = down_weight[0, 0]
    received = lax.all_to_all(copies, "ctx", split_axis=0, concat_axis=0, tiled=True)
    sources = received.shape[0]
    item_count = received.shape[1]
    flat_rows = received.reshape(sources * item_count, width_model)
    gate_part = contract_rows(flat_rows, gate_piece)
    up_part = contract_rows(flat_rows, up_piece)
    active = (jax.nn.silu(gate_part) * up_part).astype(jnp.bfloat16)
    partial_out = jnp.dot(active, down_piece, preferred_element_type=jnp.float32).astype(
        jnp.bfloat16
    )
    returned = lax.all_to_all(
        partial_out.reshape(sources, item_count, width_model),
        "ctx",
        split_axis=0,
        concat_axis=0,
        tiled=True,
    )
    piece_sum = jnp.sum(
        returned.reshape(experts_each, PIECES, exp_count, capacity, width_model).astype(
            jnp.float32
        ),
        axis=1,
    ).astype(jnp.bfloat16)
    arrived_back = lax.all_to_all(piece_sum, "exp", split_axis=1, concat_axis=1, tiled=True)
    gathered = arrived_back.reshape(slot_total, width_model)[target].astype(jnp.float32)
    weighted = gathered * route_weight[0]
    mixture = jnp.sum(weighted.reshape(tok_rows, TOPK, width_model), axis=1)
    return (summed + mixture).astype(jnp.bfloat16)[None]


AXES = ("ctx", "exp")


def spot(flat):
    ctx, exp = divmod(flat, 4)
    return ctx // 2, ctx % 2, exp // 2, exp % 2


def flat_of(z, x, y, core):
    return (z * 2 + x) * 4 + y * 2 + core


def move(array, rule):
    pairs = []
    for flat in range(32):
        there = rule(*spot(flat))
        if there is not None:
            pairs.append((flat, flat_of(*there)))
    return lax.ppermute(array, AXES, pairs)


def is_home(z, core):
    return core == z % 2


def to_twin(z, x, y, core):
    return z, x, y, 1 - core


def aside(z, x, y, core):
    return (z, x ^ 1, y, 1 - core) if is_home(z, core) else None


def homeward(z, x, y, core):
    return None if is_home(z, core) else (z ^ 1, x, y, core)


def second_hop(z, x, y, core):
    return (z, x ^ 1, y, 1 - core) if is_home(z, core) else None


def slot_targets(ids_row, z_here, y_here, capacity):
    expert_count = 8
    token_count = ids_row.shape[1]
    lanes = lax.broadcasted_iota(jnp.int32, (expert_count, token_count), 0)
    onehot = (lanes == ids_row).astype(jnp.float32)
    before = (
        lax.broadcasted_iota(jnp.int32, (token_count, token_count), 0)
        < lax.broadcasted_iota(jnp.int32, (token_count, token_count), 1)
    ).astype(jnp.bfloat16)
    earlier = jnp.dot(onehot.astype(jnp.bfloat16), before, preferred_element_type=jnp.float32)
    slot = jnp.sum(earlier * onehot, axis=0, keepdims=True).astype(jnp.int32)
    owner = lax.shift_right_logical(ids_row, 1)
    z_there = (ids_row & 1) * 2 + (owner & 1)
    y_there = lax.shift_right_logical(owner, 1)
    relative = (z_there ^ z_here) * 2 + (y_there ^ y_here)
    return relative * capacity + slot


def slot_matrix(ids_row, z_here, y_here, capacity):
    target = slot_targets(ids_row, z_here, y_here, capacity)
    rows = lax.broadcasted_iota(jnp.int32, (8 * capacity, ids_row.shape[1]), 0)
    return (rows == target).astype(jnp.bfloat16)


def fetch_all(pairs, semaphores):
    copies = [
        pltpu.make_async_copy(source, target, semaphores.at[i])
        for i, (source, target) in enumerate(pairs)
    ]
    for copy in copies:
        copy.start()
    return copies


def attend_kernel(where_ref, ids_ref, queries_from, residual_from, *refs):
    kv_from, summed_to, out_refs = refs[:2], refs[2], refs[3:11]
    queries_ref, residual_ref, kv_ref, bias_ref, mixed_ref, summed_ref, semaphores = refs[11:]
    tokens = queries_ref.shape[0]
    group = HEADS // KV_HEADS
    copies = fetch_all(
        [(kv_from[k], kv_ref.at[pl.ds(4 * k * tokens, 4 * tokens)]) for k in range(2)]
        + [(queries_from, queries_ref), (residual_from, residual_ref)],
        semaphores,
    )
    row = lax.broadcasted_iota(jnp.int32, (tokens, tokens), 0)
    column = lax.broadcasted_iota(jnp.int32, (tokens, tokens), 1)
    for k in range(8):
        span = slice(k * tokens, (k + 1) * tokens)
        if k == 0:
            bias_ref[:, span] = jnp.where(column <= row, 0.0, negative_fill)
        else:
            seen = where_ref[0] == 1 if k == 4 else where_ref[1] >= k % 4
            bias_ref[:, span] = jnp.full(
                (tokens, tokens), jnp.where(seen, 0.0, negative_fill), jnp.float32
            )
    for copy in copies[:3]:
        copy.wait()
    factor = math.log2(math.e) / math.sqrt(HD)
    heads_each = 8
    for first in range(0, HEADS, heads_each):
        kv_head = first // group
        key_side = slice(kv_head * HD, (kv_head + 1) * HD)
        value_side = slice((KV_HEADS + kv_head) * HD, (KV_HEADS + kv_head + 1) * HD)
        rows = jnp.concatenate(
            [queries_ref[:, h * HD : (h + 1) * HD] for h in range(first, first + heads_each)], axis=0
        )
        scores = contract_rows(rows, kv_ref[:, key_side])
        scores = scores + jnp.concatenate([bias_ref[...]] * heads_each, axis=0)
        largest = jnp.max(scores, axis=1, keepdims=True)
        exponent = jnp.exp2((scores - largest) * factor)
        total = jnp.sum(exponent, axis=1, keepdims=True)
        product = jnp.dot(
            exponent.astype(jnp.bfloat16), kv_ref[:, value_side], preferred_element_type=jnp.float32
        )
        result = product / total
        for j in range(heads_each):
            mixed_ref[:, (first + j) * HD : (first + j + 1) * HD] = result[
                j * tokens : (j + 1) * tokens
            ].astype(jnp.bfloat16)
    copies[3].wait()
    summed = residual_ref[...].astype(jnp.float32) + mixed_ref[...].astype(jnp.float32)
    summed_ref[...] = summed
    keep = pltpu.make_async_copy(summed_ref, summed_to, semaphores.at[4])
    keep.start()
    scale = lax.rsqrt(jnp.mean(summed * summed, axis=1, keepdims=True) + epsilon)
    normed = (summed * scale).astype(jnp.bfloat16)
    capacity = out_refs[0].shape[0]
    choose = slot_matrix(ids_ref[...], where_ref[1], where_ref[2], capacity)
    slots = jnp.dot(choose, normed, preferred_element_type=jnp.float32).astype(jnp.bfloat16)
    for k in range(8):
        out_refs[k][...] = slots[k * capacity : (k + 1) * capacity]
    keep.wait()


def strips(pack, strip, count):
    return [pack.at[pl.ds(i * strip, strip)] for i in range(count)]


def load(sources, targets, semaphores):
    return [
        pltpu.make_async_copy(sources[kind], targets[kind], semaphores.at[kind])
        for kind in range(3)
    ]


def active_of(rows, gate, up):
    gate_part = contract_rows(rows, gate)
    up_part = contract_rows(rows, up)
    silu = gate_part / (1.0 + jnp.exp(-gate_part))
    return (silu * up_part).astype(jnp.bfloat16)


def expert_kernel(row_count, where_ref, *refs):
    row_from, refs = refs[:row_count], refs[row_count:]
    first_piece = len(refs) == 11
    strip = refs[-4].shape[0]
    if first_piece:
        at_home_from = strips(refs[0], strip, 3)
        away_from = refs[1:4]
        (total_ref,), rest = refs[4:5], refs[5:]
    else:
        away_from, at_home_from, before_from = strips(refs[0], strip, 3), refs[1:4], refs[4]
        (mine_ref, twins_ref), rest = refs[5:7], refs[7:]
    rows_ref, gate_ref, up_ref, down_ref, row_semaphores, semaphores = rest
    targets = (gate_ref, up_ref, down_ref)
    loads = []
    place = 0
    for ref in row_from:
        loads.append((ref, rows_ref.at[pl.ds(place, ref.shape[0])]))
        place += ref.shape[0]
    row_copies = fetch_all(loads, row_semaphores)
    weight_copies = load(at_home_from, targets, semaphores)
    at_home = where_ref[3] == 1

    @pl.when(at_home)
    def _():
        for copy in weight_copies:
            copy.start()

    @pl.when(jnp.logical_not(at_home))
    def _():
        for copy in load(away_from, targets, semaphores):
            copy.start()

    for copy in row_copies + weight_copies[:2]:
        copy.wait()
    active = active_of(rows_ref[...], gate_ref[...], up_ref[...])
    for copy in weight_copies[2:]:
        copy.wait()
    result = jnp.dot(active, down_ref[...], preferred_element_type=jnp.float32)
    if first_piece:
        total_ref[...] = result
    else:
        result = result + before_from[...]
        half = result.shape[0] // 2
        mine_ref[...] = result[:half]
        twins_ref[...] = result[half:].astype(jnp.bfloat16)


def join_kernel(mine_from, other_from, *refs):
    out_refs, (mine_ref, other_ref, semaphores) = refs[:8], refs[8:]
    capacity = out_refs[0].shape[0]
    for copy in fetch_all([(mine_from, mine_ref), (other_from, other_ref)], semaphores):
        copy.wait()
    result = (mine_ref[...] + other_ref[...].astype(jnp.float32)).astype(jnp.bfloat16)
    for k in range(8):
        out_refs[k][...] = result[k * capacity : (k + 1) * capacity]


def combine_kernel(where_ref, ids_ref, route_ref, summed_ref, *refs):
    row_refs, out_ref = refs[:8], refs[8]
    capacity = row_refs[0].shape[0]
    choose = slot_matrix(ids_ref[...], where_ref[1], where_ref[2], capacity)
    rows = jnp.concatenate([ref[...] for ref in row_refs], axis=0)
    picked = lax.dot_general(
        choose, rows, (((0,), (0,)), ((), ())), preferred_element_type=jnp.float32
    )
    out_ref[...] = (summed_ref[...] + picked * route_ref[...]).astype(jnp.bfloat16)


IN_VMEM = pl.BlockSpec(memory_space=pltpu.VMEM)
IN_SMEM = pl.BlockSpec(memory_space=pltpu.SMEM)
IN_HBM = pl.BlockSpec(memory_space=pltpu.HBM)


def shards_cube(
    residual,
    queries,
    key_states,
    value_states,
    expert_ids,
    route_weight,
    gate_weight,
    up_weight,
    down_weight,
):
    ctx_here = lax.axis_index("ctx")
    exp_here = lax.axis_index("exp")
    at_home = ((ctx_here // 2) % 2 == exp_here % 2).astype(jnp.int32)
    where = jnp.stack([ctx_here % 2, ctx_here // 2, exp_here // 2, at_home]).astype(jnp.int32)
    tokens, width = residual.shape[1:]
    piece = gate_weight.shape[2]
    capacity = max(2, 2 * tokens * TOPK // 8)
    ids_row = expert_ids[0].reshape(1, tokens)
    kv_own = jnp.concatenate([key_states[0], value_states[0]], axis=1)
    weights = (gate_weight[0, 0], up_weight[0, 0], down_weight[0, 0])
    def along_z(steps):
        return move(
            kv_own, lambda z, x, y, core: (z + steps, x, y, core) if z + steps < 4 else None
        )

    beside = [move(w, aside) for w in weights[:2]]
    kv_along = [kv_own] + [along_z(steps) for steps in (1, 2, 3)]
    own = jnp.concatenate(weights, axis=0)
    own, where, beside[0], beside[1], *kv_along = lax.optimization_barrier(
        (own, where, *beside, *kv_along)
    )
    home = move(own, homeward)
    kv_here = jnp.concatenate(kv_along, axis=0)
    kv_list = [kv_here, move(kv_here, lambda z, x, y, core: (z, 1 - x, y, core))]
    rest, *kv_list = lax.optimization_barrier((weights[2], *kv_list))
    beside_rest = move(rest, aside)
    slot_shape = jax.ShapeDtypeStruct((capacity, width), jnp.bfloat16)
    keys_all = 8 * tokens
    rows_all = 8 * capacity
    first_out = pl.pallas_call(
        attend_kernel,
        out_shape=[jax.ShapeDtypeStruct((tokens, width), jnp.float32)] + [slot_shape] * 8,
        in_specs=[IN_SMEM, IN_VMEM] + [IN_HBM] * 4,
        out_specs=[IN_HBM] + [IN_VMEM] * 8,
        scratch_shapes=[
            pltpu.VMEM((tokens, width), jnp.bfloat16),
            pltpu.VMEM((tokens, width), jnp.bfloat16),
            pltpu.VMEM((keys_all, 2 * KV_HEADS * HD), jnp.bfloat16),
            pltpu.VMEM((tokens, keys_all), jnp.float32),
            pltpu.VMEM((tokens, width), jnp.bfloat16),
            pltpu.VMEM((tokens, width), jnp.float32),
            pltpu.SemaphoreType.DMA((5,)),
        ],
        compiler_params=pltpu.CompilerParams(vmem_limit_bytes=58 << 20),
        cost_estimate=pl.CostEstimate(
            flops=4 * tokens * keys_all * HEADS * HD,
            bytes_accessed=8 * tokens * width,
            transcendentals=tokens * keys_all * HEADS,
        ),
        name="attend",
    )(where, ids_row, queries[0], residual[0], *kv_list)
    summed, outgoing = first_out[0], list(first_out[1:])

    def swap(array, k):
        if k == 0:
            return array
        return move(array, lambda z, x, y, core: (z ^ (k >> 1), x, y ^ (k & 1), core))

    last = move(home, second_hop)
    arrived = {0: outgoing[0]}
    beside_rest, *outgoing = lax.optimization_barrier((beside_rest, *outgoing))
    for k in (4, 6, 5, 7, 2, 3, 1):
        arrived[k] = swap(outgoing[k], k)
    order = (0, 2, 3, 1, 4, 6, 5, 7)
    row_parts = [jnp.concatenate([arrived[k] for k in group]) for group in (order[:4], order[4:])]
    row_parts += [move(part, to_twin) for part in row_parts]

    def run_expert(packs, before):
        row_total = 2 * rows_all
        mine = jax.ShapeDtypeStruct((rows_all, width), jnp.float32)
        twins = jax.ShapeDtypeStruct((rows_all, width), jnp.bfloat16)
        total = jax.ShapeDtypeStruct((row_total, width), jnp.float32)
        return pl.pallas_call(
            partial(expert_kernel, len(row_parts)),
            out_shape=[mine, twins] if before else [total],
            in_specs=[IN_SMEM]
            + [IN_HBM] * (len(row_parts) + len(packs))
            + [IN_VMEM] * len(before),
            out_specs=[IN_VMEM] * (2 if before else 1),
            scratch_shapes=[
                pltpu.VMEM((row_total, width), jnp.bfloat16),
                pltpu.VMEM((piece, width), jnp.bfloat16),
                pltpu.VMEM((piece, width), jnp.bfloat16),
                pltpu.VMEM((piece, width), jnp.bfloat16),
                pltpu.SemaphoreType.DMA((4,)),
                pltpu.SemaphoreType.DMA((3,)),
            ],
            compiler_params=pltpu.CompilerParams(vmem_limit_bytes=32 << 20),
            cost_estimate=pl.CostEstimate(
                flops=6 * row_total * piece * width,
                bytes_accessed=6 * piece * width,
                transcendentals=row_total * piece,
            ),
            name="experts_rest" if before else "experts_first",
        )(where, *row_parts, *packs, *before)

    first_total = run_expert([home, *beside, beside_rest], [])
    last, *first_total = lax.optimization_barrier((last, *first_total))
    mine, twins = run_expert([last, *weights], first_total)
    joined = pl.pallas_call(
        join_kernel,
        out_shape=[slot_shape] * 8,
        in_specs=[IN_HBM] * 2,
        out_specs=[IN_VMEM] * 8,
        scratch_shapes=[
            pltpu.VMEM((rows_all, width), jnp.float32),
            pltpu.VMEM((rows_all, width), jnp.bfloat16),
            pltpu.SemaphoreType.DMA((2,)),
        ],
        compiler_params=pltpu.CompilerParams(vmem_limit_bytes=16 << 20),
        cost_estimate=pl.CostEstimate(
            flops=rows_all * width, bytes_accessed=8 * rows_all * width, transcendentals=0
        ),
        name="join",
    )(mine, move(twins, to_twin))
    results = [joined[order.index(k)] for k in range(8)]
    returned = [swap(results[k], k) for k in range(8)]
    output = pl.pallas_call(
        combine_kernel,
        out_shape=jax.ShapeDtypeStruct((tokens, width), jnp.bfloat16),
        in_specs=[IN_SMEM] + [IN_VMEM] * 11,
        out_specs=IN_VMEM,
        compiler_params=pltpu.CompilerParams(vmem_limit_bytes=12 << 20),
        cost_estimate=pl.CostEstimate(
            flops=2 * tokens * 8 * capacity * width,
            bytes_accessed=12 * tokens * width,
            transcendentals=0,
        ),
        name="combine",
    )(where, ids_row, route_weight[0], summed, *returned)
    return output[None]


def solution(mesh):
    in_specs = (
        P("exp", "ctx", None),
        P("exp", "ctx", None),
        P("exp", "ctx", None),
        P("exp", "ctx", None),
        P("exp", "ctx", None),
        P("exp", "ctx", None),
        P("exp", "ctx", None, None),
        P("exp", "ctx", None, None),
        P("exp", "ctx", None, None),
    )
    out_specs = P("exp", "ctx", None)
    cube = mesh.shape["ctx"] == 8 and mesh.shape["exp"] == 4
    body = shards_cube if cube else shards
    return jax.shard_map(body, mesh=mesh, in_specs=in_specs, out_specs=out_specs, check_vma=False)
```

```python
from functools import partial
import math

import jax
import jax.numpy as jnp
from jax import lax
from jax.experimental import pallas as pl
from jax.experimental.pallas import tpu as pltpu
from jax.sharding import PartitionSpec as P

HD = 128
HEADS = 16
KV_HEADS = 2
PIECES = 4
TOPK = 1


negative_fill = -1e30
epsilon = 1e-06


def contract_rows(left_rows, weight_rows):
    return lax.dot_general(
        left_rows, weight_rows, (((1,), (1,)), ((), ())), preferred_element_type=jnp.float32
    )


def to_groups(half_block, heads_kv, group_size, head_dim):
    token_count = half_block.shape[0]
    shaped = half_block.reshape(token_count, heads_kv, group_size, head_dim)
    return jnp.transpose(shaped, (1, 0, 2, 3)).reshape(heads_kv, token_count * group_size, head_dim)


def keep_current(current):
    return current


def block_update(current, query_rows, query_pos, key_block, value_block, key_start, score_scale):
    running_max, running_total, accumulated = current
    scores = (
        jnp.einsum("gqd,kgd->gqk", query_rows, key_block, preferred_element_type=jnp.float32)
        * score_scale
    )
    key_pos = key_start + jnp.arange(key_block.shape[0], dtype=jnp.int32)
    allowed = key_pos[None, None, :] <= query_pos[None, :, None]
    scores = jnp.where(allowed, scores, negative_fill)
    new_max = jnp.maximum(running_max, jnp.max(scores, axis=-1))
    rescale = jnp.exp(running_max - new_max)
    exponent = jnp.where(allowed, jnp.exp(scores - new_max[..., None]), 0.0)
    new_total = running_total * rescale + jnp.sum(exponent, axis=-1)
    product = jnp.einsum(
        "gqk,kgd->gqd",
        exponent.astype(jnp.bfloat16),
        value_block,
        preferred_element_type=jnp.float32,
    )
    return (new_max, new_total, accumulated * rescale[..., None] + product)


def make_folder(query_sets, position_sets, last_positions, heads_kv, head_dim, score_scale):

    def fold_keys(running, key_piece, first_key):
        key_part, value_part = key_piece
        key_count = key_part.shape[1]
        key_width = math.gcd(key_count, 512)
        key_rows = key_part.reshape(key_count, heads_kv, head_dim)
        value_rows = value_part.reshape(key_count, heads_kv, head_dim)

        def one_block(block_index, current_sets):
            offset = block_index * key_width
            key_block = lax.dynamic_slice_in_dim(key_rows, offset, key_width, 0)
            value_block = lax.dynamic_slice_in_dim(value_rows, offset, key_width, 0)
            updated = []
            for current, query_rows, query_pos, last_pos in zip(
                current_sets, query_sets, position_sets, last_positions
            ):
                step_fn = partial(
                    block_update,
                    query_rows=query_rows,
                    query_pos=query_pos,
                    key_block=key_block,
                    value_block=value_block,
                    key_start=offset,
                    score_scale=score_scale,
                )
                updated.append(lax.cond(offset <= last_pos, step_fn, keep_current, current))
            return tuple(updated)

        return lax.fori_loop(0, key_count // key_width, one_block, running)

    return fold_keys


def finish(current, token_count, heads_kv, group_size, head_dim):
    running_max, running_total, accumulated = current
    result = accumulated / running_total[..., None]
    shaped = result.reshape(heads_kv, token_count, group_size, head_dim)
    return (
        jnp.transpose(shaped, (1, 0, 2, 3))
        .reshape(token_count, heads_kv * group_size * head_dim)
        .astype(jnp.bfloat16)
    )


def shards(
    residual,
    queries,
    key_states,
    value_states,
    expert_ids,
    route_weight,
    gate_weight,
    up_weight,
    down_weight,
):
    ctx_count = lax.axis_size("ctx")
    exp_count = lax.axis_size("exp")
    ctx_rank = lax.axis_index("ctx")
    tok_rows = residual.shape[1]
    half_rows = tok_rows // 2
    group_size = HEADS // KV_HEADS
    score_scale = 1.0 / math.sqrt(HD)
    local_queries = queries[0]
    first_half = local_queries[:half_rows]
    second_half = local_queries[half_rows:]
    first_start = ctx_rank * tok_rows
    second_start = first_start + half_rows
    offsets = jnp.repeat(jnp.arange(half_rows, dtype=jnp.int32), group_size)
    query_sets = (
        to_groups(first_half, KV_HEADS, group_size, HD),
        to_groups(second_half, KV_HEADS, group_size, HD),
    )
    position_sets = (first_start + offsets, second_start + offsets)
    last_positions = (first_start + half_rows - 1, second_start + half_rows - 1)
    row_total = half_rows * group_size
    empty_state = (
        jnp.full((KV_HEADS, row_total), negative_fill, jnp.float32),
        jnp.zeros((KV_HEADS, row_total), jnp.float32),
        jnp.zeros((KV_HEADS, row_total, HD), jnp.float32),
    )
    folder = make_folder(query_sets, position_sets, last_positions, KV_HEADS, HD, score_scale)
    final_sets = folder(
        (empty_state, empty_state),
        (
            lax.all_gather(key_states, "ctx", axis=1, tiled=True),
            lax.all_gather(value_states, "ctx", axis=1, tiled=True),
        ),
        jnp.int32(0),
    )
    first_out = finish(final_sets[0], half_rows, KV_HEADS, group_size, HD)
    second_out = finish(final_sets[1], half_rows, KV_HEADS, group_size, HD)
    attention = jnp.concatenate([first_out, second_out], axis=0)
    summed = residual[0].astype(jnp.float32) + lax.optimization_barrier(attention).astype(
        jnp.float32
    )
    normed = (
        summed * lax.rsqrt(jnp.mean(summed * summed, axis=-1, keepdims=True) + epsilon)
    ).astype(jnp.bfloat16)
    width_model = normed.shape[1]
    experts_each = ctx_count // PIECES
    expert_total = experts_each * exp_count
    pair_count = tok_rows * TOPK
    capacity = max(2, 2 * tok_rows * TOPK // expert_total)
    flat_ids = expert_ids[0].reshape(pair_count)
    onehot = (flat_ids[:, None] == jnp.arange(expert_total, dtype=jnp.int32)[None, :]).astype(
        jnp.int32
    )
    earlier = jnp.cumsum(onehot, axis=0) - onehot
    slot_index = jnp.sum(earlier * onehot, axis=1)
    owner_index = flat_ids // experts_each
    local_expert = flat_ids % experts_each
    target = (local_expert * exp_count + owner_index) * capacity + slot_index
    pair_token = jnp.arange(pair_count, dtype=jnp.int32) // TOPK
    slot_total = expert_total * capacity
    slot_table = jnp.full((slot_total,), tok_rows, jnp.int32).at[target].set(pair_token)
    padded = jnp.concatenate([normed, jnp.zeros((1, width_model), jnp.bfloat16)], axis=0)
    outgoing = padded[slot_table].reshape(experts_each, exp_count, capacity, width_model)
    arrived = lax.all_to_all(outgoing, "exp", split_axis=1, concat_axis=1, tiled=True)
    copies = jnp.broadcast_to(
        arrived[:, None], (experts_each, PIECES, exp_count, capacity, width_model)
    ).reshape(ctx_count, exp_count * capacity, width_model)
    gate_piece = gate_weight[0, 0]
    up_piece = up_weight[0, 0]
    down_piece = down_weight[0, 0]
    received = lax.all_to_all(copies, "ctx", split_axis=0, concat_axis=0, tiled=True)
    sources = received.shape[0]
    item_count = received.shape[1]
    flat_rows = received.reshape(sources * item_count, width_model)
    gate_part = contract_rows(flat_rows, gate_piece)
    up_part = contract_rows(flat_rows, up_piece)
    active = (jax.nn.silu(gate_part) * up_part).astype(jnp.bfloat16)
    partial_out = jnp.dot(active, down_piece, preferred_element_type=jnp.float32).astype(
        jnp.bfloat16
    )
    returned = lax.all_to_all(
        partial_out.reshape(sources, item_count, width_model),
        "ctx",
        split_axis=0,
        concat_axis=0,
        tiled=True,
    )
    piece_sum = jnp.sum(
        returned.reshape(experts_each, PIECES, exp_count, capacity, width_model).astype(
            jnp.float32
        ),
        axis=1,
    ).astype(jnp.bfloat16)
    arrived_back = lax.all_to_all(piece_sum, "exp", split_axis=1, concat_axis=1, tiled=True)
    gathered = arrived_back.reshape(slot_total, width_model)[target].astype(jnp.float32)
    weighted = gathered * route_weight[0]
    mixture = jnp.sum(weighted.reshape(tok_rows, TOPK, width_model), axis=1)
    return (summed + mixture).astype(jnp.bfloat16)[None]


AXES = ("ctx", "exp")


def spot(flat):
    ctx, exp = divmod(flat, 4)
    return ctx // 2, ctx % 2, exp // 2, exp % 2


def flat_of(z, x, y, core):
    return (z * 2 + x) * 4 + y * 2 + core


def move(array, rule):
    pairs = []
    for flat in range(32):
        there = rule(*spot(flat))
        if there is not None:
            pairs.append((flat, flat_of(*there)))
    return lax.ppermute(array, AXES, pairs)


def is_home(z, core):
    return core == z % 2


def to_twin(z, x, y, core):
    return z, x, y, 1 - core


def aside(z, x, y, core):
    return (z, x ^ 1, y, 1 - core) if is_home(z, core) else None


def homeward(z, x, y, core):
    return None if is_home(z, core) else (z ^ 1, x, y, core)


def second_hop(z, x, y, core):
    return (z, x ^ 1, y, 1 - core) if is_home(z, core) else None


def slot_targets(ids_row, z_here, y_here, capacity):
    expert_count = 8
    token_count = ids_row.shape[1]
    lanes = lax.broadcasted_iota(jnp.int32, (expert_count, token_count), 0)
    onehot = (lanes == ids_row).astype(jnp.float32)
    before = (
        lax.broadcasted_iota(jnp.int32, (token_count, token_count), 0)
        < lax.broadcasted_iota(jnp.int32, (token_count, token_count), 1)
    ).astype(jnp.bfloat16)
    earlier = jnp.dot(onehot.astype(jnp.bfloat16), before, preferred_element_type=jnp.float32)
    slot = jnp.sum(earlier * onehot, axis=0, keepdims=True).astype(jnp.int32)
    owner = lax.shift_right_logical(ids_row, 1)
    z_there = (ids_row & 1) * 2 + (owner & 1)
    y_there = lax.shift_right_logical(owner, 1)
    relative = (z_there ^ z_here) * 2 + (y_there ^ y_here)
    return relative * capacity + slot


def slot_matrix(ids_row, z_here, y_here, capacity):
    target = slot_targets(ids_row, z_here, y_here, capacity)
    rows = lax.broadcasted_iota(jnp.int32, (8 * capacity, ids_row.shape[1]), 0)
    return (rows == target).astype(jnp.bfloat16)


def fetch_all(pairs, semaphores):
    copies = [
        pltpu.make_async_copy(source, target, semaphores.at[i])
        for i, (source, target) in enumerate(pairs)
    ]
    for copy in copies:
        copy.start()
    return copies


def attend_kernel(where_ref, ids_ref, queries_from, residual_from, *refs):
    kv_from, summed_to, out_refs = refs[:2], refs[2], refs[3:11]
    queries_ref, residual_ref, kv_ref, bias_ref, mixed_ref, summed_ref, semaphores = refs[11:]
    tokens = queries_ref.shape[0]
    group = HEADS // KV_HEADS
    copies = fetch_all(
        [(kv_from[k], kv_ref.at[pl.ds(4 * k * tokens, 4 * tokens)]) for k in range(2)]
        + [(queries_from, queries_ref), (residual_from, residual_ref)],
        semaphores,
    )
    row = lax.broadcasted_iota(jnp.int32, (tokens, tokens), 0)
    column = lax.broadcasted_iota(jnp.int32, (tokens, tokens), 1)
    for k in range(8):
        span = slice(k * tokens, (k + 1) * tokens)
        if k == 0:
            bias_ref[:, span] = jnp.where(column <= row, 0.0, negative_fill)
        else:
            seen = where_ref[0] == 1 if k == 4 else where_ref[1] >= k % 4
            bias_ref[:, span] = jnp.full(
                (tokens, tokens), jnp.where(seen, 0.0, negative_fill), jnp.float32
            )
    for copy in copies[:3]:
        copy.wait()
    factor = math.log2(math.e) / math.sqrt(HD)
    heads_each = 8
    for first in range(0, HEADS, heads_each):
        kv_head = first // group
        key_side = slice(kv_head * HD, (kv_head + 1) * HD)
        value_side = slice((KV_HEADS + kv_head) * HD, (KV_HEADS + kv_head + 1) * HD)
        rows = jnp.concatenate(
            [queries_ref[:, h * HD : (h + 1) * HD] for h in range(first, first + heads_each)], axis=0
        )
        scores = contract_rows(rows, kv_ref[:, key_side])
        scores = scores + jnp.concatenate([bias_ref[...]] * heads_each, axis=0)
        largest = jnp.max(scores, axis=1, keepdims=True)
        exponent = jnp.exp2((scores - largest) * factor)
        total = jnp.sum(exponent, axis=1, keepdims=True)
        product = jnp.dot(
            exponent.astype(jnp.bfloat16), kv_ref[:, value_side], preferred_element_type=jnp.float32
        )
        result = product / total
        for j in range(heads_each):
            mixed_ref[:, (first + j) * HD : (first + j + 1) * HD] = result[
                j * tokens : (j + 1) * tokens
            ].astype(jnp.bfloat16)
    copies[3].wait()
    summed = residual_ref[...].astype(jnp.float32) + mixed_ref[...].astype(jnp.float32)
    summed_ref[...] = summed
    keep = pltpu.make_async_copy(summed_ref, summed_to, semaphores.at[4])
    keep.start()
    scale = lax.rsqrt(jnp.mean(summed * summed, axis=1, keepdims=True) + epsilon)
    normed = (summed * scale).astype(jnp.bfloat16)
    capacity = out_refs[0].shape[0]
    choose = slot_matrix(ids_ref[...], where_ref[1], where_ref[2], capacity)
    slots = jnp.dot(choose, normed, preferred_element_type=jnp.float32).astype(jnp.bfloat16)
    for k in range(8):
        out_refs[k][...] = slots[k * capacity : (k + 1) * capacity]
    keep.wait()


def strips(pack, strip, count):
    return [pack.at[pl.ds(i * strip, strip)] for i in range(count)]


def load(sources, targets, semaphores):
    return [
        pltpu.make_async_copy(sources[kind], targets[kind], semaphores.at[kind])
        for kind in range(3)
    ]


def active_of(rows, gate, up):
    gate_part = contract_rows(rows, gate)
    up_part = contract_rows(rows, up)
    silu = gate_part / (1.0 + jnp.exp(-gate_part))
    return (silu * up_part).astype(jnp.bfloat16)


def expert_kernel(row_count, where_ref, *refs):
    row_from, refs = refs[:row_count], refs[row_count:]
    first_piece = len(refs) == 11
    strip = refs[-4].shape[0]
    if first_piece:
        at_home_from = strips(refs[0], strip, 3)
        away_from = refs[1:4]
        (total_ref,), rest = refs[4:5], refs[5:]
    else:
        away_from, at_home_from, before_from = strips(refs[0], strip, 3), refs[1:4], refs[4]
        (mine_ref, twins_ref), rest = refs[5:7], refs[7:]
    rows_ref, gate_ref, up_ref, down_ref, row_semaphores, semaphores = rest
    targets = (gate_ref, up_ref, down_ref)
    loads = []
    place = 0
    for ref in row_from:
        loads.append((ref, rows_ref.at[pl.ds(place, ref.shape[0])]))
        place += ref.shape[0]
    row_copies = fetch_all(loads, row_semaphores)
    weight_copies = load(at_home_from, targets, semaphores)
    at_home = where_ref[3] == 1

    @pl.when(at_home)
    def _():
        for copy in weight_copies:
            copy.start()

    @pl.when(jnp.logical_not(at_home))
    def _():
        for copy in load(away_from, targets, semaphores):
            copy.start()

    for copy in row_copies + weight_copies[:2]:
        copy.wait()
    active = active_of(rows_ref[...], gate_ref[...], up_ref[...])
    for copy in weight_copies[2:]:
        copy.wait()
    result = jnp.dot(active, down_ref[...], preferred_element_type=jnp.float32)
    if first_piece:
        total_ref[...] = result
    else:
        result = result + before_from[...]
        half = result.shape[0] // 2
        mine_ref[...] = result[:half]
        twins_ref[...] = result[half:].astype(jnp.bfloat16)


def join_kernel(mine_from, other_from, *refs):
    out_refs, (mine_ref, other_ref, semaphores) = refs[:8], refs[8:]
    capacity = out_refs[0].shape[0]
    for copy in fetch_all([(mine_from, mine_ref), (other_from, other_ref)], semaphores):
        copy.wait()
    result = (mine_ref[...] + other_ref[...].astype(jnp.float32)).astype(jnp.bfloat16)
    for k in range(8):
        out_refs[k][...] = result[k * capacity : (k + 1) * capacity]


def combine_kernel(where_ref, ids_ref, route_ref, summed_ref, *refs):
    row_refs, out_ref = refs[:8], refs[8]
    capacity = row_refs[0].shape[0]
    choose = slot_matrix(ids_ref[...], where_ref[1], where_ref[2], capacity)
    rows = jnp.concatenate([ref[...] for ref in row_refs], axis=0)
    picked = lax.dot_general(
        choose, rows, (((0,), (0,)), ((), ())), preferred_element_type=jnp.float32
    )
    out_ref[...] = (summed_ref[...] + picked * route_ref[...]).astype(jnp.bfloat16)


IN_VMEM = pl.BlockSpec(memory_space=pltpu.VMEM)
IN_SMEM = pl.BlockSpec(memory_space=pltpu.SMEM)
IN_HBM = pl.BlockSpec(memory_space=pltpu.HBM)


def shards_cube(
    residual,
    queries,
    key_states,
    value_states,
    expert_ids,
    route_weight,
    gate_weight,
    up_weight,
    down_weight,
):
    ctx_here = lax.axis_index("ctx")
    exp_here = lax.axis_index("exp")
    at_home = ((ctx_here // 2) % 2 == exp_here % 2).astype(jnp.int32)
    where = jnp.stack([ctx_here % 2, ctx_here // 2, exp_here // 2, at_home]).astype(jnp.int32)
    tokens, width = residual.shape[1:]
    piece = gate_weight.shape[2]
    capacity = max(2, 2 * tokens * TOPK // 8)
    ids_row = expert_ids[0].reshape(1, tokens)
    kv_own = jnp.concatenate([key_states[0], value_states[0]], axis=1)
    weights = (gate_weight[0, 0], up_weight[0, 0], down_weight[0, 0])
    def along_z(steps):
        return move(
            kv_own, lambda z, x, y, core: (z + steps, x, y, core) if z + steps < 4 else None
        )

    beside = [move(w, aside) for w in weights[:2]]
    kv_along = [kv_own] + [along_z(steps) for steps in (1, 2, 3)]
    own = jnp.concatenate(weights, axis=0)
    own, where, beside[0], beside[1], *kv_along = lax.optimization_barrier(
        (own, where, *beside, *kv_along)
    )
    home = move(own, homeward)
    kv_here = jnp.concatenate(kv_along, axis=0)
    kv_list = [kv_here, move(kv_here, lambda z, x, y, core: (z, 1 - x, y, core))]
    rest, *kv_list = lax.optimization_barrier((weights[2], *kv_list))
    beside_rest = move(rest, aside)
    slot_shape = jax.ShapeDtypeStruct((capacity, width), jnp.bfloat16)
    keys_all = 8 * tokens
    rows_all = 8 * capacity
    first_out = pl.pallas_call(
        attend_kernel,
        out_shape=[jax.ShapeDtypeStruct((tokens, width), jnp.float32)] + [slot_shape] * 8,
        in_specs=[IN_SMEM, IN_VMEM] + [IN_HBM] * 4,
        out_specs=[IN_HBM] + [IN_VMEM] * 8,
        scratch_shapes=[
            pltpu.VMEM((tokens, width), jnp.bfloat16),
            pltpu.VMEM((tokens, width), jnp.bfloat16),
            pltpu.VMEM((keys_all, 2 * KV_HEADS * HD), jnp.bfloat16),
            pltpu.VMEM((tokens, keys_all), jnp.float32),
            pltpu.VMEM((tokens, width), jnp.bfloat16),
            pltpu.VMEM((tokens, width), jnp.float32),
            pltpu.SemaphoreType.DMA((5,)),
        ],
        compiler_params=pltpu.CompilerParams(vmem_limit_bytes=58 << 20),
        cost_estimate=pl.CostEstimate(
            flops=4 * tokens * keys_all * HEADS * HD,
            bytes_accessed=8 * tokens * width,
            transcendentals=tokens * keys_all * HEADS,
        ),
        name="attend",
    )(where, ids_row, queries[0], residual[0], *kv_list)
    summed, outgoing = first_out[0], list(first_out[1:])

    def swap(array, k):
        if k == 0:
            return array
        return move(array, lambda z, x, y, core: (z ^ (k >> 1), x, y ^ (k & 1), core))

    last = move(home, second_hop)
    arrived = {0: outgoing[0]}
    arrived[4] = swap(outgoing[4], 4)
    arrived[6] = swap(outgoing[6], 6)
    beside_rest, *outgoing = lax.optimization_barrier((beside_rest, *outgoing))
    for k in (5, 7, 2, 3, 1):
        arrived[k] = swap(outgoing[k], k)
    order = (0, 2, 3, 1, 4, 6, 5, 7)
    row_parts = [jnp.concatenate([arrived[k] for k in group]) for group in (order[:4], order[4:])]
    row_parts += [move(part, to_twin) for part in row_parts]

    def run_expert(packs, before):
        row_total = 2 * rows_all
        mine = jax.ShapeDtypeStruct((rows_all, width), jnp.float32)
        twins = jax.ShapeDtypeStruct((rows_all, width), jnp.bfloat16)
        total = jax.ShapeDtypeStruct((row_total, width), jnp.float32)
        return pl.pallas_call(
            partial(expert_kernel, len(row_parts)),
            out_shape=[mine, twins] if before else [total],
            in_specs=[IN_SMEM]
            + [IN_HBM] * (len(row_parts) + len(packs))
            + [IN_VMEM] * len(before),
            out_specs=[IN_VMEM] * (2 if before else 1),
            scratch_shapes=[
                pltpu.VMEM((row_total, width), jnp.bfloat16),
                pltpu.VMEM((piece, width), jnp.bfloat16),
                pltpu.VMEM((piece, width), jnp.bfloat16),
                pltpu.VMEM((piece, width), jnp.bfloat16),
                pltpu.SemaphoreType.DMA((4,)),
                pltpu.SemaphoreType.DMA((3,)),
            ],
            compiler_params=pltpu.CompilerParams(vmem_limit_bytes=32 << 20),
            cost_estimate=pl.CostEstimate(
                flops=6 * row_total * piece * width,
                bytes_accessed=6 * piece * width,
                transcendentals=row_total * piece,
            ),
            name="experts_rest" if before else "experts_first",
        )(where, *row_parts, *packs, *before)

    first_total = run_expert([home, *beside, beside_rest], [])
    last, *first_total = lax.optimization_barrier((last, *first_total))
    mine, twins = run_expert([last, *weights], first_total)
    joined = pl.pallas_call(
        join_kernel,
        out_shape=[slot_shape] * 8,
        in_specs=[IN_HBM] * 2,
        out_specs=[IN_VMEM] * 8,
        scratch_shapes=[
            pltpu.VMEM((rows_all, width), jnp.float32),
            pltpu.VMEM((rows_all, width), jnp.bfloat16),
            pltpu.SemaphoreType.DMA((2,)),
        ],
        compiler_params=pltpu.CompilerParams(vmem_limit_bytes=16 << 20),
        cost_estimate=pl.CostEstimate(
            flops=rows_all * width, bytes_accessed=8 * rows_all * width, transcendentals=0
        ),
        name="join",
    )(mine, move(twins, to_twin))
    results = [joined[order.index(k)] for k in range(8)]
    returned = [swap(results[k], k) for k in range(8)]
    output = pl.pallas_call(
        combine_kernel,
        out_shape=jax.ShapeDtypeStruct((tokens, width), jnp.bfloat16),
        in_specs=[IN_SMEM] + [IN_VMEM] * 11,
        out_specs=IN_VMEM,
        compiler_params=pltpu.CompilerParams(vmem_limit_bytes=12 << 20),
        cost_estimate=pl.CostEstimate(
            flops=2 * tokens * 8 * capacity * width,
            bytes_accessed=12 * tokens * width,
            transcendentals=0,
        ),
        name="combine",
    )(where, ids_row, route_weight[0], summed, *returned)
    return output[None]


def solution(mesh):
    in_specs = (
        P("exp", "ctx", None),
        P("exp", "ctx", None),
        P("exp", "ctx", None),
        P("exp", "ctx", None),
        P("exp", "ctx", None),
        P("exp", "ctx", None),
        P("exp", "ctx", None, None),
        P("exp", "ctx", None, None),
        P("exp", "ctx", None, None),
    )
    out_specs = P("exp", "ctx", None)
    cube = mesh.shape["ctx"] == 8 and mesh.shape["exp"] == 4
    body = shards_cube if cube else shards
    return jax.shard_map(body, mesh=mesh, in_specs=in_specs, out_specs=out_specs, check_vma=False)
```
